256 devices in a mesh: gx: 8 (over x, core), gy: 32 (over y, z).
Axes of the slice: x: 4, y: 4, z: 8, core: 2. Of those that a mesh axis runs over, the one named last changes fastest.
Arguments:
- state: float32 [3, 3, 3, 256, 4096], P(None, None, None, 'gx', 'gy'), may hold values from -3 to 3, as said below
- bathymetry: float32 [3, 3, 256, 4096], P(None, None, 'gx', 'gy'), may hold values from -1.5 to 1.5
- flags: int32 [256, 4096], P('gx', 'gy'), may hold values from 0 to 1, as said below
Outputs:
- increment: float32 [3, 3, 3, 256, 4096], P(None, None, None, 'gx', 'gy')
The draws below stay inside these ranges and needn't reach their ends.
Inputs may be any that keep to these rules, and one draw needn't show every extreme that they name: `flags`: exactly 65536 elements are flagged; the 32 x 128 elements of one device hold at most 1024 flagged ones, and some device holds exactly 1024. `state`: component 0 (depth) is positive; each momentum is at most 1.5 times the depth in magnitude.
All inputs are finite; a program needn't handle non-finite values.
Results may differ from the reference program's by a relative error of at most 0.0003.
Values sent between devices are 32-bit elements; how exact they have to be, the bound alone decides.
No kernel may reach another device: no remote copies, remote signals or barrier semaphores. Data moves between devices by JAX's collectives and lax.ppermute only.
A program may use at most 64 MiB of HBM per device.

```python
import math
import jax
import jax.numpy as jnp
from jax import lax

TX = 32
TY = 128
TB_SHARE = 256
NPIC = 3
FLAGGED = 65536
NXE = 256
NYE = 4096
N_GX = 8
N_GY = 32


def draw_state(key, part):
    key_depth, key_speed = jax.random.split(key)
    shape = (3, 3, NXE, NYE)
    depth = jnp.exp(jax.random.uniform(key_depth, shape, jnp.float32, math.log(0.02), math.log(2.0)))
    speed = jnp.clip(0.6 * jax.random.normal(key_speed, (2,) + shape, jnp.float32), -1.5, 1.5)
    return jnp.stack([depth, depth * speed[0], depth * speed[1]])


def cell_ranks(key_cell):
    return jnp.argsort(jax.random.permutation(key_cell, TX * TY))


def draw_flags(key, part):
    devices = N_GX * N_GY
    groups = devices // 4
    key_extra, key_pick, key_top, key_perm, key_cells = jax.random.split(key, 5)
    extra = jax.random.randint(key_extra, (groups,), 0, TB_SHARE + 1)
    chosen = jax.random.randint(key_pick, (), 0, groups)
    extra = jnp.where(jnp.arange(groups) == chosen, TB_SHARE, extra)
    busiest = jax.random.randint(key_top, (groups,), 0, 4)
    member = jnp.arange(4)[None, :]
    counts = jnp.where(member == busiest[:, None], TB_SHARE + 3 * extra[:, None], TB_SHARE - extra[:, None]).reshape(devices)
    counts = counts[jax.random.permutation(key_perm, devices)]
    ranks = jax.vmap(cell_ranks)(jax.random.split(key_cells, devices))
    marks = (ranks < counts[:, None]).astype(jnp.int32)
    return marks.reshape(N_GX, N_GY, TX, TY).transpose(0, 2, 1, 3).reshape(NXE, NYE)


def block_scale(rng, dims, cuts, least, high):
    gain = 1.0
    for position, blocks in cuts:
        steps = jax.random.uniform(jax.random.fold_in(jax.random.fold_in(rng, 6), position), (blocks,), jnp.float32, least / len(cuts), high / len(cuts))
        gain = gain * jnp.repeat(jnp.exp(steps), dims[position] // blocks).reshape((-1,) + (1,) * (len(dims) - 1 - position))
    return gain


def noise(stream_key, shape, scale, limit, shards=(), kind=jnp.bfloat16):
    loudness = block_scale(stream_key, shape, shards, -0.22, 0.18) if shards else 1.0
    values = jax.random.normal(stream_key, shape, jnp.float32) * scale * loudness
    return jnp.minimum(jnp.maximum(values, -limit), limit).astype(kind)


def setup_inputs(seed: int = 0) -> dict:
    seeds = jax.random.split(jax.random.key(seed), 4)
    state = draw_state(jax.random.fold_in(seeds[3], 71), 0)
    bathymetry = noise(seeds[1], (3, 3, NXE, NYE), 0.3, 1.5, ((2, 8), (3, 32)), jnp.float32)
    flags = draw_flags(jax.random.fold_in(seeds[3], 71), 0)
    return {"state": state, "bathymetry": bathymetry, "flags": flags}


GRAV = 1.0
DRY = 0.05
COURANT = 0.05

def lagrange_terms(gauss_nodes, k):
    others = [gauss_nodes[m] for m in range(3) if m != k]
    denom = (gauss_nodes[k] - others[0]) * (gauss_nodes[k] - others[1])
    return (others[0] + others[1], others[0] * others[1], denom)

def value_at(terms, point):
    return (point * point - terms[0] * point + terms[1]) / terms[2]

def slope_at(terms, point):
    return (2.0 * point - terms[0]) / terms[2]

def integral_to(terms, point):
    return (point * point * point / 3.0 - terms[0] * point * point / 2.0 + terms[1] * point) / terms[2]

def invert_three(matrix):
    cofactor = [[0.0] * 3 for row in range(3)]
    for i in range(3):
        for j in range(3):
            rows = [r for r in range(3) if r != i]
            cols = [c for c in range(3) if c != j]
            minor = matrix[rows[0]][cols[0]] * matrix[rows[1]][cols[1]] - matrix[rows[0]][cols[1]] * matrix[rows[1]][cols[0]]
            cofactor[i][j] = minor * (1.0 if (i + j) % 2 == 0 else -1.0)
    determinant = sum((matrix[0][j] * cofactor[0][j] for j in range(3)))
    return [[cofactor[j][i] / determinant for j in range(3)] for i in range(3)]

def tables():
    spread = math.sqrt(15.0) / 10.0
    gauss_nodes = [0.5 - spread, 0.5, 0.5 + spread]
    weights = [5.0 / 18.0, 8.0 / 18.0, 5.0 / 18.0]
    lagrange = [lagrange_terms(gauss_nodes, k) for k in range(3)]
    derivative = [[slope_at(lagrange[k], gauss_nodes[i]) for k in range(3)] for i in range(3)]
    lower = [value_at(lagrange[k], 0.0) for k in range(3)]
    upper = [value_at(lagrange[k], 1.0) for k in range(3)]
    time_weights = [[integral_to(lagrange[n], gauss_nodes[m]) for n in range(3)] for m in range(3)]
    projector = [[7.0 * (integral_to(lagrange[k], (a + 1) / 7.0) - integral_to(lagrange[k], a / 7.0)) for k in range(3)] for a in range(7)]
    gram = [[sum((projector[a][i] * projector[a][j] for a in range(7))) for j in range(3)] for i in range(3)]
    inverse = invert_three(gram)
    restorer = [[sum((inverse[i][j] * projector[a][j] for j in range(3))) for a in range(7)] for i in range(3)]
    stiffness = [[weights[k] * derivative[k][i] / weights[i] for k in range(3)] for i in range(3)]
    return (weights, derivative, lower, upper, time_weights, projector, restorer, stiffness)

def velocity(depth, momentum):
    return momentum * depth / (depth * depth + DRY * DRY)

def celerity(depth):
    return jnp.sqrt(GRAV * jnp.sqrt(depth * depth + DRY * DRY))

def fluxes(state):
    depth, flow_x, flow_y = (state[0], state[1], state[2])
    speed_x = velocity(depth, flow_x)
    speed_y = velocity(depth, flow_y)
    pressure = 0.5 * GRAV * depth * depth
    return ((flow_x, flow_x * speed_x + pressure, flow_y * speed_x), (flow_y, flow_x * speed_y, flow_y * speed_y + pressure))

def rusanov(left, right, direction):
    flux_left = fluxes(left)[direction]
    flux_right = fluxes(right)[direction]
    signal = jnp.maximum(jnp.abs(velocity(left[0], left[1 + direction])) + celerity(left[0]), jnp.abs(velocity(right[0], right[1 + direction])) + celerity(right[0]))
    return tuple((0.5 * (flux_left[v] + flux_right[v]) - 0.5 * signal * (right[v] - left[v]) for v in range(3)))

def along_first(table, field):
    return jnp.stack([sum((table[i][k] * field[k] for k in range(3))) for i in range(len(table))])

def along_second(table, field):
    return jnp.stack([sum((table[i][k] * field[:, k] for k in range(3))) for i in range(len(table))], axis=1)

def trace_first(vector, field):
    return sum((vector[k] * field[k] for k in range(3)))

def trace_second(vector, field):
    return sum((vector[k] * field[:, k] for k in range(3)))

def dg_increment(padded):
    weights, derivative, lower, upper, time_weights, projector, restorer, stiffness = tables()
    start = (padded[0], padded[1], padded[2])
    bottom = padded[3]
    slope_x = along_first(derivative, bottom)
    slope_y = along_second(derivative, bottom)

    def rate(state):
        along_x, along_y = fluxes(state)
        result = [-(along_first(derivative, along_x[v]) + along_second(derivative, along_y[v])) for v in range(3)]
        result[1] = result[1] - GRAV * state[0] * slope_x
        result[2] = result[2] - GRAV * state[0] * slope_y
        return result
    levels = [start, start, start]
    for sweep in range(NPIC):
        if sweep == 0:
            first = rate(start)
            rates = [first, first, first]
        else:
            rates = [rate(level) for level in levels]
        levels = [tuple((start[v] + COURANT * sum((time_weights[m][n] * rates[n][v] for n in range(3))) for v in range(3))) for m in range(3)]
    inner = [tuple((level[v][:, :, 1:-1, 1:-1] for v in range(3))) for level in levels]
    inner_fluxes = [fluxes(level) for level in inner]
    result = []
    for v in range(3):
        mean_x = sum((weights[m] * inner_fluxes[m][0][v] for m in range(3)))
        mean_y = sum((weights[m] * inner_fluxes[m][1][v] for m in range(3)))
        result.append(along_first(stiffness, mean_x) + along_second(stiffness, mean_y))
    mean_depth = sum((weights[m] * inner[m][0] for m in range(3)))
    result[1] = result[1] - GRAV * mean_depth * slope_x[:, :, 1:-1, 1:-1]
    result[2] = result[2] - GRAV * mean_depth * slope_y[:, :, 1:-1, 1:-1]
    face_x = [0.0, 0.0, 0.0]
    face_y = [0.0, 0.0, 0.0]
    for m in range(3):
        east = tuple((trace_first(upper, levels[m][v][:, :, :, 1:-1]) for v in range(3)))
        west = tuple((trace_first(lower, levels[m][v][:, :, :, 1:-1]) for v in range(3)))
        numeric = rusanov(tuple((e[:, :-1] for e in east)), tuple((w[:, 1:] for w in west)), 0)
        face_x = [face_x[v] + weights[m] * numeric[v] for v in range(3)]
        north = tuple((trace_second(upper, levels[m][v][:, :, 1:-1, :]) for v in range(3)))
        south = tuple((trace_second(lower, levels[m][v][:, :, 1:-1, :]) for v in range(3)))
        numeric = rusanov(tuple((e[:, :, :-1] for e in north)), tuple((w[:, :, 1:] for w in south)), 1)
        face_y = [face_y[v] + weights[m] * numeric[v] for v in range(3)]
    for v in range(3):
        east_flux = face_x[v][:, 1:]
        west_flux = face_x[v][:, :-1]
        surface_x = jnp.stack([(upper[i] * east_flux - lower[i] * west_flux) / weights[i] for i in range(3)])
        north_flux = face_y[v][:, :, 1:]
        south_flux = face_y[v][:, :, :-1]
        surface_y = jnp.stack([(upper[j] * north_flux - lower[j] * south_flux) / weights[j] for j in range(3)], axis=1)
        result[v] = result[v] - surface_x - surface_y
    return jnp.stack(result)

def subcell_increment(block):
    tabs = tables()
    projector = jnp.asarray(tabs[5], jnp.float32)
    restorer = jnp.asarray(tabs[6], jnp.float32)
    exact = lax.Precision.HIGHEST
    own = jnp.einsum('ai,bj,qijn->qabn', projector, projector, block[0], precision=exact)
    west = jnp.einsum('i,bj,qijn->qbn', projector[6], projector, block[1], precision=exact)
    east = jnp.einsum('i,bj,qijn->qbn', projector[0], projector, block[2], precision=exact)
    south = jnp.einsum('ai,j,qijn->qan', projector, projector[6], block[3], precision=exact)
    north = jnp.einsum('ai,j,qijn->qan', projector, projector[0], block[4], precision=exact)
    wide_x = jnp.concatenate([west[:, None], own, east[:, None]], axis=1)
    wide_y = jnp.concatenate([south[:, :, None], own, north[:, :, None]], axis=2)
    flux_x = rusanov(tuple((wide_x[v, :-1] for v in range(3))), tuple((wide_x[v, 1:] for v in range(3))), 0)
    flux_y = rusanov(tuple((wide_y[v, :, :-1] for v in range(3))), tuple((wide_y[v, :, 1:] for v in range(3))), 1)
    change = [-(flux_x[v][1:] - flux_x[v][:-1]) - (flux_y[v][:, 1:] - flux_y[v][:, :-1]) for v in range(3)]
    change[1] = change[1] - GRAV * own[0] * 0.5 * (wide_x[3, 2:] - wide_x[3, :-2])
    change[2] = change[2] - GRAV * own[0] * 0.5 * (wide_y[3, :, 2:] - wide_y[3, :, :-2])
    return 7.0 * jnp.einsum('ia,jb,qabn->qijn', restorer, restorer, jnp.stack(change), precision=exact)

def to_block(payload):
    count = payload.shape[0]
    return payload.reshape(count, 5, 4, 3, 3).transpose(1, 2, 3, 4, 0)

def wall_pad(packed):
    sign_x = jnp.array([1.0, -1.0, 1.0, 1.0], jnp.float32).reshape(4, 1, 1, 1)
    sign_y = jnp.array([1.0, 1.0, -1.0, 1.0], jnp.float32).reshape(4, 1, 1, 1)
    padded = jnp.pad(packed, ((0, 0), (0, 0), (0, 0), (1, 1), (1, 1)))
    padded = padded.at[:, :, :, 0, 1:-1].set(packed[:, ::-1, :, 0] * sign_x)
    padded = padded.at[:, :, :, -1, 1:-1].set(packed[:, ::-1, :, -1] * sign_x)
    padded = padded.at[:, :, :, 1:-1, 0].set(packed[:, :, ::-1, :, 0] * sign_y)
    padded = padded.at[:, :, :, 1:-1, -1].set(packed[:, :, ::-1, :, -1] * sign_y)
    return padded

def reference(state, bathymetry, flags):
    packed = jnp.concatenate([state, bathymetry[None]], axis=0)
    padded = wall_pad(packed)
    strips = NXE // TX

    def strip(index):
        piece = lax.dynamic_slice_in_dim(padded, index * TX, TX + 2, 3)
        return dg_increment(piece)
    parts = lax.map(strip, jnp.arange(strips, dtype=jnp.int32))
    increment = jnp.moveaxis(parts, 0, 3).reshape(3, 3, 3, NXE, NYE)
    rows_x, rows_y = jnp.nonzero(flags, size=FLAGGED)
    rows_x = rows_x.astype(jnp.int32)
    rows_y = rows_y.astype(jnp.int32)
    span = NYE + 2
    centre = (rows_x + 1) * span + rows_y + 1
    offsets = jnp.array([0, -span, span, -1, 1], jnp.int32)
    table = padded.reshape(36, -1).T
    payload = table[centre[:, None] + offsets[None, :]].reshape(FLAGGED, 180)
    limited = subcell_increment(to_block(payload))
    return increment.at[:, :, :, rows_x, rows_y].set(limited)
```

```python
import math

import jax
import jax.numpy as jnp
from jax import lax
from jax.experimental import pallas as pl
from jax.experimental.pallas import tpu as pltpu
from jax.sharding import PartitionSpec as P

GRAV = 1.0
DRY2 = 0.05 * 0.05
COURANT = 0.05
SPREAD = math.sqrt(15.0) / 10.0
NODES = [0.5 - SPREAD, 0.5, 0.5 + SPREAD]
W = [5.0 / 18.0, 8.0 / 18.0, 5.0 / 18.0]


def _terms(k):
    o = [NODES[m] for m in range(3) if m != k]
    return o[0] + o[1], o[0] * o[1], (NODES[k] - o[0]) * (NODES[k] - o[1])


def _value(k, x):
    t = _terms(k)
    return (x * x - t[0] * x + t[1]) / t[2]


def _integral(k, x):
    t = _terms(k)
    return (x * x * x / 3.0 - t[0] * x * x / 2.0 + t[1] * x) / t[2]


UPPER = [_value(k, 1.0) for k in range(3)]
LOWER = [_value(k, 0.0) for k in range(3)]
AT = [[_integral(n, NODES[m]) for n in range(3)] for m in range(3)]
SLOPE = 0.5 / SPREAD
PA = 0.5 / SPREAD / 7.0
PE2 = 0.5 / (SPREAD * SPREAD) / 49.0
PE0 = PE2 / 12.0
_S2, _S4 = 28.0, 196.0
_DET = 7.0 * _S4 - _S2 * _S2


def _restorer():
    b0, b2 = -_S2 / _DET / PE2, 7.0 / _DET / PE2
    m0, m2 = _S4 / _DET - PE0 * b0, -_S2 / _DET - PE0 * b2
    return (m0, m2, m0 + b0 / 2.0, m2 + b2 / 2.0, 0.5 / _S2 / PA)


RM0, RM2, RE0, RE2, RA1 = _restorer()
NX, NY = 32, 128
F32 = jnp.float32


def deriv3(f0, f1, f2):
    a = f2 - f0
    e = f0 + f2
    c = (e + e) - 4.0 * f1
    return a - c, a, a + c


def stiff3(f0, f1, f2):
    a = f2 - f0
    g = f0 + f2 + 1.6 * f1
    a2 = a + a
    return a2 - g, -2.5 * a, a2 + g


def ends3(f0, f1, f2):
    m = (0.5 * (UPPER[0] + UPPER[2])) * (f0 + f2) + UPPER[1] * f1
    n = (0.5 * (UPPER[2] - UPPER[0])) * (f2 - f0)
    return m + n, m - n


def project7(f0, f1, f2):
    b = (f0 + f2) - (f1 + f1)
    x = PE2 * b
    y = PA * (f2 - f0)
    c = f1 + PE0 * b
    y2 = y + y
    y3 = y2 + y
    z1 = c + x
    z2 = c + 4.0 * x
    z3 = c + 9.0 * x
    return [z3 - y3, z2 - y2, z1 - y, c, z1 + y, z2 + y2, z3 + y3]


def project_ends(f0, f1, f2):
    b = (f0 + f2) - (f1 + f1)
    z = f1 + (PE0 + 9.0 * PE2) * b
    y = (3.0 * PA) * (f2 - f0)
    return z - y, z + y


def moments7(c):
    e1, a1 = c[4] + c[2], c[4] - c[2]
    e2, a2 = c[5] + c[1], c[5] - c[1]
    e3, a3 = c[6] + c[0], c[6] - c[0]
    return (
        (c[3] + e1) + (e2 + e3),
        a1 + (a2 + a2) + 3.0 * a3,
        e1 + 4.0 * e2 + 9.0 * e3,
    )


def nodes_of_moments(m0, m1, m2):
    e = RE0 * m0 + RE2 * m2
    a = RA1 * m1
    return e - a, RM0 * m0 + RM2 * m2, e + a


def node_fluxes(h, p, r):
    h2 = h * h
    y = lax.rsqrt(h2 + DRY2)
    k = h * (y * y)
    u = p * k
    pr = 0.5 * h2
    ru = r * u
    return p * u + pr, ru, r * (r * k) + pr


def side_flux(h, n, t):
    h2 = h * h
    y = lax.rsqrt(h2 + DRY2)
    u = n * (h * (y * y))
    return n, n * u + 0.5 * h2, t * u, jnp.abs(u) + lax.rsqrt(y)


def rusanov2(qa, fa, qb, fb):
    s = jnp.maximum(fa[3], fb[3])
    return [(fa[v] + fb[v]) - s * (qb[v] - qa[v]) for v in range(3)]


def grid3(f):
    return [[f(i, j) for j in range(3)] for i in range(3)]


def bottom_slopes(b):
    bx = [[None] * 3 for _ in range(3)]
    by = [[None] * 3 for _ in range(3)]
    for j in range(3):
        d = deriv3(b[0][j], b[1][j], b[2][j])
        for i in range(3):
            bx[i][j] = d[i]
    for i in range(3):
        by[i] = list(deriv3(b[i][0], b[i][1], b[i][2]))
    return bx, by


def rate(q, bx, by):
    fl = grid3(lambda i, j: node_fluxes(q[0][i][j], q[1][i][j], q[2][i][j]))
    pu = grid3(lambda i, j: fl[i][j][0])
    ru = grid3(lambda i, j: fl[i][j][1])
    rv = grid3(lambda i, j: fl[i][j][2])
    out = []
    for fx, gy in ((q[1], q[2]), (pu, ru), (ru, rv)):
        acc = [[None] * 3 for _ in range(3)]
        for j in range(3):
            d = deriv3(fx[0][j], fx[1][j], fx[2][j])
            for i in range(3):
                acc[i][j] = d[i]
        for i in range(3):
            d = deriv3(gy[i][0], gy[i][1], gy[i][2])
            for j in range(3):
                acc[i][j] = acc[i][j] + d[j]
        out.append(acc)
    for i in range(3):
        for j in range(3):
            out[1][i][j] = out[1][i][j] + q[0][i][j] * bx[i][j]
            out[2][i][j] = out[2][i][j] + q[0][i][j] * by[i][j]
    return out


def predict(q0, bx, by):
    f = -COURANT * SLOPE
    r = rate(q0, bx, by)
    lv = [[None] * 3 for _ in range(3)]
    for v in range(3):
        mid = grid3(lambda i, j: q0[v][i][j] + (f * 0.5) * r[v][i][j])
        dif = grid3(lambda i, j: (f * SPREAD) * r[v][i][j])
        lv[0][v] = grid3(lambda i, j: mid[i][j] - dif[i][j])
        lv[1][v] = mid
        lv[2][v] = grid3(lambda i, j: mid[i][j] + dif[i][j])
    ka = f * W[0] / 2.0
    kb = f * W[1] / 2.0
    k1 = f * (AT[1][0] - W[0] / 2.0)
    k2 = f * (AT[0][2] - W[2] / 2.0)
    for _ in range(2):
        rs = [rate(lv[m], bx, by) for m in range(3)]
        new = [[[[None] * 3 for _ in range(3)] for _ in range(3)] for _ in range(3)]
        for v in range(3):
            for i in range(3):
                for j in range(3):
                    r0, r1, r2 = rs[0][v][i][j], rs[1][v][i][j], rs[2][v][i][j]
                    base = q0[v][i][j] + ka * (r0 + r2) + kb * r1
                    c1 = (2.0 * k2) * r1
                    new[0][v][i][j] = base + (c1 + k2 * r2)
                    new[1][v][i][j] = base + k1 * (r0 - r2)
                    new[2][v][i][j] = base - (c1 + k2 * r0)
        lv = new
    return lv


def face_mean(f):
    return [(f[0][v] + f[2][v]) + 1.6 * f[1][v] for v in range(3)]


def volume(lv, bx, by):
    fl = [grid3(lambda i, j: node_fluxes(lv[m][0][i][j], lv[m][1][i][j], lv[m][2][i][j])) for m in range(3)]

    def mean(get):
        return grid3(lambda i, j: (get(0, i, j) + get(2, i, j)) + 1.6 * get(1, i, j))

    hm, pm, rm = [mean(lambda m, i, j: lv[m][v][i][j]) for v in range(3)]
    pu, ru, rv = [mean(lambda m, i, j: fl[m][i][j][c]) for c in range(3)]
    out = []
    for fx, gy in ((pm, rm), (pu, ru), (ru, rv)):
        acc = [[None] * 3 for _ in range(3)]
        for j in range(3):
            d = stiff3(fx[0][j], fx[1][j], fx[2][j])
            for i in range(3):
                acc[i][j] = d[i]
        for i in range(3):
            d = stiff3(gy[i][0], gy[i][1], gy[i][2])
            for j in range(3):
                acc[i][j] = acc[i][j] + d[j]
        out.append(acc)
    for i in range(3):
        for j in range(3):
            out[1][i][j] = out[1][i][j] - hm[i][j] * bx[i][j]
            out[2][i][j] = out[2][i][j] - hm[i][j] * by[i][j]
    return out


def traces_x(lv):
    up = [[[None] * 3 for _ in range(3)] for _ in range(3)]
    lo = [[[None] * 3 for _ in range(3)] for _ in range(3)]
    for m in range(3):
        for v in range(3):
            for j in range(3):
                up[m][v][j], lo[m][v][j] = ends3(lv[m][v][0][j], lv[m][v][1][j], lv[m][v][2][j])
    return up, lo


def traces_y(lv):
    up = [[[None] * 3 for _ in range(3)] for _ in range(3)]
    lo = [[[None] * 3 for _ in range(3)] for _ in range(3)]
    for m in range(3):
        for v in range(3):
            for i in range(3):
                up[m][v][i], lo[m][v][i] = ends3(lv[m][v][i][0], lv[m][v][i][1], lv[m][v][i][2])
    return up, lo


def lift(acc, lo, up, along_x, scale):
    ko = [scale * LOWER[i] / W[i] for i in range(3)]
    for v in range(3):
        for t in range(3):
            d = lo[v][t] - up[v][t]
            c = ko[1] * d
            x = ko[0] * lo[v][t] - ko[2] * up[v][t]
            z = ko[2] * lo[v][t] - ko[0] * up[v][t]
            for n, k in enumerate((x, c, z)):
                if along_x:
                    acc[v][n][t] = acc[v][n][t] + k
                else:
                    acc[v][t][n] = acc[v][t][n] + k
    return acc


NT = 27
NU = 28


def k27(a, b, c):
    return a * 9 + b * 3 + c


def lane(x, k):
    return jnp.broadcast_to(x[:, k : k + 1], (8, NY))


def body(walls, st, bt, fg, oxl, oxu, oyl, oyu, ixl, ixu, iyl, iyu, out,
         own, rec, te, tw, u6, u0, zz, zt, part, mom, fx):
    sub = lax.broadcasted_iota(jnp.int32, (8, NY), 0)
    lan = lax.broadcasted_iota(jnp.int32, (8, NY), 1)

    own[...] = jnp.zeros((36, 8, NY), F32)
    rec[...] = jnp.zeros((36, 8, NY), F32)
    own[:, 7, :] = oxl[...]
    own[:, 0, :] = oxu[...]
    own[:, 2, 0:NX] = oyl[...]
    own[:, 3, 0:NX] = oyu[...]
    rec[:, 7, :] = ixl[...]
    rec[:, 0, :] = ixu[...]
    rec[:, 2, 0:NX] = iyl[...]
    rec[:, 3, 0:NX] = iyu[...]
    isx = (sub == 7) | (sub == 0)
    atwall = (
        ((sub == 7) & (walls[0] > 0))
        | ((sub == 0) & (walls[1] > 0))
        | ((sub == 2) & (walls[2] > 0))
        | ((sub == 3) & (walls[3] > 0))
    )
    sgn_x = jnp.where(isx, -1.0, 1.0).astype(F32)
    sgn_y = -sgn_x

    def halo(v, i, j):
        m = jnp.where(isx, own[k27(v, 2 - i, j)], own[k27(v, i, 2 - j)])
        if v == 1:
            m = m * sgn_x
        if v == 2:
            m = m * sgn_y
        return jnp.where(atwall, m, rec[k27(v, i, j)])

    q = [grid3(lambda i, j: halo(v, i, j)) for v in range(4)]
    bx, by = bottom_slopes(q[3])
    lv = predict(q[:3], bx, by)
    up, lo = traces_x(lv)
    for m in range(3):
        for v in range(3):
            for j in range(3):
                te[k27(m, v, j), 0:8, :] = up[m][v][j]
                tw[k27(m, v, j), 40:48, :] = lo[m][v][j]
    up, lo = traces_y(lv)
    for m in range(3):
        for v in range(3):
            for i in range(3):
                zz[k27(m, v, i)] = up[m][v][i]
                zz[NT + NU + k27(m, v, i)] = lo[m][v][i]
    for v in range(4):
        e = [project_ends(q[v][0][j], q[v][1][j], q[v][2][j]) for j in range(3)]
        c0 = project7(e[0][0], e[1][0], e[2][0])
        c6 = project7(e[0][1], e[1][1], e[2][1])
        for b in range(7):
            u6[v * 7 + b, 0:8, :] = c6[b]
            u0[v * 7 + b, 40:48, :] = c0[b]
        e = [project_ends(q[v][i][0], q[v][i][1], q[v][i][2]) for i in range(3)]
        c0 = project7(e[0][0], e[1][0], e[2][0])
        c6 = project7(e[0][1], e[1][1], e[2][1])
        for a in range(7):
            zz[NT + v * 7 + a] = c6[a]
            zz[NT + NU + NT + v * 7 + a] = c0[a]
    low = zz[0 : NT + NU, 2, :]
    high = zz[NT + NU : 2 * (NT + NU), 3, :]
    both = jnp.concatenate([low, high, jnp.zeros((128 - 2 * (NT + NU), NY), F32)], 0)
    zt[...] = both.T

    first_lane = lan == 0
    last_lane = lan == NY - 1

    def from_lower(x, k, z):
        return jnp.where(first_lane, lane(z, k), pltpu.roll(x, 1, 1))

    def from_upper(x, k, z):
        return jnp.where(last_lane, lane(z, k), pltpu.roll(x, NY - 1, 1))

    def tile(t, carry):
        row = pl.multiple_of(t * 8, 8)
        rows = pl.ds(row, 8)
        wide = pl.ds(pl.multiple_of(t * 8 + 8, 8), 8)
        z = zt[rows, :]
        q = [grid3(lambda i, j: st[k27(v, i, j), rows, :]) for v in range(3)]
        b = grid3(lambda i, j: bt[i * 3 + j, rows, :])
        bx, by = bottom_slopes(b)
        lv = predict(q, bx, by)
        acc = volume(lv, bx, by)
        up, lo = traces_x(lv)
        for m in range(3):
            for v in range(3):
                for j in range(3):
                    te[k27(m, v, j), wide, :] = up[m][v][j]
                    tw[k27(m, v, j), wide, :] = lo[m][v][j]
        up, lo = traces_y(lv)
        flo = [[None] * 3 for _ in range(3)]
        fup = [[None] * 3 for _ in range(3)]
        for i in range(3):
            fl, fu = [], []
            for m in range(3):
                a = [up[m][v][i] for v in (0, 2, 1)]
                c = [lo[m][v][i] for v in (0, 2, 1)]
                nb = [from_upper(lo[m][v][i], NT + NU + k27(m, v, i), z) for v in (0, 2, 1)]
                fu.append(rusanov2(a, side_flux(*a), nb, side_flux(*nb)))
                na = [lane(z, k27(m, v, i)) for v in (0, 2, 1)]
                fl.append((na, c))
            fum = face_mean(fu)
            edge = []
            for m in range(3):
                na, c = fl[m]
                edge.append(rusanov2(na, side_flux(*na), c, side_flux(*c)))
            edm = face_mean(edge)
            for s, v in enumerate((0, 2, 1)):
                fup[v][i] = fum[s]
                flo[v][i] = jnp.where(first_lane, edm[s], pltpu.roll(fum[s], 1, 1))
        acc = lift(acc, flo, fup, False, 0.5 / SLOPE)
        for v in range(3):
            for i in range(3):
                for j in range(3):
                    part[k27(v, i, j), rows, :] = acc[v][i][j]
        q = q + [b]
        cols = [[project7(q[v][0][j], q[v][1][j], q[v][2][j]) for j in range(3)] for v in range(4)]
        cell = [[None] * 4 for _ in range(7)]
        for a in range(7):
            for v in range(4):
                cell[a][v] = project7(cols[v][0][a], cols[v][1][a], cols[v][2][a])
        for v in range(4):
            for c in range(7):
                u0[v * 7 + c, wide, :] = cell[0][v][c]
                u6[v * 7 + c, wide, :] = cell[6][v][c]
        rowm = []
        prev = None
        fxs_prev = None
        pending = None
        for a in range(7):
            hs, ps, rs, bs = cell[a]
            fl = []
            for c in range(7):
                h, p, r = hs[c], ps[c], rs[c]
                h2 = h * h
                y = lax.rsqrt(h2 + DRY2)
                k = h * (y * y)
                u = p * k
                w = r * k
                pr = 0.5 * h2
                ru = r * u
                cc = lax.rsqrt(y)
                fl.append((p * u + pr, ru, r * w + pr, jnp.abs(u) + cc, jnp.abs(w) + cc))
            gy = []
            for c in range(6):
                s = jnp.maximum(fl[c][4], fl[c + 1][4])
                gy.append(
                    (
                        (rs[c] + rs[c + 1]) - s * (hs[c + 1] - hs[c]),
                        (fl[c][1] + fl[c + 1][1]) - s * (ps[c + 1] - ps[c]),
                        (fl[c][2] + fl[c + 1][2]) - s * (rs[c + 1] - rs[c]),
                    )
                )
            base = NT + NU + NT
            nb = [from_upper(cell[a][v][0], base + v * 7 + a, z) for v in (0, 2, 1)]
            own_q = [hs[6], rs[6], ps[6]]
            gu = rusanov2(own_q, (rs[6], fl[6][2], fl[6][1], fl[6][4]), nb, side_flux(*nb))
            na = [lane(z, NT + v * 7 + a) for v in (0, 2, 1)]
            ge = rusanov2(na, side_flux(*na), [hs[0], rs[0], ps[0]], (rs[0], fl[0][2], fl[0][1], fl[0][4]))
            gl = [jnp.where(first_lane, ge[n], pltpu.roll(gu[n], 1, 1)) for n in range(3)]
            gy = [(gl[0], gl[2], gl[1])] + gy + [(gu[0], gu[2], gu[1])]
            b_hi = from_upper(bs[0], base + 21 + a, z)
            b_lo = from_lower(bs[6], NT + 21 + a, z)
            bw = [b_lo] + bs + [b_hi]
            ch = [[gy[c][v] - gy[c + 1][v] for c in range(7)] for v in range(3)]
            ch[2] = [ch[2][c] - hs[c] * (bw[c + 2] - bw[c]) for c in range(7)]
            if prev is not None:
                ph, pp, prr, pb, pfl, pch = prev
                fxs = []
                for c in range(7):
                    s = jnp.maximum(pfl[c][3], fl[c][3])
                    fxs.append(
                        (
                            (pp[c] + ps[c]) - s * (hs[c] - ph[c]),
                            (pfl[c][0] + fl[c][0]) - s * (ps[c] - pp[c]),
                            (pfl[c][1] + fl[c][1]) - s * (rs[c] - prr[c]),
                        )
                    )
                for v in range(3):
                    pch[v] = [pch[v][c] - fxs[c][v] for c in range(7)]
                    ch[v] = [ch[v][c] + fxs[c][v] for c in range(7)]
                if a >= 2:
                    bb = [bs[c] - cell[a - 2][3][c] for c in range(7)]
                else:
                    bb = bs
                pch[1] = [pch[1][c] - ph[c] * bb[c] for c in range(7)]
                rowm.append([moments7(pch[v]) for v in range(3)])
            prev = (hs, ps, rs, bs, fl, ch)
        hs = prev[0]
        ch = prev[5]
        ch[1] = [ch[1][c] + hs[c] * cell[5][3][c] for c in range(7)]
        rowm.append([moments7(ch[v]) for v in range(3)])
        for v in range(3):
            for n in range(3):
                mm = moments7([rowm[a][v][n] for a in range(7)])
                for m in range(3):
                    mom[k27(v, m, n), rows, :] = mm[m]
        return carry

    lax.fori_loop(0, NX // 8, tile, 0)

    def faces(t, carry):
        here = pl.ds(pl.multiple_of(t * 8 + 8, 8), 8)
        back = pl.ds(t * 8 + 7, 8)
        dst = pl.ds(pl.multiple_of(t * 8, 8), 8)
        for j in range(3):
            f = []
            for m in range(3):
                qa = [te[k27(m, v, j), back, :] for v in range(3)]
                qb = [tw[k27(m, v, j), here, :] for v in range(3)]
                f.append(rusanov2(qa, side_flux(*qa), qb, side_flux(*qb)))
            f = face_mean(f)
            for v in range(3):
                fx[v * 3 + j, dst, :] = f[v]
        cs = []
        for c in range(7):
            qa = [u6[v * 7 + c, back, :] for v in range(3)]
            qb = [u0[v * 7 + c, here, :] for v in range(3)]
            cs.append(rusanov2(qa, side_flux(*qa), qb, side_flux(*qb)))
        for v in range(3):
            mm = moments7([cs[c][v] for c in range(7)])
            for n in range(3):
                fx[9 + v * 3 + n, dst, :] = mm[n]
        return carry

    lax.fori_loop(0, NX // 8 + 1, faces, 0)

    def finish(t, carry):
        rows = pl.ds(pl.multiple_of(t * 8, 8), 8)
        wide = pl.ds(pl.multiple_of(t * 8 + 8, 8), 8)
        back = pl.ds(t * 8 + 7, 8)
        front = pl.ds(t * 8 + 9, 8)
        nxt = pl.ds(t * 8 + 1, 8)
        acc = [grid3(lambda i, j: part[k27(v, i, j), rows, :]) for v in range(3)]
        flo = [[fx[v * 3 + j, rows, :] for j in range(3)] for v in range(3)]
        fup = [[fx[v * 3 + j, nxt, :] for j in range(3)] for v in range(3)]
        acc = lift(acc, flo, fup, True, 0.5 / SLOPE)
        mm = [grid3(lambda m, n: mom[k27(v, m, n), rows, :]) for v in range(3)]
        slo = moments7([u0[c, wide, :] * u6[21 + c, back, :] for c in range(7)])
        shi = moments7([u6[c, wide, :] * u0[21 + c, front, :] for c in range(7)])
        flag = fg[rows, :] > 0
        for v in range(3):
            grid = [[None] * 3 for _ in range(3)]
            for n in range(3):
                lo_ = fx[9 + v * 3 + n, rows, :]
                hi_ = fx[9 + v * 3 + n, nxt, :]
                if v == 1:
                    lo_ = lo_ + slo[n]
                    hi_ = hi_ + shi[n]
                s = lo_ - hi_
                d = lo_ + hi_
                c = nodes_of_moments(mm[v][0][n] + s, mm[v][1][n] - 3.0 * d, mm[v][2][n] + 9.0 * s)
                for i in range(3):
                    grid[i][n] = c[i]
            for i in range(3):
                c = nodes_of_moments(grid[i][0], grid[i][1], grid[i][2])
                for j in range(3):
                    out[k27(v, i, j), rows, :] = jnp.where(
                        flag, 3.5 * c[j], (SLOPE * W[0]) * acc[v][i][j]
                    )
        return carry

    lax.fori_loop(0, NX // 8, finish, 0)


def shards(state, bathymetry, flags):
    st = state.reshape(27, NX, NY)
    bt = bathymetry.reshape(9, NX, NY)
    nx, ny = lax.axis_size("gx"), lax.axis_size("gy")
    ix, iy = lax.axis_index("gx"), lax.axis_index("gy")
    packed = jnp.concatenate([st, bt], axis=0)
    oxl, oxu = packed[:, 0, :], packed[:, NX - 1, :]
    oyl, oyu = packed[:, :, 0], packed[:, :, NY - 1]
    up_x = [(i, (i + 1) % nx) for i in range(nx)]
    dn_x = [(j, i) for i, j in up_x]
    up_y = [(i, (i + 1) % ny) for i in range(ny)]
    dn_y = [(j, i) for i, j in up_y]
    ixl = lax.ppermute(oxu, "gx", up_x)
    ixu = lax.ppermute(oxl, "gx", dn_x)
    iyl = lax.ppermute(oyu, "gy", up_y)
    iyu = lax.ppermute(oyl, "gy", dn_y)
    walls = jnp.stack([ix == 0, ix == nx - 1, iy == 0, iy == ny - 1]).astype(jnp.int32)
    vm = pl.BlockSpec(memory_space=pltpu.VMEM)
    out = pl.pallas_call(
        body,
        out_shape=jax.ShapeDtypeStruct((27, NX, NY), F32),
        in_specs=[pl.BlockSpec(memory_space=pltpu.SMEM)] + [vm] * 11,
        out_specs=vm,
        scratch_shapes=[
            pltpu.VMEM((36, 8, NY), F32),
            pltpu.VMEM((36, 8, NY), F32),
            pltpu.VMEM((NT, 48, NY), F32),
            pltpu.VMEM((NT, 48, NY), F32),
            pltpu.VMEM((NU, 48, NY), F32),
            pltpu.VMEM((NU, 48, NY), F32),
            pltpu.VMEM((2 * (NT + NU), 8, NY), F32),
            pltpu.VMEM((NY, NY), F32),
            pltpu.VMEM((27, NX, NY), F32),
            pltpu.VMEM((27, NX, NY), F32),
            pltpu.VMEM((18, 40, NY), F32),
        ],
        compiler_params=pltpu.CompilerParams(vmem_limit_bytes=48 * 1024 * 1024),
        name="step",
    )(walls, st, bt, flags, oxl, oxu, oyl, oyu, ixl, ixu, iyl, iyu)
    return out.reshape(3, 3, 3, NX, NY)


def solution(mesh):
    in_specs = (P(None, None, None, "gx", "gy"), P(None, None, "gx", "gy"), P("gx", "gy"))
    out_specs = P(None, None, None, "gx", "gy")
    return jax.shard_map(shards, mesh=mesh, in_specs=in_specs, out_specs=out_specs, check_vma=False)
```

```python
import math

import jax
import jax.numpy as jnp
from jax import lax
from jax.experimental import pallas as pl
from jax.experimental.pallas import tpu as pltpu
from jax.sharding import PartitionSpec as P

GRAV = 1.0
DRY2 = 0.05 * 0.05
COURANT = 0.05
SPREAD = math.sqrt(15.0) / 10.0
NODES = [0.5 - SPREAD, 0.5, 0.5 + SPREAD]
W = [5.0 / 18.0, 8.0 / 18.0, 5.0 / 18.0]


def _terms(k):
    o = [NODES[m] for m in range(3) if m != k]
    return o[0] + o[1], o[0] * o[1], (NODES[k] - o[0]) * (NODES[k] - o[1])


def _value(k, x):
    t = _terms(k)
    return (x * x - t[0] * x + t[1]) / t[2]


def _integral(k, x):
    t = _terms(k)
    return (x * x * x / 3.0 - t[0] * x * x / 2.0 + t[1] * x) / t[2]


UPPER = [_value(k, 1.0) for k in range(3)]
LOWER = [_value(k, 0.0) for k in range(3)]
AT = [[_integral(n, NODES[m]) for n in range(3)] for m in range(3)]
SLOPE = 0.5 / SPREAD
PA = 0.5 / SPREAD / 7.0
PE2 = 0.5 / (SPREAD * SPREAD) / 49.0
PE0 = PE2 / 12.0
_S2, _S4 = 28.0, 196.0
_DET = 7.0 * _S4 - _S2 * _S2


def _restorer():
    b0, b2 = -_S2 / _DET / PE2, 7.0 / _DET / PE2
    m0, m2 = _S4 / _DET - PE0 * b0, -_S2 / _DET - PE0 * b2
    return (m0, m2, m0 + b0 / 2.0, m2 + b2 / 2.0, 0.5 / _S2 / PA)


RM0, RM2, RE0, RE2, RA1 = _restorer()
NX, NY = 32, 128
F32 = jnp.float32


def deriv3(f0, f1, f2):
    a = f2 - f0
    e = f0 + f2
    c = (e + e) - 4.0 * f1
    return a - c, a, a + c


def stiff3(f0, f1, f2):
    a = f2 - f0
    g = f0 + f2 + 1.6 * f1
    a2 = a + a
    return a2 - g, -2.5 * a, a2 + g


def ends3(f0, f1, f2):
    m = (0.5 * (UPPER[0] + UPPER[2])) * (f0 + f2) + UPPER[1] * f1
    n = (0.5 * (UPPER[2] - UPPER[0])) * (f2 - f0)
    return m + n, m - n


def project7(f0, f1, f2):
    b = (f0 + f2) - (f1 + f1)
    x = PE2 * b
    y = PA * (f2 - f0)
    c = f1 + PE0 * b
    y2 = y + y
    y3 = y2 + y
    z1 = c + x
    z2 = c + 4.0 * x
    z3 = c + 9.0 * x
    return [z3 - y3, z2 - y2, z1 - y, c, z1 + y, z2 + y2, z3 + y3]


def project_ends(f0, f1, f2):
    b = (f0 + f2) - (f1 + f1)
    z = f1 + (PE0 + 9.0 * PE2) * b
    y = (3.0 * PA) * (f2 - f0)
    return z - y, z + y


def moments7(c):
    e1, a1 = c[4] + c[2], c[4] - c[2]
    e2, a2 = c[5] + c[1], c[5] - c[1]
    e3, a3 = c[6] + c[0], c[6] - c[0]
    return (
        (c[3] + e1) + (e2 + e3),
        a1 + (a2 + a2) + 3.0 * a3,
        e1 + 4.0 * e2 + 9.0 * e3,
    )


def nodes_of_moments(m0, m1, m2):
    e = RE0 * m0 + RE2 * m2
    a = RA1 * m1
    return e - a, RM0 * m0 + RM2 * m2, e + a


def node_fluxes(h, p, r):
    h2 = h * h
    y = lax.rsqrt(h2 + DRY2)
    k = h * (y * y)
    u = p * k
    pr = 0.5 * h2
    ru = r * u
    return p * u + pr, ru, r * (r * k) + pr


def side_flux(h, n, t):
    h2 = h * h
    y = lax.rsqrt(h2 + DRY2)
    u = n * (h * (y * y))
    return n, n * u + 0.5 * h2, t * u, jnp.abs(u) + lax.rsqrt(y)


def rusanov2(qa, fa, qb, fb):
    s = jnp.maximum(fa[3], fb[3])
    return [(fa[v] + fb[v]) - s * (qb[v] - qa[v]) for v in range(3)]


def grid3(f):
    return [[f(i, j) for j in range(3)] for i in range(3)]


def bottom_slopes(b):
    bx = [[None] * 3 for _ in range(3)]
    by = [[None] * 3 for _ in range(3)]
    for j in range(3):
        d = deriv3(b[0][j], b[1][j], b[2][j])
        for i in range(3):
            bx[i][j] = d[i]
    for i in range(3):
        by[i] = list(deriv3(b[i][0], b[i][1], b[i][2]))
    return bx, by


def rate(q, bx, by):
    fl = grid3(lambda i, j: node_fluxes(q[0][i][j], q[1][i][j], q[2][i][j]))
    pu = grid3(lambda i, j: fl[i][j][0])
    ru = grid3(lambda i, j: fl[i][j][1])
    rv = grid3(lambda i, j: fl[i][j][2])
    out = []
    for fx, gy in ((q[1], q[2]), (pu, ru), (ru, rv)):
        acc = [[None] * 3 for _ in range(3)]
        for j in range(3):
            d = deriv3(fx[0][j], fx[1][j], fx[2][j])
            for i in range(3):
                acc[i][j] = d[i]
        for i in range(3):
            d = deriv3(gy[i][0], gy[i][1], gy[i][2])
            for j in range(3):
                acc[i][j] = acc[i][j] + d[j]
        out.append(acc)
    for i in range(3):
        for j in range(3):
            out[1][i][j] = out[1][i][j] + q[0][i][j] * bx[i][j]
            out[2][i][j] = out[2][i][j] + q[0][i][j] * by[i][j]
    return out


def predict(q0, bx, by):
    f = -COURANT * SLOPE
    r = rate(q0, bx, by)
    lv = [[None] * 3 for _ in range(3)]
    for v in range(3):
        mid = grid3(lambda i, j: q0[v][i][j] + (f * 0.5) * r[v][i][j])
        dif = grid3(lambda i, j: (f * SPREAD) * r[v][i][j])
        lv[0][v] = grid3(lambda i, j: mid[i][j] - dif[i][j])
        lv[1][v] = mid
        lv[2][v] = grid3(lambda i, j: mid[i][j] + dif[i][j])
    ka = f * W[0] / 2.0
    kb = f * W[1] / 2.0
    k1 = f * (AT[1][0] - W[0] / 2.0)
    k2 = f * (AT[0][2] - W[2] / 2.0)
    for _ in range(2):
        rs = [rate(lv[m], bx, by) for m in range(3)]
        new = [[[[None] * 3 for _ in range(3)] for _ in range(3)] for _ in range(3)]
        for v in range(3):
            for i in range(3):
                for j in range(3):
                    r0, r1, r2 = rs[0][v][i][j], rs[1][v][i][j], rs[2][v][i][j]
                    base = q0[v][i][j] + ka * (r0 + r2) + kb * r1
                    c1 = (2.0 * k2) * r1
                    new[0][v][i][j] = base + (c1 + k2 * r2)
                    new[1][v][i][j] = base + k1 * (r0 - r2)
                    new[2][v][i][j] = base - (c1 + k2 * r0)
        lv = new
    return lv


def face_mean(f):
    return [(f[0][v] + f[2][v]) + 1.6 * f[1][v] for v in range(3)]


def volume(lv, bx, by):
    fl = [grid3(lambda i, j: node_fluxes(lv[m][0][i][j], lv[m][1][i][j], lv[m][2][i][j])) for m in range(3)]

    def mean(get):
        return grid3(lambda i, j: (get(0, i, j) + get(2, i, j)) + 1.6 * get(1, i, j))

    hm, pm, rm = [mean(lambda m, i, j: lv[m][v][i][j]) for v in range(3)]
    pu, ru, rv = [mean(lambda m, i, j: fl[m][i][j][c]) for c in range(3)]
    out = []
    for fx, gy in ((pm, rm), (pu, ru), (ru, rv)):
        acc = [[None] * 3 for _ in range(3)]
        for j in range(3):
            d = stiff3(fx[0][j], fx[1][j], fx[2][j])
            for i in range(3):
                acc[i][j] = d[i]
        for i in range(3):
            d = stiff3(gy[i][0], gy[i][1], gy[i][2])
            for j in range(3):
                acc[i][j] = acc[i][j] + d[j]
        out.append(acc)
    for i in range(3):
        for j in range(3):
            out[1][i][j] = out[1][i][j] - hm[i][j] * bx[i][j]
            out[2][i][j] = out[2][i][j] - hm[i][j] * by[i][j]
    return out


def traces_x(lv):
    up = [[[None] * 3 for _ in range(3)] for _ in range(3)]
    lo = [[[None] * 3 for _ in range(3)] for _ in range(3)]
    for m in range(3):
        for v in range(3):
            for j in range(3):
                up[m][v][j], lo[m][v][j] = ends3(lv[m][v][0][j], lv[m][v][1][j], lv[m][v][2][j])
    return up, lo


def traces_y(lv):
    up = [[[None] * 3 for _ in range(3)] for _ in range(3)]
    lo = [[[None] * 3 for _ in range(3)] for _ in range(3)]
    for m in range(3):
        for v in range(3):
            for i in range(3):
                up[m][v][i], lo[m][v][i] = ends3(lv[m][v][i][0], lv[m][v][i][1], lv[m][v][i][2])
    return up, lo


def lift(acc, lo, up, along_x, scale):
    ko = [scale * LOWER[i] / W[i] for i in range(3)]
    for v in range(3):
        for t in range(3):
            d = lo[v][t] - up[v][t]
            c = ko[1] * d
            x = ko[0] * lo[v][t] - ko[2] * up[v][t]
            z = ko[2] * lo[v][t] - ko[0] * up[v][t]
            for n, k in enumerate((x, c, z)):
                if along_x:
                    acc[v][n][t] = acc[v][n][t] + k
                else:
                    acc[v][t][n] = acc[v][t][n] + k
    return acc


NT = 27
NS = 40
TILES = NX // 8


def k27(a, b, c):
    return a * 9 + b * 3 + c


def lane(x, k):
    return jnp.broadcast_to(x[:, k : k + 1], (8, NY))


def down(x):
    return pltpu.roll(x, NY - 1, 1)


def up1(x):
    return pltpu.roll(x, 1, 1)


def iotas():
    return (
        lax.broadcasted_iota(jnp.int32, (8, NY), 0),
        lax.broadcasted_iota(jnp.int32, (8, NY), 1),
    )


def dg_body(st, bt, fg, dg, ax, bx_, ay, by_, te, tw, part, fx, ends, sq):
    sub, lan = iotas()
    first_lane = lan == 0
    last_lane = lan == NY - 1
    sq[NX:, :] = jnp.zeros((NY - NX, NY), F32)
    for n in range(9):
        fx[n, NX : NX + 8, :] = jnp.zeros((8, NY), F32)
    for k in range(NT):
        te[k, 0:8, :] = jnp.zeros((8, NY), F32)

    def tile(t, carry):
        rows = pl.ds(pl.multiple_of(t * 8, 8), 8)
        wide = pl.ds(pl.multiple_of(t * 8 + 8, 8), 8)
        q = [grid3(lambda i, j: st[k27(v, i, j), rows, :]) for v in range(3)]
        b = grid3(lambda i, j: bt[i * 3 + j, rows, :])
        bx, by = bottom_slopes(b)
        lv = predict(q, bx, by)
        acc = volume(lv, bx, by)
        up, lo = traces_x(lv)
        for m in range(3):
            for v in range(3):
                for j in range(3):
                    te[k27(m, v, j), wide, :] = up[m][v][j]
                    tw[k27(m, v, j), rows, :] = lo[m][v][j]
        up, lo = traces_y(lv)
        col = jnp.zeros((8, NY), F32)

        def put(col, k, x_lo, x_up):
            col = jnp.where(lan == k, lane(x_lo, 0), col)
            return jnp.where(lan == 64 + k, lane(x_up, NY - 1), col)

        for m in range(3):
            for c, v in enumerate((0, 2, 1)):
                for i in range(3):
                    col = put(col, k27(m, c, i), lo[m][v][i], up[m][v][i])
        for c, f in enumerate((q[0], q[2], q[1], b)):
            for i in range(3):
                e0, e6 = project_ends(f[i][0], f[i][1], f[i][2])
                col = put(col, NT + c * 3 + i, e0, e6)
        f = fg[rows, :].astype(F32)
        sq[rows, :] = put(col, NS - 1, f, f)
        flo = [[None] * 3 for _ in range(3)]
        fup = [[None] * 3 for _ in range(3)]
        for i in range(3):
            fu = []
            for m in range(3):
                qa = [up[m][v][i] for v in (0, 2, 1)]
                qb = [lo[m][v][i] for v in (0, 2, 1)]
                fb = side_flux(*qb)
                qn = [down(x) for x in qb]
                fn = [qn[1]] + [down(x) for x in fb[1:]]
                fu.append(rusanov2(qa, side_flux(*qa), qn, fn))
            fum = face_mean(fu)
            for s, v in enumerate((0, 2, 1)):
                fup[v][i] = jnp.where(last_lane, 0.0, fum[s])
                flo[v][i] = up1(fup[v][i])
        acc = lift(acc, flo, fup, False, 0.5 / SLOPE)
        for v in range(3):
            for i in range(3):
                for j in range(3):
                    part[k27(v, i, j), rows, :] = acc[v][i][j]
        return carry

    lax.fori_loop(0, TILES, tile, 0)

    for c in range(4):
        for j in range(3):
            if c < 3:
                lo_f = [st[k27(c, i, j), 0:8, :] for i in range(3)]
                up_f = [st[k27(c, i, j), NX - 8 : NX, :] for i in range(3)]
            else:
                lo_f = [bt[i * 3 + j, 0:8, :] for i in range(3)]
                up_f = [bt[i * 3 + j, NX - 8 : NX, :] for i in range(3)]
            ends[c * 3 + j, 0:8, :] = project_ends(*lo_f)[0]
            ends[c * 3 + j, 8:16, :] = project_ends(*up_f)[1]
    even_x = lax.axis_index("gx") % 2 == 0
    even_y = lax.axis_index("gy") % 2 == 0
    sets = (
        (0, NT, tw[:, 0, :], te[:, NX + 7, :]),
        (NT, NS - 1, ends[:, 0, :], ends[:, 15, :]),
        (NS - 1, NS, fg[0:1, :].astype(F32), fg[NX - 1 : NX, :].astype(F32)),
    )
    for a, b, lo_, up_ in sets:
        ax[a:b, :] = jnp.where(even_x, up_, lo_)
        bx_[a:b, :] = jnp.where(even_x, lo_, up_)
    turned = sq[...].T
    lo_, up_ = turned[0:NS], turned[64 : 64 + NS]
    ay[...] = jnp.where(even_y, up_, lo_)
    by_[...] = jnp.where(even_y, lo_, up_)

    def faces(t, carry):
        rows = pl.ds(pl.multiple_of(t * 8, 8), 8)
        back = pl.ds(t * 8 + 7, 8)
        wall = (sub == 0) & (t == 0)
        for j in range(3):
            f = []
            for m in range(3):
                qa = [te[k27(m, v, j), back, :] for v in range(3)]
                qb = [tw[k27(m, v, j), rows, :] for v in range(3)]
                f.append(rusanov2(qa, side_flux(*qa), qb, side_flux(*qb)))
            f = face_mean(f)
            for v in range(3):
                fx[v * 3 + j, rows, :] = jnp.where(wall, 0.0, f[v])
        return carry

    lax.fori_loop(0, TILES, faces, 0)

    def finish(t, carry):
        rows = pl.ds(pl.multiple_of(t * 8, 8), 8)
        nxt = pl.ds(t * 8 + 1, 8)
        acc = [grid3(lambda i, j: part[k27(v, i, j), rows, :]) for v in range(3)]
        flo = [[fx[v * 3 + j, rows, :] for j in range(3)] for v in range(3)]
        fup = [[fx[v * 3 + j, nxt, :] for j in range(3)] for v in range(3)]
        acc = lift(acc, flo, fup, True, 0.5 / SLOPE)
        for v in range(3):
            for i in range(3):
                for j in range(3):
                    dg[k27(v, i, j), rows, :] = (SLOPE * W[0]) * acc[v][i][j]
        return carry

    lax.fori_loop(0, TILES, finish, 0)


def sub_body(st, bt, fg, dg, out, c6, c0, mom, fx):
    sub, lan = iotas()
    first_lane = lan == 0
    last_lane = lan == NY - 1
    for k in range(49):
        c6[k, 0:8, :] = jnp.zeros((8, NY), F32)
        c0[k, NX : NX + 8, :] = jnp.zeros((8, NY), F32)
    for n in range(9):
        fx[n, NX : NX + 8, :] = jnp.zeros((8, NY), F32)

    def tile(t, carry):
        rows = pl.ds(pl.multiple_of(t * 8, 8), 8)
        wide = pl.ds(pl.multiple_of(t * 8 + 8, 8), 8)
        q = [grid3(lambda i, j: st[k27(v, i, j), rows, :]) for v in range(3)]
        q = q + [grid3(lambda i, j: bt[i * 3 + j, rows, :])]
        cols = [[project7(q[v][0][j], q[v][1][j], q[v][2][j]) for j in range(3)] for v in range(4)]
        rowm = []
        cell = []
        prev = None
        for a in range(7):
            cell.append([project7(cols[v][0][a], cols[v][1][a], cols[v][2][a]) for v in range(4)])
            hs, ps, rs, bs = cell[a]
            fl = []
            for c in range(7):
                h, p, r = hs[c], ps[c], rs[c]
                h2 = h * h
                y = lax.rsqrt(h2 + DRY2)
                k = h * (y * y)
                u = p * k
                w = r * k
                pr = 0.5 * h2
                ru = r * u
                cc = lax.rsqrt(y)
                fl.append((p * u + pr, ru, r * w + pr, jnp.abs(u) + cc, jnp.abs(w) + cc))
            if a == 0 or a == 6:
                dst, where_ = (c0, rows) if a == 0 else (c6, wide)
                for c in range(7):
                    for n, x in enumerate((hs[c], ps[c], rs[c], bs[c], fl[c][0], fl[c][1], fl[c][3])):
                        dst[n * 7 + c, where_, :] = x
            gy = []
            for c in range(7):
                f = fl[c]
                if c < 6:
                    g = fl[c + 1]
                    hn, pn, rn, f1, f2, sn = hs[c + 1], ps[c + 1], rs[c + 1], g[1], g[2], g[4]
                else:
                    g = fl[0]
                    hn, pn, rn, f1, f2, sn = [down(x) for x in (hs[0], ps[0], rs[0], g[1], g[2], g[4])]
                s = jnp.maximum(f[4], sn)
                gy.append(
                    (
                        (rs[c] + rn) - s * (hn - hs[c]),
                        (f[1] + f1) - s * (pn - ps[c]),
                        (f[2] + f2) - s * (rn - rs[c]),
                    )
                )
            gy[6] = tuple(jnp.where(last_lane, 0.0, x) for x in gy[6])
            gy = [tuple(up1(x) for x in gy[6])] + gy
            b_hi = jnp.where(last_lane, 0.0, down(bs[0]))
            b_lo = jnp.where(first_lane, 0.0, up1(bs[6]))
            bw = [b_lo] + bs + [b_hi]
            ch = [[gy[c][v] - gy[c + 1][v] for c in range(7)] for v in range(3)]
            ch[2] = [ch[2][c] - hs[c] * (bw[c + 2] - bw[c]) for c in range(7)]
            if prev is not None:
                ph, pp, prr, pb, pfl, pch = prev
                for c in range(7):
                    s = jnp.maximum(pfl[c][3], fl[c][3])
                    f = (
                        (pp[c] + ps[c]) - s * (hs[c] - ph[c]),
                        (pfl[c][0] + fl[c][0]) - s * (ps[c] - pp[c]),
                        (pfl[c][1] + fl[c][1]) - s * (rs[c] - prr[c]),
                    )
                    for v in range(3):
                        pch[v][c] = pch[v][c] - f[v]
                        ch[v][c] = ch[v][c] + f[v]
                for c in range(7):
                    bb = bs[c] - cell[a - 2][3][c] if a >= 2 else bs[c]
                    pch[1][c] = pch[1][c] - ph[c] * bb
                rowm.append([moments7(pch[v]) for v in range(3)])
            prev = (hs, ps, rs, bs, fl, ch)
        ch = prev[5]
        ch[1] = [ch[1][c] + cell[6][0][c] * cell[5][3][c] for c in range(7)]
        rowm.append([moments7(ch[v]) for v in range(3)])
        for v in range(3):
            for n in range(3):
                mm = moments7([rowm[a][v][n] for a in range(7)])
                for m in range(3):
                    mom[k27(v, m, n), rows, :] = mm[m]
        return carry

    lax.fori_loop(0, TILES, tile, 0)

    def faces(t, carry):
        rows = pl.ds(pl.multiple_of(t * 8, 8), 8)
        back = pl.ds(t * 8 + 7, 8)
        wall = (sub == 0) & (t == 0)
        cs = []
        for c in range(7):
            a = [c6[n * 7 + c, back, :] for n in (0, 1, 2, 4, 5, 6)]
            b = [c0[n * 7 + c, rows, :] for n in (0, 1, 2, 4, 5, 6)]
            cs.append(rusanov2(a[:3], (a[1], a[3], a[4], a[5]), b[:3], (b[1], b[3], b[4], b[5])))
        for v in range(3):
            mm = moments7([cs[c][v] for c in range(7)])
            for n in range(3):
                fx[v * 3 + n, rows, :] = jnp.where(wall, 0.0, mm[n])
        return carry

    lax.fori_loop(0, TILES, faces, 0)

    def finish(t, carry):
        rows = pl.ds(pl.multiple_of(t * 8, 8), 8)
        wide = pl.ds(pl.multiple_of(t * 8 + 8, 8), 8)
        back = pl.ds(t * 8 + 7, 8)
        nxt = pl.ds(t * 8 + 1, 8)
        mm = [grid3(lambda m, n: mom[k27(v, m, n), rows, :]) for v in range(3)]
        slo = moments7([c0[c, rows, :] * c6[21 + c, back, :] for c in range(7)])
        shi = moments7([c6[c, wide, :] * c0[21 + c, nxt, :] for c in range(7)])
        flag = fg[rows, :] > 0
        for v in range(3):
            grid = [[None] * 3 for _ in range(3)]
            for n in range(3):
                lo_ = fx[v * 3 + n, rows, :]
                hi_ = fx[v * 3 + n, nxt, :]
                if v == 1:
                    lo_ = lo_ + slo[n]
                    hi_ = hi_ + shi[n]
                s = lo_ - hi_
                d = lo_ + hi_
                c = nodes_of_moments(mm[v][0][n] + s, mm[v][1][n] - 3.0 * d, mm[v][2][n] + 9.0 * s)
                for i in range(3):
                    grid[i][n] = c[i]
            for i in range(3):
                c = nodes_of_moments(grid[i][0], grid[i][1], grid[i][2])
                for j in range(3):
                    k = k27(v, i, j)
                    out[k, rows, :] = jnp.where(flag, 3.5 * c[j], dg[k, rows, :])
        return carry

    lax.fori_loop(0, TILES, finish, 0)


def edge_body(inc, ax, bx_, ay, by_, rax, rbx, ray, rby, out, own, rec, kq, kt):
    sub, lan = iotas()
    ix, iy = lax.axis_index("gx"), lax.axis_index("gy")
    nx, ny = lax.axis_size("gx"), lax.axis_size("gy")
    even_x = ix % 2 == 0
    even_y = iy % 2 == 0
    own[...] = jnp.zeros((NS, 8, NY), F32)
    rec[...] = jnp.zeros((NS, 8, NY), F32)
    for buf, a, b, c, d in ((own, ax, bx_, ay, by_), (rec, rax, rbx, ray, rby)):
        a, b, c, d = a[...], b[...], c[...], d[...]
        buf[:, 0, :] = jnp.where(even_x, b, a)
        buf[:, 7, :] = jnp.where(even_x, a, b)
        buf[:, 2, :] = jnp.where(even_y, d, c)
        buf[:, 3, :] = jnp.where(even_y, c, d)
    lower = (sub == 0) | (sub == 2)
    atwall = (
        ((sub == 0) & (ix == 0))
        | ((sub == 7) & (ix == nx - 1))
        | ((sub == 2) & (iy == 0))
        | ((sub == 3) & (iy == ny - 1))
    )
    sg = jnp.where(lower, -1.0, 1.0).astype(F32)
    sr = jnp.where(atwall, -sg, sg)
    flag = own[NS - 1] > 0.5
    phd = []
    for n in range(3):
        f = []
        for m in range(3):
            qa = [own[k27(m, c, n)] for c in range(3)]
            qb = [rec[k27(m, c, n)] for c in range(3)]
            qa[1] = qa[1] * sg
            qb[1] = qb[1] * sr
            f.append(rusanov2(qa, side_flux(*qa), qb, side_flux(*qb)))
        phd.append(face_mean(f))
    ua = [project7(*[own[NT + c * 3 + n] for n in range(3)]) for c in range(3)]
    ub = [project7(*[rec[NT + c * 3 + n] for n in range(3)]) for c in range(4)]
    fl = []
    for c in range(7):
        qa = [ua[0][c], ua[1][c] * sg, ua[2][c]]
        qb = [ub[0][c], ub[1][c] * sr, ub[2][c]]
        f = rusanov2(qa, side_flux(*qa), qb, side_flux(*qb))
        f[1] = f[1] + qa[0] * ub[3][c]
        fl.append(f)
    phl = [nodes_of_moments(*moments7([fl[c][v] for c in range(7)])) for v in range(3)]
    rq = nodes_of_moments(1.0, 3.0, 9.0)
    for c in range(3):
        for n in range(3):
            vd = phd[n][c]
            vl = phl[c][n]
            if c == 1:
                vd = vd * sg
                vl = vl * sg
            for k in range(3):
                kq[k27(c, n, k)] = jnp.where(flag, (-3.5 * rq[k]) * vl, (-0.5 * W[0] * UPPER[k] / W[k]) * vd)
    low = kq[:, 2, :]
    high = kq[:, 3, :]
    both = jnp.concatenate([low, jnp.zeros((5, NY), F32), high, jnp.zeros((NY - 59, NY), F32)], 0)
    kt[...] = both.T
    first_lane = lan == 0
    last_lane = lan == NY - 1
    for t in range(TILES):
        rows = slice(t * 8, t * 8 + 8)
        z = kt[rows, :]
        for v in range(3):
            c = (0, 2, 1)[v]
            for i in range(3):
                for j in range(3):
                    k = k27(v, i, j)
                    lo_ = lane(z, k27(c, i, 2 - j))
                    up_ = lane(z, 32 + k27(c, i, j))
                    x = inc[k, rows, :]
                    x = x + jnp.where(first_lane, lo_, jnp.where(last_lane, up_, 0.0))
                    if t == 0:
                        x = x + jnp.where(sub == 0, kq[k27(v, j, 2 - i)], 0.0)
                    if t == TILES - 1:
                        x = x + jnp.where(sub == 7, kq[k27(v, j, i)], 0.0)
                    out[k, rows, :] = x


def pairs(n):
    first = [(i, i ^ 1) for i in range(n)]
    second = [(i, i + 1 if i % 2 else i - 1) for i in range(n)]
    second = [(i, j if 0 <= j < n else i) for i, j in second]
    return first, second


VM = pl.BlockSpec(memory_space=pltpu.VMEM)
PARAMS = pltpu.CompilerParams(vmem_limit_bytes=40 * 1024 * 1024)


def planes(n, rows=NX):
    return pltpu.VMEM((n, rows, NY), F32)


def call(body, name, args, outs, scratch, cost):
    return pl.pallas_call(
        body,
        out_shape=outs,
        in_specs=[VM] * len(args),
        out_specs=jax.tree.map(lambda _: VM, outs),
        scratch_shapes=scratch,
        compiler_params=PARAMS,
        cost_estimate=pl.CostEstimate(flops=cost, transcendentals=0, bytes_accessed=2**20),
        name=name,
    )(*args)


def shards(state, bathymetry, flags):
    st = state.reshape(27, NX, NY)
    bt = bathymetry.reshape(9, NX, NY)
    full = jax.ShapeDtypeStruct((27, NX, NY), F32)
    edge = jax.ShapeDtypeStruct((NS, NY), F32)
    dg, ax, bx, ay, by = call(
        dg_body, "dg", (st, bt, flags), (full, edge, edge, edge, edge),
        [planes(NT, NX + 8), planes(NT), planes(27), planes(9, NX + 8), planes(12, 16), pltpu.VMEM((NY, NY), F32)],
        2**24,
    )
    x1, x2 = pairs(lax.axis_size("gx"))
    y1, y2 = pairs(lax.axis_size("gy"))
    rax = lax.ppermute(ax, "gx", x1)
    rbx = lax.ppermute(bx, "gx", x2)
    ray = lax.ppermute(ay, "gy", y1)
    rby = lax.ppermute(by, "gy", y2)
    inc = call(
        sub_body, "subcell", (st, bt, flags, dg), full,
        [planes(49, NX + 8), planes(49, NX + 8), planes(27), planes(9, NX + 8)],
        2**24,
    )
    out = call(
        edge_body, "edge", (inc, ax, bx, ay, by, rax, rbx, ray, rby), full,
        [planes(NS, 8), planes(NS, 8), planes(27, 8), pltpu.VMEM((NY, NY), F32)],
        2**20,
    )
    return out.reshape(3, 3, 3, NX, NY)


def solution(mesh):
    in_specs = (P(None, None, None, "gx", "gy"), P(None, None, "gx", "gy"), P("gx", "gy"))
    out_specs = P(None, None, None, "gx", "gy")
    return jax.shard_map(shards, mesh=mesh, in_specs=in_specs, out_specs=out_specs, check_vma=False)
```

```python
import functools
import math

import jax
import jax.numpy as jnp
from jax import lax
from jax.experimental import pallas as pl
from jax.experimental.pallas import tpu as pltpu
from jax.sharding import PartitionSpec as P

GRAV = 1.0
DRY2 = 0.05 * 0.05
COURANT = 0.05
SPREAD = math.sqrt(15.0) / 10.0
NODES = [0.5 - SPREAD, 0.5, 0.5 + SPREAD]
W = [5.0 / 18.0, 8.0 / 18.0, 5.0 / 18.0]


def _terms(k):
    o = [NODES[m] for m in range(3) if m != k]
    return o[0] + o[1], o[0] * o[1], (NODES[k] - o[0]) * (NODES[k] - o[1])


def _value(k, x):
    t = _terms(k)
    return (x * x - t[0] * x + t[1]) / t[2]


def _integral(k, x):
    t = _terms(k)
    return (x * x * x / 3.0 - t[0] * x * x / 2.0 + t[1] * x) / t[2]


UPPER = [_value(k, 1.0) for k in range(3)]
LOWER = [_value(k, 0.0) for k in range(3)]
AT = [[_integral(n, NODES[m]) for n in range(3)] for m in range(3)]
SLOPE = 0.5 / SPREAD
PA = 0.5 / SPREAD / 7.0
PE2 = 0.5 / (SPREAD * SPREAD) / 49.0
PE0 = PE2 / 12.0
_S2, _S4 = 28.0, 196.0
_DET = 7.0 * _S4 - _S2 * _S2


def _restorer():
    b0, b2 = -_S2 / _DET / PE2, 7.0 / _DET / PE2
    m0, m2 = _S4 / _DET - PE0 * b0, -_S2 / _DET - PE0 * b2
    return (m0, m2, m0 + b0 / 2.0, m2 + b2 / 2.0, 0.5 / _S2 / PA)


RM0, RM2, RE0, RE2, RA1 = _restorer()
NX, NY = 32, 128
F32 = jnp.float32


def deriv3(f0, f1, f2):
    a = f2 - f0
    e = f0 + f2
    c = (e + e) - 4.0 * f1
    return a - c, a, a + c


def stiff3(f0, f1, f2):
    a = f2 - f0
    g = f0 + f2 + 1.6 * f1
    a2 = a + a
    return a2 - g, -2.5 * a, a2 + g


def ends3(f0, f1, f2):
    m = (0.5 * (UPPER[0] + UPPER[2])) * (f0 + f2) + UPPER[1] * f1
    n = (0.5 * (UPPER[2] - UPPER[0])) * (f2 - f0)
    return m + n, m - n


def project7(f0, f1, f2):
    b = (f0 + f2) - (f1 + f1)
    x = PE2 * b
    y = PA * (f2 - f0)
    c = f1 + PE0 * b
    y2 = y + y
    y3 = y2 + y
    z1 = c + x
    z2 = c + 4.0 * x
    z3 = c + 9.0 * x
    return [z3 - y3, z2 - y2, z1 - y, c, z1 + y, z2 + y2, z3 + y3]


def project_ends(f0, f1, f2):
    b = (f0 + f2) - (f1 + f1)
    z = f1 + (PE0 + 9.0 * PE2) * b
    y = (3.0 * PA) * (f2 - f0)
    return z - y, z + y


def moments7(c):
    e1, a1 = c[4] + c[2], c[4] - c[2]
    e2, a2 = c[5] + c[1], c[5] - c[1]
    e3, a3 = c[6] + c[0], c[6] - c[0]
    return (
        (c[3] + e1) + (e2 + e3),
        a1 + (a2 + a2) + 3.0 * a3,
        e1 + 4.0 * e2 + 9.0 * e3,
    )


def nodes_of_moments(m0, m1, m2):
    e = RE0 * m0 + RE2 * m2
    a = RA1 * m1
    return e - a, RM0 * m0 + RM2 * m2, e + a


def node_fluxes(h, p, r):
    h2 = h * h
    y = lax.rsqrt(h2 + DRY2)
    k = h * (y * y)
    u = p * k
    pr = 0.5 * h2
    ru = r * u
    return p * u + pr, ru, r * (r * k) + pr


def side_flux(h, n, t):
    h2 = h * h
    y = lax.rsqrt(h2 + DRY2)
    u = n * (h * (y * y))
    return n, n * u + 0.5 * h2, t * u, jnp.abs(u) + lax.rsqrt(y)


def rusanov2(qa, fa, qb, fb):
    s = jnp.maximum(fa[3], fb[3])
    return [(fa[v] + fb[v]) - s * (qb[v] - qa[v]) for v in range(3)]


def grid3(f):
    return [[f(i, j) for j in range(3)] for i in range(3)]


def bottom_slopes(b):
    bx = [[None] * 3 for _ in range(3)]
    by = [[None] * 3 for _ in range(3)]
    for j in range(3):
        d = deriv3(b[0][j], b[1][j], b[2][j])
        for i in range(3):
            bx[i][j] = d[i]
    for i in range(3):
        by[i] = list(deriv3(b[i][0], b[i][1], b[i][2]))
    return bx, by


def rate(q, bx, by):
    fl = grid3(lambda i, j: node_fluxes(q[0][i][j], q[1][i][j], q[2][i][j]))
    pu = grid3(lambda i, j: fl[i][j][0])
    ru = grid3(lambda i, j: fl[i][j][1])
    rv = grid3(lambda i, j: fl[i][j][2])
    out = []
    for fx, gy in ((q[1], q[2]), (pu, ru), (ru, rv)):
        acc = [[None] * 3 for _ in range(3)]
        for j in range(3):
            d = deriv3(fx[0][j], fx[1][j], fx[2][j])
            for i in range(3):
                acc[i][j] = d[i]
        for i in range(3):
            d = deriv3(gy[i][0], gy[i][1], gy[i][2])
            for j in range(3):
                acc[i][j] = acc[i][j] + d[j]
        out.append(acc)
    for i in range(3):
        for j in range(3):
            out[1][i][j] = out[1][i][j] + q[0][i][j] * bx[i][j]
            out[2][i][j] = out[2][i][j] + q[0][i][j] * by[i][j]
    return out


def predict(q0, bx, by):
    f = -COURANT * SLOPE
    r = rate(q0, bx, by)
    lv = [[None] * 3 for _ in range(3)]
    for v in range(3):
        mid = grid3(lambda i, j: q0[v][i][j] + (f * 0.5) * r[v][i][j])
        dif = grid3(lambda i, j: (f * SPREAD) * r[v][i][j])
        lv[0][v] = grid3(lambda i, j: mid[i][j] - dif[i][j])
        lv[1][v] = mid
        lv[2][v] = grid3(lambda i, j: mid[i][j] + dif[i][j])
    ka = f * W[0] / 2.0
    kb = f * W[1] / 2.0
    k1 = f * (AT[1][0] - W[0] / 2.0)
    k2 = f * (AT[0][2] - W[2] / 2.0)
    for _ in range(2):
        rs = [rate(lv[m], bx, by) for m in range(3)]
        new = [[[[None] * 3 for _ in range(3)] for _ in range(3)] for _ in range(3)]
        for v in range(3):
            for i in range(3):
                for j in range(3):
                    r0, r1, r2 = rs[0][v][i][j], rs[1][v][i][j], rs[2][v][i][j]
                    base = q0[v][i][j] + ka * (r0 + r2) + kb * r1
                    c1 = (2.0 * k2) * r1
                    new[0][v][i][j] = base + (c1 + k2 * r2)
                    new[1][v][i][j] = base + k1 * (r0 - r2)
                    new[2][v][i][j] = base - (c1 + k2 * r0)
        lv = new
    return lv


def face_mean(f):
    return [(f[0][v] + f[2][v]) + 1.6 * f[1][v] for v in range(3)]


def volume(lv, bx, by):
    fl = [grid3(lambda i, j: node_fluxes(lv[m][0][i][j], lv[m][1][i][j], lv[m][2][i][j])) for m in range(3)]

    def mean(get):
        return grid3(lambda i, j: (get(0, i, j) + get(2, i, j)) + 1.6 * get(1, i, j))

    hm, pm, rm = [mean(lambda m, i, j: lv[m][v][i][j]) for v in range(3)]
    pu, ru, rv = [mean(lambda m, i, j: fl[m][i][j][c]) for c in range(3)]
    out = []
    for fx, gy in ((pm, rm), (pu, ru), (ru, rv)):
        acc = [[None] * 3 for _ in range(3)]
        for j in range(3):
            d = stiff3(fx[0][j], fx[1][j], fx[2][j])
            for i in range(3):
                acc[i][j] = d[i]
        for i in range(3):
            d = stiff3(gy[i][0], gy[i][1], gy[i][2])
            for j in range(3):
                acc[i][j] = acc[i][j] + d[j]
        out.append(acc)
    for i in range(3):
        for j in range(3):
            out[1][i][j] = out[1][i][j] - hm[i][j] * bx[i][j]
            out[2][i][j] = out[2][i][j] - hm[i][j] * by[i][j]
    return out


def traces_x(lv):
    up = [[[None] * 3 for _ in range(3)] for _ in range(3)]
    lo = [[[None] * 3 for _ in range(3)] for _ in range(3)]
    for m in range(3):
        for v in range(3):
            for j in range(3):
                up[m][v][j], lo[m][v][j] = ends3(lv[m][v][0][j], lv[m][v][1][j], lv[m][v][2][j])
    return up, lo


def traces_y(lv):
    up = [[[None] * 3 for _ in range(3)] for _ in range(3)]
    lo = [[[None] * 3 for _ in range(3)] for _ in range(3)]
    for m in range(3):
        for v in range(3):
            for i in range(3):
                up[m][v][i], lo[m][v][i] = ends3(lv[m][v][i][0], lv[m][v][i][1], lv[m][v][i][2])
    return up, lo


def lift(acc, lo, up, along_x, scale):
    ko = [scale * LOWER[i] / W[i] for i in range(3)]
    for v in range(3):
        for t in range(3):
            d = lo[v][t] - up[v][t]
            c = ko[1] * d
            x = ko[0] * lo[v][t] - ko[2] * up[v][t]
            z = ko[2] * lo[v][t] - ko[0] * up[v][t]
            for n, k in enumerate((x, c, z)):
                if along_x:
                    acc[v][n][t] = acc[v][n][t] + k
                else:
                    acc[v][t][n] = acc[v][t][n] + k
    return acc


NT = 27
NS = 40
TILES = NX // 8
CHIPS_Z = 8


def k27(a, b, c):
    return a * 9 + b * 3 + c


def lane(x, k):
    return jnp.broadcast_to(x[:, k : k + 1], (8, NY))


def down(x):
    return pltpu.roll(x, NY - 1, 1)


def up1(x):
    return pltpu.roll(x, 1, 1)


def iotas():
    return (
        lax.broadcasted_iota(jnp.int32, (8, NY), 0),
        lax.broadcasted_iota(jnp.int32, (8, NY), 1),
    )


def load_body(st_h, bt_h, fg_h, st, bt, fg, lv_o, te, tw, tu, tl, ax, bx_, ay, by_, ends, sq, sem):
    sub, lan = iotas()

    def copies(t):
        rows = pl.ds(t * 8, 8)
        return [
            pltpu.make_async_copy(h.at[(slice(None),) * n + (rows,)], v.at[(slice(None),) * n + (rows,)], sem.at[k, t])
            for k, (h, v, n) in enumerate(((st_h, st, 1), (bt_h, bt, 1), (fg_h, fg, 0)))
        ]

    for t in range(TILES):
        for c in copies(t):
            c.start()
    sq[NX:, :] = jnp.zeros((NY - NX, NY), F32)
    for k in range(NT):
        te[k, 0:8, :] = jnp.zeros((8, NY), F32)

    def tile(t, carry):
        rows = pl.ds(pl.multiple_of(t * 8, 8), 8)
        wide = pl.ds(pl.multiple_of(t * 8 + 8, 8), 8)
        for c in copies(pl.multiple_of(t, 1)):
            c.wait()
        q = [grid3(lambda i, j: st[k27(v, i, j), rows, :]) for v in range(3)]
        b = grid3(lambda i, j: bt[i * 3 + j, rows, :])
        bx, by = bottom_slopes(b)
        lv = predict(q, bx, by)
        for m in range(3):
            for v in range(3):
                for i in range(3):
                    for j in range(3):
                        lv_o[m * 27 + k27(v, i, j), rows, :] = lv[m][v][i][j]
        up, lo = traces_x(lv)
        for m in range(3):
            for v in range(3):
                for j in range(3):
                    te[k27(m, v, j), wide, :] = up[m][v][j]
                    tw[k27(m, v, j), rows, :] = lo[m][v][j]
        up, lo = traces_y(lv)
        col = jnp.zeros((8, NY), F32)

        def put(col, k, x_lo, x_up):
            col = jnp.where(lan == k, lane(x_lo, 0), col)
            return jnp.where(lan == 64 + k, lane(x_up, NY - 1), col)

        for m in range(3):
            for c, v in enumerate((0, 2, 1)):
                for i in range(3):
                    k = k27(m, c, i)
                    col = put(col, k, lo[m][v][i], up[m][v][i])
                    tu[k, rows, :] = up[m][v][i]
                    tl[k, rows, :] = lo[m][v][i]
        for c, f in enumerate((q[0], q[2], q[1], b)):
            for i in range(3):
                e0, e6 = project_ends(f[i][0], f[i][1], f[i][2])
                col = put(col, NT + c * 3 + i, e0, e6)
        f = fg[rows, :].astype(F32)
        sq[rows, :] = put(col, NS - 1, f, f)
        return carry

    lax.fori_loop(0, TILES, tile, 0)

    for c in range(4):
        for j in range(3):
            if c < 3:
                lo_f = [st[k27(c, i, j), 0:8, :] for i in range(3)]
                up_f = [st[k27(c, i, j), NX - 8 : NX, :] for i in range(3)]
            else:
                lo_f = [bt[i * 3 + j, 0:8, :] for i in range(3)]
                up_f = [bt[i * 3 + j, NX - 8 : NX, :] for i in range(3)]
            ends[c * 3 + j, 0:8, :] = project_ends(*lo_f)[0]
            ends[c * 3 + j, 8:16, :] = project_ends(*up_f)[1]
    even_x = lax.axis_index("gx") % 2 == 0
    even_y = lax.axis_index("gy") % 2 == 0
    sets = (
        (0, NT, tw[:, 0, :], te[:, NX + 7, :]),
        (NT, NS - 1, ends[:, 0, :], ends[:, 15, :]),
        (NS - 1, NS, fg[0:1, :].astype(F32), fg[NX - 1 : NX, :].astype(F32)),
    )
    for a, b, lo_, up_ in sets:
        ax[a:b, :] = jnp.where(even_x, up_, lo_)
        bx_[a:b, :] = jnp.where(even_x, lo_, up_)
    turned = sq[...].T
    lo_, up_ = turned[0:NS], turned[64 : 64 + NS]
    ay[...] = jnp.where(even_y, up_, lo_)
    by_[...] = jnp.where(even_y, lo_, up_)


def crossing():
    iy = lax.axis_index("gy")
    return (iy % CHIPS_Z == 0) & (iy > 0)


def inner_body(early, st, bt, fg, lv_i, te, tw, tu, tl, out, *scratch):
    @pl.when(crossing() if early else jnp.logical_not(crossing()))
    def _():
        inner(st, bt, fg, lv_i, te, tw, tu, tl, out, *scratch)


def inner(st, bt, fg, lv_i, te, tw, tu, tl, out, c6, c0, mom, fx, dg, fd):
    sub, lan = iotas()
    first_lane = lan == 0
    last_lane = lan == NY - 1
    for n in range(9):
        fd[n, NX : NX + 8, :] = jnp.zeros((8, NY), F32)

    def dg_tile(t, carry):
        rows = pl.ds(pl.multiple_of(t * 8, 8), 8)
        b = grid3(lambda i, j: bt[i * 3 + j, rows, :])
        bx, by = bottom_slopes(b)
        lv = [[grid3(lambda i, j: lv_i[m * 27 + k27(v, i, j), rows, :]) for v in range(3)] for m in range(3)]
        acc = volume(lv, bx, by)
        flo = [[None] * 3 for _ in range(3)]
        fup = [[None] * 3 for _ in range(3)]
        for i in range(3):
            fu = []
            for m in range(3):
                qa = [tu[k27(m, c, i), rows, :] for c in range(3)]
                qb = [tl[k27(m, c, i), rows, :] for c in range(3)]
                fb = side_flux(*qb)
                qn = [down(x) for x in qb]
                fn = [qn[1]] + [down(x) for x in fb[1:]]
                fu.append(rusanov2(qa, side_flux(*qa), qn, fn))
            fum = face_mean(fu)
            for s, v in enumerate((0, 2, 1)):
                fup[v][i] = jnp.where(last_lane, 0.0, fum[s])
                flo[v][i] = up1(fup[v][i])
        acc = lift(acc, flo, fup, False, 0.5 / SLOPE)
        for v in range(3):
            for i in range(3):
                for j in range(3):
                    dg[k27(v, i, j), rows, :] = acc[v][i][j]
        back = pl.ds(t * 8 + 7, 8)
        wall = (sub == 0) & (t == 0)
        for j in range(3):
            f = []
            for m in range(3):
                qa = [te[k27(m, v, j), back, :] for v in range(3)]
                qb = [tw[k27(m, v, j), rows, :] for v in range(3)]
                f.append(rusanov2(qa, side_flux(*qa), qb, side_flux(*qb)))
            f = face_mean(f)
            for v in range(3):
                fd[v * 3 + j, rows, :] = jnp.where(wall, 0.0, f[v])
        return carry

    lax.fori_loop(0, TILES, dg_tile, 0)
    for k in range(49):
        c6[k, 0:8, :] = jnp.zeros((8, NY), F32)
        c0[k, NX : NX + 8, :] = jnp.zeros((8, NY), F32)
    for n in range(9):
        fx[n, NX : NX + 8, :] = jnp.zeros((8, NY), F32)

    def tile(t, carry):
        rows = pl.ds(pl.multiple_of(t * 8, 8), 8)
        wide = pl.ds(pl.multiple_of(t * 8 + 8, 8), 8)
        q = [grid3(lambda i, j: st[k27(v, i, j), rows, :]) for v in range(3)]
        q = q + [grid3(lambda i, j: bt[i * 3 + j, rows, :])]
        cols = [[project7(q[v][0][j], q[v][1][j], q[v][2][j]) for j in range(3)] for v in range(4)]
        rowm = []
        cell = []
        prev = None
        for a in range(7):
            cell.append([project7(cols[v][0][a], cols[v][1][a], cols[v][2][a]) for v in range(4)])
            hs, ps, rs, bs = cell[a]
            fl = []
            for c in range(7):
                h, p, r = hs[c], ps[c], rs[c]
                h2 = h * h
                y = lax.rsqrt(h2 + DRY2)
                k = h * (y * y)
                u = p * k
                w = r * k
                pr = 0.5 * h2
                ru = r * u
                cc = lax.rsqrt(y)
                fl.append((p * u + pr, ru, r * w + pr, jnp.abs(u) + cc, jnp.abs(w) + cc))
            if a == 0 or a == 6:
                dst, where_ = (c0, rows) if a == 0 else (c6, wide)
                for c in range(7):
                    for n, x in enumerate((hs[c], ps[c], rs[c], bs[c], fl[c][0], fl[c][1], fl[c][3])):
                        dst[n * 7 + c, where_, :] = x
            gy = []
            for c in range(7):
                f = fl[c]
                if c < 6:
                    g = fl[c + 1]
                    hn, pn, rn, f1, f2, sn = hs[c + 1], ps[c + 1], rs[c + 1], g[1], g[2], g[4]
                else:
                    g = fl[0]
                    hn, pn, rn, f1, f2, sn = [down(x) for x in (hs[0], ps[0], rs[0], g[1], g[2], g[4])]
                s = jnp.maximum(f[4], sn)
                gy.append(
                    (
                        (rs[c] + rn) - s * (hn - hs[c]),
                        (f[1] + f1) - s * (pn - ps[c]),
                        (f[2] + f2) - s * (rn - rs[c]),
                    )
                )
            gy[6] = tuple(jnp.where(last_lane, 0.0, x) for x in gy[6])
            gy = [tuple(up1(x) for x in gy[6])] + gy
            b_hi = jnp.where(last_lane, 0.0, down(bs[0]))
            b_lo = jnp.where(first_lane, 0.0, up1(bs[6]))
            bw = [b_lo] + bs + [b_hi]
            ch = [[gy[c][v] - gy[c + 1][v] for c in range(7)] for v in range(3)]
            ch[2] = [ch[2][c] - hs[c] * (bw[c + 2] - bw[c]) for c in range(7)]
            if prev is not None:
                ph, pp, prr, pb, pfl, pch = prev
                for c in range(7):
                    s = jnp.maximum(pfl[c][3], fl[c][3])
                    f = (
                        (pp[c] + ps[c]) - s * (hs[c] - ph[c]),
                        (pfl[c][0] + fl[c][0]) - s * (ps[c] - pp[c]),
                        (pfl[c][1] + fl[c][1]) - s * (rs[c] - prr[c]),
                    )
                    for v in range(3):
                        pch[v][c] = pch[v][c] - f[v]
                        ch[v][c] = ch[v][c] + f[v]
                for c in range(7):
                    bb = bs[c] - cell[a - 2][3][c] if a >= 2 else bs[c]
                    pch[1][c] = pch[1][c] - ph[c] * bb
                rowm.append([moments7(pch[v]) for v in range(3)])
            prev = (hs, ps, rs, bs, fl, ch)
        ch = prev[5]
        ch[1] = [ch[1][c] + cell[6][0][c] * cell[5][3][c] for c in range(7)]
        rowm.append([moments7(ch[v]) for v in range(3)])
        for v in range(3):
            for n in range(3):
                mm = moments7([rowm[a][v][n] for a in range(7)])
                for m in range(3):
                    mom[k27(v, m, n), rows, :] = mm[m]
        return carry

    lax.fori_loop(0, TILES, tile, 0)

    def faces(t, carry):
        rows = pl.ds(pl.multiple_of(t * 8, 8), 8)
        back = pl.ds(t * 8 + 7, 8)
        wall = (sub == 0) & (t == 0)
        cs = []
        for c in range(7):
            a = [c6[n * 7 + c, back, :] for n in (0, 1, 2, 4, 5, 6)]
            b = [c0[n * 7 + c, rows, :] for n in (0, 1, 2, 4, 5, 6)]
            cs.append(rusanov2(a[:3], (a[1], a[3], a[4], a[5]), b[:3], (b[1], b[3], b[4], b[5])))
        for v in range(3):
            mm = moments7([cs[c][v] for c in range(7)])
            for n in range(3):
                fx[v * 3 + n, rows, :] = jnp.where(wall, 0.0, mm[n])
        return carry

    lax.fori_loop(0, TILES, faces, 0)

    def finish(t, carry):
        rows = pl.ds(pl.multiple_of(t * 8, 8), 8)
        wide = pl.ds(pl.multiple_of(t * 8 + 8, 8), 8)
        back = pl.ds(t * 8 + 7, 8)
        nxt = pl.ds(t * 8 + 1, 8)
        mm = [grid3(lambda m, n: mom[k27(v, m, n), rows, :]) for v in range(3)]
        slo = moments7([c0[c, rows, :] * c6[21 + c, back, :] for c in range(7)])
        shi = moments7([c6[c, wide, :] * c0[21 + c, nxt, :] for c in range(7)])
        flag = fg[rows, :] > 0
        acc = [grid3(lambda i, j: dg[k27(v, i, j), rows, :]) for v in range(3)]
        flo = [[fd[v * 3 + j, rows, :] for j in range(3)] for v in range(3)]
        fup = [[fd[v * 3 + j, nxt, :] for j in range(3)] for v in range(3)]
        acc = lift(acc, flo, fup, True, 0.5 / SLOPE)
        for v in range(3):
            grid = [[None] * 3 for _ in range(3)]
            for n in range(3):
                lo_ = fx[v * 3 + n, rows, :]
                hi_ = fx[v * 3 + n, nxt, :]
                if v == 1:
                    lo_ = lo_ + slo[n]
                    hi_ = hi_ + shi[n]
                s = lo_ - hi_
                d = lo_ + hi_
                c = nodes_of_moments(mm[v][0][n] + s, mm[v][1][n] - 3.0 * d, mm[v][2][n] + 9.0 * s)
                for i in range(3):
                    grid[i][n] = c[i]
            for i in range(3):
                c = nodes_of_moments(grid[i][0], grid[i][1], grid[i][2])
                for j in range(3):
                    k = k27(v, i, j)
                    out[k, rows, :] = jnp.where(flag, 3.5 * c[j], (SLOPE * W[0]) * acc[v][i][j])
        return carry

    lax.fori_loop(0, TILES, finish, 0)


def edge_body(inc1, inc2, ax, bx_, ay, by_, rax, rbx, ray, rby, out, own, rec, kq, kt, buf_o, sem):
    sub, lan = iotas()
    ix, iy = lax.axis_index("gx"), lax.axis_index("gy")
    nx, ny = lax.axis_size("gx"), lax.axis_size("gy")
    even_x = ix % 2 == 0
    even_y = iy % 2 == 0
    own[...] = jnp.zeros((NS, 8, NY), F32)
    rec[...] = jnp.zeros((NS, 8, NY), F32)
    for buf, a, b, c, d in ((own, ax, bx_, ay, by_), (rec, rax, rbx, ray, rby)):
        a, b, c, d = a[...], b[...], c[...], d[...]
        buf[:, 0, :] = jnp.where(even_x, b, a)
        buf[:, 7, :] = jnp.where(even_x, a, b)
        buf[:, 2, :] = jnp.where(even_y, d, c)
        buf[:, 3, :] = jnp.where(even_y, c, d)
    lower = (sub == 0) | (sub == 2)
    atwall = (
        ((sub == 0) & (ix == 0))
        | ((sub == 7) & (ix == nx - 1))
        | ((sub == 2) & (iy == 0))
        | ((sub == 3) & (iy == ny - 1))
    )
    sg = jnp.where(lower, -1.0, 1.0).astype(F32)
    sr = jnp.where(atwall, -sg, sg)
    flag = own[NS - 1] > 0.5

    def other(k):
        return jnp.where(atwall, own[k], rec[k])

    phd = []
    for n in range(3):
        f = []
        for m in range(3):
            qa = [own[k27(m, c, n)] for c in range(3)]
            qb = [other(k27(m, c, n)) for c in range(3)]
            qa[1] = qa[1] * sg
            qb[1] = qb[1] * sr
            f.append(rusanov2(qa, side_flux(*qa), qb, side_flux(*qb)))
        phd.append(face_mean(f))
    ua = [project7(*[own[NT + c * 3 + n] for n in range(3)]) for c in range(3)]
    ub = [project7(*[other(NT + c * 3 + n) for n in range(3)]) for c in range(4)]
    fl = []
    for c in range(7):
        qa = [ua[0][c], ua[1][c] * sg, ua[2][c]]
        qb = [ub[0][c], ub[1][c] * sr, ub[2][c]]
        f = rusanov2(qa, side_flux(*qa), qb, side_flux(*qb))
        f[1] = f[1] + qa[0] * ub[3][c]
        fl.append(f)
    phl = [nodes_of_moments(*moments7([fl[c][v] for c in range(7)])) for v in range(3)]
    rq = nodes_of_moments(1.0, 3.0, 9.0)
    for c in range(3):
        for n in range(3):
            vd = phd[n][c]
            vl = phl[c][n]
            if c == 1:
                vd = vd * sg
                vl = vl * sg
            for k in range(3):
                kq[k27(c, n, k)] = jnp.where(flag, (-3.5 * rq[k]) * vl, (-0.5 * W[0] * UPPER[k] / W[k]) * vd)
    low = kq[:, 2, :]
    high = kq[:, 3, :]
    both = jnp.concatenate([low, jnp.zeros((5, NY), F32), high, jnp.zeros((NY - 59, NY), F32)], 0)
    kt[...] = both.T
    first_lane = lan == 0
    last_lane = lan == NY - 1
    early = crossing()
    copies = []
    for t in range(TILES):
        rows = slice(t * 8, t * 8 + 8)
        z = kt[rows, :]
        for v in range(3):
            c = (0, 2, 1)[v]
            for i in range(3):
                for j in range(3):
                    k = k27(v, i, j)
                    lo_ = lane(z, k27(c, i, 2 - j))
                    up_ = lane(z, 32 + k27(c, i, j))
                    x = jnp.where(early, inc1[k, rows, :], inc2[k, rows, :])
                    x = x + jnp.where(first_lane, lo_, jnp.where(last_lane, up_, 0.0))
                    if t == 0:
                        x = x + jnp.where(sub == 0, kq[k27(v, j, 2 - i)], 0.0)
                    if t == TILES - 1:
                        x = x + jnp.where(sub == 7, kq[k27(v, j, i)], 0.0)
                    buf_o[k, rows, :] = x
        cp = pltpu.make_async_copy(buf_o.at[:, pl.ds(t * 8, 8), :], out.at[:, pl.ds(t * 8, 8), :], sem.at[t])
        cp.start()
        copies.append(cp)
    for cp in copies:
        cp.wait()


def swap_first(n):
    return [(i, i ^ 1) for i in range(n)]


def swap_second(n):
    return [(i, (i + 1 if i % 2 else i - 1) % n) for i in range(n)]


def swap_second_both(nx, ny):
    out = []
    for a in range(nx):
        for i in range(ny):
            j = i + 1 if i % 2 else i - 1
            if 0 <= j < ny:
                out.append((a * ny + i, a * ny + j))
            else:
                out.append((a * ny + i, (a ^ 1) * ny + i))
    return out


VM = pl.BlockSpec(memory_space=pltpu.VMEM)
HB = pl.BlockSpec(memory_space=pltpu.HBM)
PARAMS = pltpu.CompilerParams(vmem_limit_bytes=16 * 1024 * 1024)


def planes(n, rows=NX):
    return pltpu.VMEM((n, rows, NY), F32)


def call(body, name, args, outs, scratch, cost, ins=VM, out_spec=VM):
    return pl.pallas_call(
        body,
        out_shape=outs,
        in_specs=[ins] * len(args),
        out_specs=jax.tree.map(lambda _: out_spec, outs),
        scratch_shapes=scratch,
        compiler_params=PARAMS,
        cost_estimate=pl.CostEstimate(flops=cost, transcendentals=0, bytes_accessed=2**20),
        name=name,
    )(*args)


def shape(*dims, dtype=F32):
    return jax.ShapeDtypeStruct(dims, dtype)


def shards(state, bathymetry, flags):
    full = shape(27, NX, NY)
    edge = shape(NS, NY)
    nx, ny = lax.axis_size("gx"), lax.axis_size("gy")
    st, bt, fg, lv, te, tw, tu, tl, ax, bx, ay, by = call(
        load_body, "predict",
        tuple(pltpu.with_memory_space_constraint(x, pltpu.HBM)
              for x in (state.reshape(27, NX, NY), bathymetry.reshape(9, NX, NY), flags)),
        (full, shape(9, NX, NY), shape(NX, NY, dtype=jnp.int32), shape(81, NX, NY), shape(NT, NX + 8, NY),
         full, full, full, edge, edge, edge, edge),
        [planes(12, 16), pltpu.VMEM((NY, NY), F32), pltpu.SemaphoreType.DMA((3, TILES))],
        2**24, ins=HB,
    )
    rax = lax.ppermute(ax, "gx", swap_first(nx))
    rbx = lax.ppermute(bx, "gx", swap_second(nx))
    ray = lax.ppermute(ay, "gy", swap_first(ny))
    args = (st, bt, fg, lv, te, tw, tu, tl)
    scratch = [planes(49, NX + 8), planes(49, NX + 8), planes(27), planes(9, NX + 8), planes(27), planes(9, NX + 8)]
    inc1 = call(functools.partial(inner_body, True), "inner_early", args, full, scratch, 2**24)
    by_, inc1 = lax.optimization_barrier((by, inc1))
    rby = lax.ppermute(by_, ("gx", "gy"), swap_second_both(nx, ny))
    inc2 = call(functools.partial(inner_body, False), "inner", args, full, scratch, 2**24)
    out = call(
        edge_body, "edge", (inc1, inc2, ax, bx, ay, by, rax, rbx, ray, rby), full,
        [planes(NS, 8), planes(NS, 8), planes(27, 8), pltpu.VMEM((NY, NY), F32), planes(27),
         pltpu.SemaphoreType.DMA((TILES,))],
        2**20, out_spec=HB,
    )
    return out.reshape(3, 3, 3, NX, NY)


def solution(mesh):
    in_specs = (P(None, None, None, "gx", "gy"), P(None, None, "gx", "gy"), P("gx", "gy"))
    out_specs = P(None, None, None, "gx", "gy")
    return jax.shard_map(shards, mesh=mesh, in_specs=in_specs, out_specs=out_specs, check_vma=False)
```

```python
import functools
import math

import jax
import jax.numpy as jnp
from jax import lax
from jax.experimental import pallas as pl
from jax.experimental.pallas import tpu as pltpu
from jax.sharding import PartitionSpec as P

GRAV = 1.0
DRY2 = 0.05 * 0.05
COURANT = 0.05
SPREAD = math.sqrt(15.0) / 10.0
NODES = [0.5 - SPREAD, 0.5, 0.5 + SPREAD]
W = [5.0 / 18.0, 8.0 / 18.0, 5.0 / 18.0]


def _terms(k):
    o = [NODES[m] for m in range(3) if m != k]
    return o[0] + o[1], o[0] * o[1], (NODES[k] - o[0]) * (NODES[k] - o[1])


def _value(k, x):
    t = _terms(k)
    return (x * x - t[0] * x + t[1]) / t[2]


def _integral(k, x):
    t = _terms(k)
    return (x * x * x / 3.0 - t[0] * x * x / 2.0 + t[1] * x) / t[2]


UPPER = [_value(k, 1.0) for k in range(3)]
LOWER = [_value(k, 0.0) for k in range(3)]
AT = [[_integral(n, NODES[m]) for n in range(3)] for m in range(3)]
SLOPE = 0.5 / SPREAD
PA = 0.5 / SPREAD / 7.0
PE2 = 0.5 / (SPREAD * SPREAD) / 49.0
PE0 = PE2 / 12.0
_S2, _S4 = 28.0, 196.0
_DET = 7.0 * _S4 - _S2 * _S2


def _restorer():
    b0, b2 = -_S2 / _DET / PE2, 7.0 / _DET / PE2
    m0, m2 = _S4 / _DET - PE0 * b0, -_S2 / _DET - PE0 * b2
    return (m0, m2, m0 + b0 / 2.0, m2 + b2 / 2.0, 0.5 / _S2 / PA)


RM0, RM2, RE0, RE2, RA1 = _restorer()
NX, NY = 32, 128
F32 = jnp.float32


def deriv3(f0, f1, f2):
    a = f2 - f0
    e = f0 + f2
    c = (e + e) - 4.0 * f1
    return a - c, a, a + c


def stiff3(f0, f1, f2):
    a = f2 - f0
    g = f0 + f2 + 1.6 * f1
    a2 = a + a
    return a2 - g, -2.5 * a, a2 + g


def ends3(f0, f1, f2):
    m = (0.5 * (UPPER[0] + UPPER[2])) * (f0 + f2) + UPPER[1] * f1
    n = (0.5 * (UPPER[2] - UPPER[0])) * (f2 - f0)
    return m + n, m - n


def project7(f0, f1, f2):
    b = (f0 + f2) - (f1 + f1)
    x = PE2 * b
    y = PA * (f2 - f0)
    c = f1 + PE0 * b
    y2 = y + y
    y3 = y2 + y
    z1 = c + x
    z2 = c + 4.0 * x
    z3 = c + 9.0 * x
    return [z3 - y3, z2 - y2, z1 - y, c, z1 + y, z2 + y2, z3 + y3]


def project_ends(f0, f1, f2):
    b = (f0 + f2) - (f1 + f1)
    z = f1 + (PE0 + 9.0 * PE2) * b
    y = (3.0 * PA) * (f2 - f0)
    return z - y, z + y


def moments7(c):
    e1, a1 = c[4] + c[2], c[4] - c[2]
    e2, a2 = c[5] + c[1], c[5] - c[1]
    e3, a3 = c[6] + c[0], c[6] - c[0]
    return (
        (c[3] + e1) + (e2 + e3),
        a1 + (a2 + a2) + 3.0 * a3,
        e1 + 4.0 * e2 + 9.0 * e3,
    )


def nodes_of_moments(m0, m1, m2):
    e = RE0 * m0 + RE2 * m2
    a = RA1 * m1
    return e - a, RM0 * m0 + RM2 * m2, e + a


def node_fluxes(h, p, r):
    h2 = h * h
    y = lax.rsqrt(h2 + DRY2)
    k = h * (y * y)
    u = p * k
    pr = 0.5 * h2
    ru = r * u
    return p * u + pr, ru, r * (r * k) + pr


def side_flux(h, n, t):
    h2 = h * h
    y = lax.rsqrt(h2 + DRY2)
    u = n * (h * (y * y))
    return n, n * u + 0.5 * h2, t * u, jnp.abs(u) + lax.rsqrt(y)


def rusanov2(qa, fa, qb, fb):
    s = jnp.maximum(fa[3], fb[3])
    return [(fa[v] + fb[v]) - s * (qb[v] - qa[v]) for v in range(3)]


def grid3(f):
    return [[f(i, j) for j in range(3)] for i in range(3)]


def bottom_slopes(b):
    bx = [[None] * 3 for _ in range(3)]
    by = [[None] * 3 for _ in range(3)]
    for j in range(3):
        d = deriv3(b[0][j], b[1][j], b[2][j])
        for i in range(3):
            bx[i][j] = d[i]
    for i in range(3):
        by[i] = list(deriv3(b[i][0], b[i][1], b[i][2]))
    return bx, by


def rate(q, bx, by):
    fl = grid3(lambda i, j: node_fluxes(q[0][i][j], q[1][i][j], q[2][i][j]))
    pu = grid3(lambda i, j: fl[i][j][0])
    ru = grid3(lambda i, j: fl[i][j][1])
    rv = grid3(lambda i, j: fl[i][j][2])
    out = []
    for fx, gy in ((q[1], q[2]), (pu, ru), (ru, rv)):
        acc = [[None] * 3 for _ in range(3)]
        for j in range(3):
            d = deriv3(fx[0][j], fx[1][j], fx[2][j])
            for i in range(3):
                acc[i][j] = d[i]
        for i in range(3):
            d = deriv3(gy[i][0], gy[i][1], gy[i][2])
            for j in range(3):
                acc[i][j] = acc[i][j] + d[j]
        out.append(acc)
    for i in range(3):
        for j in range(3):
            out[1][i][j] = out[1][i][j] + q[0][i][j] * bx[i][j]
            out[2][i][j] = out[2][i][j] + q[0][i][j] * by[i][j]
    return out


def predict(q0, bx, by):
    f = -COURANT * SLOPE
    r = rate(q0, bx, by)
    lv = [[None] * 3 for _ in range(3)]
    for v in range(3):
        mid = grid3(lambda i, j: q0[v][i][j] + (f * 0.5) * r[v][i][j])
        dif = grid3(lambda i, j: (f * SPREAD) * r[v][i][j])
        lv[0][v] = grid3(lambda i, j: mid[i][j] - dif[i][j])
        lv[1][v] = mid
        lv[2][v] = grid3(lambda i, j: mid[i][j] + dif[i][j])
    ka = f * W[0] / 2.0
    kb = f * W[1] / 2.0
    k1 = f * (AT[1][0] - W[0] / 2.0)
    k2 = f * (AT[0][2] - W[2] / 2.0)
    for _ in range(2):
        rs = [rate(lv[m], bx, by) for m in range(3)]
        new = [[[[None] * 3 for _ in range(3)] for _ in range(3)] for _ in range(3)]
        for v in range(3):
            for i in range(3):
                for j in range(3):
                    r0, r1, r2 = rs[0][v][i][j], rs[1][v][i][j], rs[2][v][i][j]
                    base = q0[v][i][j] + ka * (r0 + r2) + kb * r1
                    c1 = (2.0 * k2) * r1
                    new[0][v][i][j] = base + (c1 + k2 * r2)
                    new[1][v][i][j] = base + k1 * (r0 - r2)
                    new[2][v][i][j] = base - (c1 + k2 * r0)
        lv = new
    return lv


def face_mean(f):
    return [(f[0][v] + f[2][v]) + 1.6 * f[1][v] for v in range(3)]


def volume(lv, bx, by):
    fl = [grid3(lambda i, j: node_fluxes(lv[m][0][i][j], lv[m][1][i][j], lv[m][2][i][j])) for m in range(3)]

    def mean(get):
        return grid3(lambda i, j: (get(0, i, j) + get(2, i, j)) + 1.6 * get(1, i, j))

    hm, pm, rm = [mean(lambda m, i, j: lv[m][v][i][j]) for v in range(3)]
    pu, ru, rv = [mean(lambda m, i, j: fl[m][i][j][c]) for c in range(3)]
    out = []
    for fx, gy in ((pm, rm), (pu, ru), (ru, rv)):
        acc = [[None] * 3 for _ in range(3)]
        for j in range(3):
            d = stiff3(fx[0][j], fx[1][j], fx[2][j])
            for i in range(3):
                acc[i][j] = d[i]
        for i in range(3):
            d = stiff3(gy[i][0], gy[i][1], gy[i][2])
            for j in range(3):
                acc[i][j] = acc[i][j] + d[j]
        out.append(acc)
    for i in range(3):
        for j in range(3):
            out[1][i][j] = out[1][i][j] - hm[i][j] * bx[i][j]
            out[2][i][j] = out[2][i][j] - hm[i][j] * by[i][j]
    return out


def traces_x(lv):
    up = [[[None] * 3 for _ in range(3)] for _ in range(3)]
    lo = [[[None] * 3 for _ in range(3)] for _ in range(3)]
    for m in range(3):
        for v in range(3):
            for j in range(3):
                up[m][v][j], lo[m][v][j] = ends3(lv[m][v][0][j], lv[m][v][1][j], lv[m][v][2][j])
    return up, lo


def traces_y(lv):
    up = [[[None] * 3 for _ in range(3)] for _ in range(3)]
    lo = [[[None] * 3 for _ in range(3)] for _ in range(3)]
    for m in range(3):
        for v in range(3):
            for i in range(3):
                up[m][v][i], lo[m][v][i] = ends3(lv[m][v][i][0], lv[m][v][i][1], lv[m][v][i][2])
    return up, lo


def lift(acc, lo, up, along_x, scale):
    ko = [scale * LOWER[i] / W[i] for i in range(3)]
    for v in range(3):
        for t in range(3):
            d = lo[v][t] - up[v][t]
            c = ko[1] * d
            x = ko[0] * lo[v][t] - ko[2] * up[v][t]
            z = ko[2] * lo[v][t] - ko[0] * up[v][t]
            for n, k in enumerate((x, c, z)):
                if along_x:
                    acc[v][n][t] = acc[v][n][t] + k
                else:
                    acc[v][t][n] = acc[v][t][n] + k
    return acc


NT = 27
NS = 40
TILES = NX // 8
CHIPS_Z = 8


def k27(a, b, c):
    return a * 9 + b * 3 + c


def lane(x, k):
    return jnp.broadcast_to(x[:, k : k + 1], (8, NY))


def down(x):
    return pltpu.roll(x, NY - 1, 1)


def up1(x):
    return pltpu.roll(x, 1, 1)


def iotas():
    return (
        lax.broadcasted_iota(jnp.int32, (8, NY), 0),
        lax.broadcasted_iota(jnp.int32, (8, NY), 1),
    )


def load_body(st_h, bt_h, fg_h, st, bt, fg, lv_o, te, tw, tu, tl, ax, bx_, ay, by_, ends, sq, sem):
    sub, lan = iotas()

    def copies(t):
        rows = pl.ds(t * 8, 8)
        return [
            pltpu.make_async_copy(h.at[(slice(None),) * n + (rows,)], v.at[(slice(None),) * n + (rows,)], sem.at[k, t])
            for k, (h, v, n) in enumerate(((st_h, st, 1), (bt_h, bt, 1), (fg_h, fg, 0)))
        ]

    for t in range(TILES):
        for c in copies(t):
            c.start()
    sq[NX:, :] = jnp.zeros((NY - NX, NY), F32)
    for k in range(NT):
        te[k, 0:8, :] = jnp.zeros((8, NY), F32)

    def tile(t, carry):
        rows = pl.ds(pl.multiple_of(t * 8, 8), 8)
        wide = pl.ds(pl.multiple_of(t * 8 + 8, 8), 8)
        for c in copies(pl.multiple_of(t, 1)):
            c.wait()
        q = [grid3(lambda i, j: st[k27(v, i, j), rows, :]) for v in range(3)]
        b = grid3(lambda i, j: bt[i * 3 + j, rows, :])
        bx, by = bottom_slopes(b)
        lv = predict(q, bx, by)
        for m in range(3):
            for v in range(3):
                for i in range(3):
                    for j in range(3):
                        lv_o[m * 27 + k27(v, i, j), rows, :] = lv[m][v][i][j]
        up, lo = traces_x(lv)
        for m in range(3):
            for v in range(3):
                for j in range(3):
                    te[k27(m, v, j), wide, :] = up[m][v][j]
                    tw[k27(m, v, j), rows, :] = lo[m][v][j]
        up, lo = traces_y(lv)
        col = jnp.zeros((8, NY), F32)

        def put(col, k, x_lo, x_up):
            col = jnp.where(lan == k, lane(x_lo, 0), col)
            return jnp.where(lan == 64 + k, lane(x_up, NY - 1), col)

        for m in range(3):
            for c, v in enumerate((0, 2, 1)):
                for i in range(3):
                    k = k27(m, c, i)
                    col = put(col, k, lo[m][v][i], up[m][v][i])
                    tu[k, rows, :] = up[m][v][i]
                    tl[k, rows, :] = lo[m][v][i]
        for c, f in enumerate((q[0], q[2], q[1], b)):
            for i in range(3):
                e0, e6 = project_ends(f[i][0], f[i][1], f[i][2])
                col = put(col, NT + c * 3 + i, e0, e6)
        f = fg[rows, :].astype(F32)
        sq[rows, :] = put(col, NS - 1, f, f)
        return carry

    lax.fori_loop(0, TILES, tile, 0)

    for c in range(4):
        for j in range(3):
            if c < 3:
                lo_f = [st[k27(c, i, j), 0:8, :] for i in range(3)]
                up_f = [st[k27(c, i, j), NX - 8 : NX, :] for i in range(3)]
            else:
                lo_f = [bt[i * 3 + j, 0:8, :] for i in range(3)]
                up_f = [bt[i * 3 + j, NX - 8 : NX, :] for i in range(3)]
            ends[c * 3 + j, 0:8, :] = project_ends(*lo_f)[0]
            ends[c * 3 + j, 8:16, :] = project_ends(*up_f)[1]
    even_x = lax.axis_index("gx") % 2 == 0
    even_y = lax.axis_index("gy") % 2 == 0
    sets = (
        (0, NT, tw[:, 0, :], te[:, NX + 7, :]),
        (NT, NS - 1, ends[:, 0, :], ends[:, 15, :]),
        (NS - 1, NS, fg[0:1, :].astype(F32), fg[NX - 1 : NX, :].astype(F32)),
    )
    for a, b, lo_, up_ in sets:
        ax[a:b, :] = jnp.where(even_x, up_, lo_)
        bx_[a:b, :] = jnp.where(even_x, lo_, up_)
    turned = sq[...].T
    lo_, up_ = turned[0:NS], turned[64 : 64 + NS]
    ay[...] = jnp.where(even_y, up_, lo_)
    by_[...] = jnp.where(even_y, lo_, up_)


def crossing():
    iy = lax.axis_index("gy")
    return (iy % CHIPS_Z == 0) & (iy > 0)


def inner_body(early, st, bt, fg, lv_i, te, tw, tu, tl, out, *scratch):
    @pl.when(crossing() if early else jnp.logical_not(crossing()))
    def _():
        inner(st, bt, fg, lv_i, te, tw, tu, tl, out, *scratch)


def inner(st, bt, fg, lv_i, te, tw, tu, tl, out, c6, c0, mom, fx, dg, fd):
    sub, lan = iotas()
    first_lane = lan == 0
    last_lane = lan == NY - 1
    for n in range(9):
        fd[n, NX : NX + 8, :] = jnp.zeros((8, NY), F32)

    def dg_tile(t, carry):
        rows = pl.ds(pl.multiple_of(t * 8, 8), 8)
        b = grid3(lambda i, j: bt[i * 3 + j, rows, :])
        bx, by = bottom_slopes(b)
        lv = [[grid3(lambda i, j: lv_i[m * 27 + k27(v, i, j), rows, :]) for v in range(3)] for m in range(3)]
        acc = volume(lv, bx, by)
        flo = [[None] * 3 for _ in range(3)]
        fup = [[None] * 3 for _ in range(3)]
        for i in range(3):
            fu = []
            for m in range(3):
                qa = [tu[k27(m, c, i), rows, :] for c in range(3)]
                qb = [tl[k27(m, c, i), rows, :] for c in range(3)]
                fb = side_flux(*qb)
                qn = [down(x) for x in qb]
                fn = [qn[1]] + [down(x) for x in fb[1:]]
                fu.append(rusanov2(qa, side_flux(*qa), qn, fn))
            fum = face_mean(fu)
            for s, v in enumerate((0, 2, 1)):
                fup[v][i] = jnp.where(last_lane, 0.0, fum[s])
                flo[v][i] = up1(fup[v][i])
        acc = lift(acc, flo, fup, False, 0.5 / SLOPE)
        for v in range(3):
            for i in range(3):
                for j in range(3):
                    dg[k27(v, i, j), rows, :] = acc[v][i][j]
        back = pl.ds(t * 8 + 7, 8)
        wall = (sub == 0) & (t == 0)
        for j in range(3):
            f = []
            for m in range(3):
                qa = [te[k27(m, v, j), back, :] for v in range(3)]
                qb = [tw[k27(m, v, j), rows, :] for v in range(3)]
                f.append(rusanov2(qa, side_flux(*qa), qb, side_flux(*qb)))
            f = face_mean(f)
            for v in range(3):
                fd[v * 3 + j, rows, :] = jnp.where(wall, 0.0, f[v])
        return carry

    lax.fori_loop(0, TILES, dg_tile, 0)
    for k in range(49):
        c6[k, 0:8, :] = jnp.zeros((8, NY), F32)
        c0[k, NX : NX + 8, :] = jnp.zeros((8, NY), F32)
    for n in range(9):
        fx[n, NX : NX + 8, :] = jnp.zeros((8, NY), F32)

    def tile(t, carry):
        rows = pl.ds(pl.multiple_of(t * 8, 8), 8)
        wide = pl.ds(pl.multiple_of(t * 8 + 8, 8), 8)
        q = [grid3(lambda i, j: st[k27(v, i, j), rows, :]) for v in range(3)]
        q = q + [grid3(lambda i, j: bt[i * 3 + j, rows, :])]
        cols = [[project7(q[v][0][j], q[v][1][j], q[v][2][j]) for j in range(3)] for v in range(4)]
        rowm = []
        cell = []
        prev = None
        for a in range(7):
            cell.append([project7(cols[v][0][a], cols[v][1][a], cols[v][2][a]) for v in range(4)])
            hs, ps, rs, bs = cell[a]
            fl = []
            for c in range(7):
                h, p, r = hs[c], ps[c], rs[c]
                h2 = h * h
                y = lax.rsqrt(h2 + DRY2)
                k = h * (y * y)
                u = p * k
                w = r * k
                pr = 0.5 * h2
                ru = r * u
                cc = lax.rsqrt(y)
                fl.append((p * u + pr, ru, r * w + pr, jnp.abs(u) + cc, jnp.abs(w) + cc))
            if a == 0 or a == 6:
                dst, where_ = (c0, rows) if a == 0 else (c6, wide)
                for c in range(7):
                    for n, x in enumerate((hs[c], ps[c], rs[c], bs[c], fl[c][0], fl[c][1], fl[c][3])):
                        dst[n * 7 + c, where_, :] = x
            gy = []
            for c in range(7):
                f = fl[c]
                if c < 6:
                    g = fl[c + 1]
                    hn, pn, rn, f1, f2, sn = hs[c + 1], ps[c + 1], rs[c + 1], g[1], g[2], g[4]
                else:
                    g = fl[0]
                    hn, pn, rn, f1, f2, sn = [down(x) for x in (hs[0], ps[0], rs[0], g[1], g[2], g[4])]
                s = jnp.maximum(f[4], sn)
                gy.append(
                    (
                        (rs[c] + rn) - s * (hn - hs[c]),
                        (f[1] + f1) - s * (pn - ps[c]),
                        (f[2] + f2) - s * (rn - rs[c]),
                    )
                )
            gy[6] = tuple(jnp.where(last_lane, 0.0, x) for x in gy[6])
            gy = [tuple(up1(x) for x in gy[6])] + gy
            b_hi = jnp.where(last_lane, 0.0, down(bs[0]))
            b_lo = jnp.where(first_lane, 0.0, up1(bs[6]))
            bw = [b_lo] + bs + [b_hi]
            ch = [[gy[c][v] - gy[c + 1][v] for c in range(7)] for v in range(3)]
            ch[2] = [ch[2][c] - hs[c] * (bw[c + 2] - bw[c]) for c in range(7)]
            if prev is not None:
                ph, pp, prr, pb, pfl, pch = prev
                for c in range(7):
                    s = jnp.maximum(pfl[c][3], fl[c][3])
                    f = (
                        (pp[c] + ps[c]) - s * (hs[c] - ph[c]),
                        (pfl[c][0] + fl[c][0]) - s * (ps[c] - pp[c]),
                        (pfl[c][1] + fl[c][1]) - s * (rs[c] - prr[c]),
                    )
                    for v in range(3):
                        pch[v][c] = pch[v][c] - f[v]
                        ch[v][c] = ch[v][c] + f[v]
                for c in range(7):
                    bb = bs[c] - cell[a - 2][3][c] if a >= 2 else bs[c]
                    pch[1][c] = pch[1][c] - ph[c] * bb
                rowm.append([moments7(pch[v]) for v in range(3)])
            prev = (hs, ps, rs, bs, fl, ch)
        ch = prev[5]
        ch[1] = [ch[1][c] + cell[6][0][c] * cell[5][3][c] for c in range(7)]
        rowm.append([moments7(ch[v]) for v in range(3)])
        for v in range(3):
            for n in range(3):
                mm = moments7([rowm[a][v][n] for a in range(7)])
                for m in range(3):
                    mom[k27(v, m, n), rows, :] = mm[m]
        return carry

    lax.fori_loop(0, TILES, tile, 0)

    def faces(t, carry):
        rows = pl.ds(pl.multiple_of(t * 8, 8), 8)
        back = pl.ds(t * 8 + 7, 8)
        wall = (sub == 0) & (t == 0)
        cs = []
        for c in range(7):
            a = [c6[n * 7 + c, back, :] for n in (0, 1, 2, 4, 5, 6)]
            b = [c0[n * 7 + c, rows, :] for n in (0, 1, 2, 4, 5, 6)]
            cs.append(rusanov2(a[:3], (a[1], a[3], a[4], a[5]), b[:3], (b[1], b[3], b[4], b[5])))
        for v in range(3):
            mm = moments7([cs[c][v] for c in range(7)])
            for n in range(3):
                fx[v * 3 + n, rows, :] = jnp.where(wall, 0.0, mm[n])
        return carry

    lax.fori_loop(0, TILES, faces, 0)

    def finish(t, carry):
        rows = pl.ds(pl.multiple_of(t * 8, 8), 8)
        wide = pl.ds(pl.multiple_of(t * 8 + 8, 8), 8)
        back = pl.ds(t * 8 + 7, 8)
        nxt = pl.ds(t * 8 + 1, 8)
        mm = [grid3(lambda m, n: mom[k27(v, m, n), rows, :]) for v in range(3)]
        slo = moments7([c0[c, rows, :] * c6[21 + c, back, :] for c in range(7)])
        shi = moments7([c6[c, wide, :] * c0[21 + c, nxt, :] for c in range(7)])
        flag = fg[rows, :] > 0
        acc = [grid3(lambda i, j: dg[k27(v, i, j), rows, :]) for v in range(3)]
        flo = [[fd[v * 3 + j, rows, :] for j in range(3)] for v in range(3)]
        fup = [[fd[v * 3 + j, nxt, :] for j in range(3)] for v in range(3)]
        acc = lift(acc, flo, fup, True, 0.5 / SLOPE)
        for v in range(3):
            grid = [[None] * 3 for _ in range(3)]
            for n in range(3):
                lo_ = fx[v * 3 + n, rows, :]
                hi_ = fx[v * 3 + n, nxt, :]
                if v == 1:
                    lo_ = lo_ + slo[n]
                    hi_ = hi_ + shi[n]
                s = lo_ - hi_
                d = lo_ + hi_
                c = nodes_of_moments(mm[v][0][n] + s, mm[v][1][n] - 3.0 * d, mm[v][2][n] + 9.0 * s)
                for i in range(3):
                    grid[i][n] = c[i]
            for i in range(3):
                c = nodes_of_moments(grid[i][0], grid[i][1], grid[i][2])
                for j in range(3):
                    k = k27(v, i, j)
                    out[k, rows, :] = jnp.where(flag, 3.5 * c[j], (SLOPE * W[0]) * acc[v][i][j])
        return carry

    lax.fori_loop(0, TILES, finish, 0)


def edge_body(inc1, inc2, ax, bx_, ay, by_, rax, rbx, ray, rby, out, own, rec, kq, kt, buf_o, sem):
    sub, lan = iotas()
    ix, iy = lax.axis_index("gx"), lax.axis_index("gy")
    nx, ny = lax.axis_size("gx"), lax.axis_size("gy")
    even_x = ix % 2 == 0
    even_y = iy % 2 == 0
    own[...] = jnp.zeros((NS, 8, NY), F32)
    rec[...] = jnp.zeros((NS, 8, NY), F32)
    for buf, a, b, c, d in ((own, ax, bx_, ay, by_), (rec, rax, rbx, ray, rby)):
        a, b, c, d = a[...], b[...], c[...], d[...]
        buf[:, 0, :] = jnp.where(even_x, b, a)
        buf[:, 7, :] = jnp.where(even_x, a, b)
        buf[:, 2, :] = jnp.where(even_y, d, c)
        buf[:, 3, :] = jnp.where(even_y, c, d)
    lower = (sub == 0) | (sub == 2)
    atwall = (
        ((sub == 0) & (ix == 0))
        | ((sub == 7) & (ix == nx - 1))
        | ((sub == 2) & (iy == 0))
        | ((sub == 3) & (iy == ny - 1))
    )
    sg = jnp.where(lower, -1.0, 1.0).astype(F32)
    sr = jnp.where(atwall, -sg, sg)
    flag = own[NS - 1] > 0.5

    def other(k):
        return jnp.where(atwall, own[k], rec[k])

    phd = []
    for n in range(3):
        f = []
        for m in range(3):
            qa = [own[k27(m, c, n)] for c in range(3)]
            qb = [other(k27(m, c, n)) for c in range(3)]
            qa[1] = qa[1] * sg
            qb[1] = qb[1] * sr
            f.append(rusanov2(qa, side_flux(*qa), qb, side_flux(*qb)))
        phd.append(face_mean(f))
    ua = [project7(*[own[NT + c * 3 + n] for n in range(3)]) for c in range(3)]
    ub = [project7(*[other(NT + c * 3 + n) for n in range(3)]) for c in range(4)]
    fl = []
    for c in range(7):
        qa = [ua[0][c], ua[1][c] * sg, ua[2][c]]
        qb = [ub[0][c], ub[1][c] * sr, ub[2][c]]
        f = rusanov2(qa, side_flux(*qa), qb, side_flux(*qb))
        f[1] = f[1] + qa[0] * ub[3][c]
        fl.append(f)
    phl = [nodes_of_moments(*moments7([fl[c][v] for c in range(7)])) for v in range(3)]
    rq = nodes_of_moments(1.0, 3.0, 9.0)
    for c in range(3):
        for n in range(3):
            vd = phd[n][c]
            vl = phl[c][n]
            if c == 1:
                vd = vd * sg
                vl = vl * sg
            for k in range(3):
                kq[k27(c, n, k)] = jnp.where(flag, (-3.5 * rq[k]) * vl, (-0.5 * W[0] * UPPER[k] / W[k]) * vd)
    low = kq[:, 2, :]
    high = kq[:, 3, :]
    both = jnp.concatenate([low, jnp.zeros((5, NY), F32), high, jnp.zeros((NY - 59, NY), F32)], 0)
    kt[...] = both.T
    first_lane = lan == 0
    last_lane = lan == NY - 1
    early = crossing()
    copies = []
    for t in range(TILES):
        rows = slice(t * 8, t * 8 + 8)
        z = kt[rows, :]
        for v in range(3):
            c = (0, 2, 1)[v]
            for i in range(3):
                for j in range(3):
                    k = k27(v, i, j)
                    lo_ = lane(z, k27(c, i, 2 - j))
                    up_ = lane(z, 32 + k27(c, i, j))
                    x = jnp.where(early, inc1[k, rows, :], inc2[k, rows, :])
                    x = x + jnp.where(first_lane, lo_, jnp.where(last_lane, up_, 0.0))
                    if t == 0:
                        x = x + jnp.where(sub == 0, kq[k27(v, j, 2 - i)], 0.0)
                    if t == TILES - 1:
                        x = x + jnp.where(sub == 7, kq[k27(v, j, i)], 0.0)
                    buf_o[k, rows, :] = x
        cp = pltpu.make_async_copy(buf_o.at[:, pl.ds(t * 8, 8), :], out.at[:, pl.ds(t * 8, 8), :], sem.at[t])
        cp.start()
        copies.append(cp)
    for cp in copies:
        cp.wait()


def swap_first(n):
    return [(i, i ^ 1) for i in range(n)]


def swap_second(nx, ny, axis):
    out = []
    for a in range(nx):
        for b in range(ny):
            i, n = (a, nx) if axis == 0 else (b, ny)
            j = i + 1 if i % 2 else i - 1
            if not 0 <= j < n:
                to = (a, b ^ CHIPS_Z) if axis == 0 else (a ^ 1, b)
            else:
                to = (j, b) if axis == 0 else (a, j)
            out.append((a * ny + b, to[0] * ny + to[1]))
    return out


VM = pl.BlockSpec(memory_space=pltpu.VMEM)
HB = pl.BlockSpec(memory_space=pltpu.HBM)
PARAMS = pltpu.CompilerParams(vmem_limit_bytes=16 * 1024 * 1024)


def planes(n, rows=NX):
    return pltpu.VMEM((n, rows, NY), F32)


def call(body, name, args, outs, scratch, cost, ins=VM, out_spec=VM):
    return pl.pallas_call(
        body,
        out_shape=outs,
        in_specs=[ins] * len(args),
        out_specs=jax.tree.map(lambda _: out_spec, outs),
        scratch_shapes=scratch,
        compiler_params=PARAMS,
        cost_estimate=pl.CostEstimate(flops=cost, transcendentals=0, bytes_accessed=min(cost, 2**20)),
        name=name,
    )(*args)


def shape(*dims, dtype=F32):
    return jax.ShapeDtypeStruct(dims, dtype)


def shards(state, bathymetry, flags):
    full = shape(27, NX, NY)
    edge = shape(NS, NY)
    nx, ny = lax.axis_size("gx"), lax.axis_size("gy")
    st, bt, fg, lv, te, tw, tu, tl, ax, bx, ay, by = call(
        load_body, "predict",
        tuple(pltpu.with_memory_space_constraint(x, pltpu.HBM)
              for x in (state.reshape(27, NX, NY), bathymetry.reshape(9, NX, NY), flags)),
        (full, shape(9, NX, NY), shape(NX, NY, dtype=jnp.int32), shape(81, NX, NY), shape(NT, NX + 8, NY),
         full, full, full, edge, edge, edge, edge),
        [planes(12, 16), pltpu.VMEM((NY, NY), F32), pltpu.SemaphoreType.DMA((3, TILES))],
        2**24, ins=HB,
    )
    ray = lax.ppermute(ay, "gy", swap_first(ny))
    rax = lax.ppermute(ax, "gx", swap_first(nx))
    rbx = lax.ppermute(bx, ("gx", "gy"), swap_second(nx, ny, 0))
    args = (st, bt, fg, lv, te, tw, tu, tl)
    scratch = [planes(49, NX + 8), planes(49, NX + 8), planes(27), planes(9, NX + 8), planes(27), planes(9, NX + 8)]
    st_, rax = lax.optimization_barrier((st, rax))
    inc1 = call(functools.partial(inner_body, True), "inner_early", (st_,) + args[1:], full, scratch, 2**30)
    by_, inc1 = lax.optimization_barrier((by, inc1))
    rby = lax.ppermute(by_, ("gx", "gy"), swap_second(nx, ny, 1))
    inc2 = call(functools.partial(inner_body, False), "inner", args, full, scratch, 2**10)
    out = call(
        edge_body, "edge", (inc1, inc2, ax, bx, ay, by, rax, rbx, ray, rby), full,
        [planes(NS, 8), planes(NS, 8), planes(27, 8), pltpu.VMEM((NY, NY), F32), planes(27),
         pltpu.SemaphoreType.DMA((TILES,))],
        2**20, out_spec=HB,
    )
    return out.reshape(3, 3, 3, NX, NY)


def solution(mesh):
    in_specs = (P(None, None, None, "gx", "gy"), P(None, None, "gx", "gy"), P("gx", "gy"))
    out_specs = P(None, None, None, "gx", "gy")
    return jax.shard_map(shards, mesh=mesh, in_specs=in_specs, out_specs=out_specs, check_vma=False)
```

```python
import math

import jax
import jax.numpy as jnp
from jax import lax
from jax.experimental import pallas as pl
from jax.experimental.pallas import tpu as pltpu
from jax.sharding import PartitionSpec as P

GRAV = 1.0
DRY2 = 0.05 * 0.05
COURANT = 0.05
SPREAD = math.sqrt(15.0) / 10.0
NODES = [0.5 - SPREAD, 0.5, 0.5 + SPREAD]
W = [5.0 / 18.0, 8.0 / 18.0, 5.0 / 18.0]


def _terms(k):
    o = [NODES[m] for m in range(3) if m != k]
    return o[0] + o[1], o[0] * o[1], (NODES[k] - o[0]) * (NODES[k] - o[1])


def _value(k, x):
    t = _terms(k)
    return (x * x - t[0] * x + t[1]) / t[2]


def _integral(k, x):
    t = _terms(k)
    return (x * x * x / 3.0 - t[0] * x * x / 2.0 + t[1] * x) / t[2]


UPPER = [_value(k, 1.0) for k in range(3)]
LOWER = [_value(k, 0.0) for k in range(3)]
AT = [[_integral(n, NODES[m]) for n in range(3)] for m in range(3)]
SLOPE = 0.5 / SPREAD
PA = 0.5 / SPREAD / 7.0
PE2 = 0.5 / (SPREAD * SPREAD) / 49.0
PE0 = PE2 / 12.0
_S2, _S4 = 28.0, 196.0
_DET = 7.0 * _S4 - _S2 * _S2


def _restorer():
    b0, b2 = -_S2 / _DET / PE2, 7.0 / _DET / PE2
    m0, m2 = _S4 / _DET - PE0 * b0, -_S2 / _DET - PE0 * b2
    return (m0, m2, m0 + b0 / 2.0, m2 + b2 / 2.0, 0.5 / _S2 / PA)


RM0, RM2, RE0, RE2, RA1 = _restorer()
NX, NY = 32, 128
F32 = jnp.float32


def deriv3(f0, f1, f2):
    a = f2 - f0
    e = f0 + f2
    c = (e + e) - 4.0 * f1
    return a - c, a, a + c


def stiff3(f0, f1, f2):
    a = f2 - f0
    g = f0 + f2 + 1.6 * f1
    a2 = a + a
    return a2 - g, -2.5 * a, a2 + g


def ends3(f0, f1, f2):
    m = (0.5 * (UPPER[0] + UPPER[2])) * (f0 + f2) + UPPER[1] * f1
    n = (0.5 * (UPPER[2] - UPPER[0])) * (f2 - f0)
    return m + n, m - n


def project7(f0, f1, f2):
    b = (f0 + f2) - (f1 + f1)
    x = PE2 * b
    y = PA * (f2 - f0)
    c = f1 + PE0 * b
    y2 = y + y
    y3 = y2 + y
    z1 = c + x
    z2 = c + 4.0 * x
    z3 = c + 9.0 * x
    return [z3 - y3, z2 - y2, z1 - y, c, z1 + y, z2 + y2, z3 + y3]


def project_ends(f0, f1, f2):
    b = (f0 + f2) - (f1 + f1)
    z = f1 + (PE0 + 9.0 * PE2) * b
    y = (3.0 * PA) * (f2 - f0)
    return z - y, z + y


def moments7(c):
    e1, a1 = c[4] + c[2], c[4] - c[2]
    e2, a2 = c[5] + c[1], c[5] - c[1]
    e3, a3 = c[6] + c[0], c[6] - c[0]
    return (
        (c[3] + e1) + (e2 + e3),
        a1 + (a2 + a2) + 3.0 * a3,
        e1 + 4.0 * e2 + 9.0 * e3,
    )


def nodes_of_moments(m0, m1, m2):
    e = RE0 * m0 + RE2 * m2
    a = RA1 * m1
    return e - a, RM0 * m0 + RM2 * m2, e + a


def node_fluxes(h, p, r):
    h2 = h * h
    y = lax.rsqrt(h2 + DRY2)
    k = h * (y * y)
    u = p * k
    pr = 0.5 * h2
    ru = r * u
    return p * u + pr, ru, r * (r * k) + pr


def side_flux(h, n, t):
    h2 = h * h
    y = lax.rsqrt(h2 + DRY2)
    u = n * (h * (y * y))
    return n, n * u + 0.5 * h2, t * u, jnp.abs(u) + lax.rsqrt(y)


def rusanov2(qa, fa, qb, fb):
    s = jnp.maximum(fa[3], fb[3])
    return [(fa[v] + fb[v]) - s * (qb[v] - qa[v]) for v in range(3)]


def grid3(f):
    return [[f(i, j) for j in range(3)] for i in range(3)]


def bottom_slopes(b):
    bx = [[None] * 3 for _ in range(3)]
    by = [[None] * 3 for _ in range(3)]
    for j in range(3):
        d = deriv3(b[0][j], b[1][j], b[2][j])
        for i in range(3):
            bx[i][j] = d[i]
    for i in range(3):
        by[i] = list(deriv3(b[i][0], b[i][1], b[i][2]))
    return bx, by


def rate(q, bx, by):
    fl = grid3(lambda i, j: node_fluxes(q[0][i][j], q[1][i][j], q[2][i][j]))
    pu = grid3(lambda i, j: fl[i][j][0])
    ru = grid3(lambda i, j: fl[i][j][1])
    rv = grid3(lambda i, j: fl[i][j][2])
    out = []
    for fx, gy in ((q[1], q[2]), (pu, ru), (ru, rv)):
        acc = [[None] * 3 for _ in range(3)]
        for j in range(3):
            d = deriv3(fx[0][j], fx[1][j], fx[2][j])
            for i in range(3):
                acc[i][j] = d[i]
        for i in range(3):
            d = deriv3(gy[i][0], gy[i][1], gy[i][2])
            for j in range(3):
                acc[i][j] = acc[i][j] + d[j]
        out.append(acc)
    for i in range(3):
        for j in range(3):
            out[1][i][j] = out[1][i][j] + q[0][i][j] * bx[i][j]
            out[2][i][j] = out[2][i][j] + q[0][i][j] * by[i][j]
    return out


def predict(q0, bx, by):
    f = -COURANT * SLOPE
    r = rate(q0, bx, by)
    lv = [[None] * 3 for _ in range(3)]
    for v in range(3):
        mid = grid3(lambda i, j: q0[v][i][j] + (f * 0.5) * r[v][i][j])
        dif = grid3(lambda i, j: (f * SPREAD) * r[v][i][j])
        lv[0][v] = grid3(lambda i, j: mid[i][j] - dif[i][j])
        lv[1][v] = mid
        lv[2][v] = grid3(lambda i, j: mid[i][j] + dif[i][j])
    ka = f * W[0] / 2.0
    kb = f * W[1] / 2.0
    k1 = f * (AT[1][0] - W[0] / 2.0)
    k2 = f * (AT[0][2] - W[2] / 2.0)
    for _ in range(2):
        rs = [rate(lv[m], bx, by) for m in range(3)]
        new = [[[[None] * 3 for _ in range(3)] for _ in range(3)] for _ in range(3)]
        for v in range(3):
            for i in range(3):
                for j in range(3):
                    r0, r1, r2 = rs[0][v][i][j], rs[1][v][i][j], rs[2][v][i][j]
                    base = q0[v][i][j] + ka * (r0 + r2) + kb * r1
                    c1 = (2.0 * k2) * r1
                    new[0][v][i][j] = base + (c1 + k2 * r2)
                    new[1][v][i][j] = base + k1 * (r0 - r2)
                    new[2][v][i][j] = base - (c1 + k2 * r0)
        lv = new
    return lv


def face_mean(f):
    return [(f[0][v] + f[2][v]) + 1.6 * f[1][v] for v in range(3)]


def volume(lv, bx, by):
    fl = [grid3(lambda i, j: node_fluxes(lv[m][0][i][j], lv[m][1][i][j], lv[m][2][i][j])) for m in range(3)]

    def mean(get):
        return grid3(lambda i, j: (get(0, i, j) + get(2, i, j)) + 1.6 * get(1, i, j))

    hm, pm, rm = [mean(lambda m, i, j: lv[m][v][i][j]) for v in range(3)]
    pu, ru, rv = [mean(lambda m, i, j: fl[m][i][j][c]) for c in range(3)]
    out = []
    for fx, gy in ((pm, rm), (pu, ru), (ru, rv)):
        acc = [[None] * 3 for _ in range(3)]
        for j in range(3):
            d = stiff3(fx[0][j], fx[1][j], fx[2][j])
            for i in range(3):
                acc[i][j] = d[i]
        for i in range(3):
            d = stiff3(gy[i][0], gy[i][1], gy[i][2])
            for j in range(3):
                acc[i][j] = acc[i][j] + d[j]
        out.append(acc)
    for i in range(3):
        for j in range(3):
            out[1][i][j] = out[1][i][j] - hm[i][j] * bx[i][j]
            out[2][i][j] = out[2][i][j] - hm[i][j] * by[i][j]
    return out


def traces_x(lv):
    up = [[[None] * 3 for _ in range(3)] for _ in range(3)]
    lo = [[[None] * 3 for _ in range(3)] for _ in range(3)]
    for m in range(3):
        for v in range(3):
            for j in range(3):
                up[m][v][j], lo[m][v][j] = ends3(lv[m][v][0][j], lv[m][v][1][j], lv[m][v][2][j])
    return up, lo


def traces_y(lv):
    up = [[[None] * 3 for _ in range(3)] for _ in range(3)]
    lo = [[[None] * 3 for _ in range(3)] for _ in range(3)]
    for m in range(3):
        for v in range(3):
            for i in range(3):
                up[m][v][i], lo[m][v][i] = ends3(lv[m][v][i][0], lv[m][v][i][1], lv[m][v][i][2])
    return up, lo


def lift(acc, lo, up, along_x, scale):
    ko = [scale * LOWER[i] / W[i] for i in range(3)]
    for v in range(3):
        for t in range(3):
            d = lo[v][t] - up[v][t]
            c = ko[1] * d
            x = ko[0] * lo[v][t] - ko[2] * up[v][t]
            z = ko[2] * lo[v][t] - ko[0] * up[v][t]
            for n, k in enumerate((x, c, z)):
                if along_x:
                    acc[v][n][t] = acc[v][n][t] + k
                else:
                    acc[v][t][n] = acc[v][t][n] + k
    return acc


NT = 27
NS = 40
TILES = NX // 8
CHIPS_Z = 8
EARLY_LONG, EARLY_NEAR = 3, 2


def k27(a, b, c):
    return a * 9 + b * 3 + c


def lane(x, k):
    return jnp.broadcast_to(x[:, k : k + 1], (8, NY))


def down(x):
    return pltpu.roll(x, NY - 1, 1)


def up1(x):
    return pltpu.roll(x, 1, 1)


def iotas():
    return (
        lax.broadcasted_iota(jnp.int32, (8, NY), 0),
        lax.broadcasted_iota(jnp.int32, (8, NY), 1),
    )


def load_body(st_h, bt_h, fg_h, st, bt, fg, lv_o, te, tw, tu, tl, ax, bx_, ay, by_, ends, sq, sem):
    sub, lan = iotas()

    def copies(t):
        rows = pl.ds(t * 8, 8)
        return [
            pltpu.make_async_copy(h.at[(slice(None),) * n + (rows,)], v.at[(slice(None),) * n + (rows,)], sem.at[k, t])
            for k, (h, v, n) in enumerate(((st_h, st, 1), (bt_h, bt, 1), (fg_h, fg, 0)))
        ]

    for t in range(TILES):
        for c in copies(t):
            c.start()
    sq[NX:, :] = jnp.zeros((NY - NX, NY), F32)
    for k in range(NT):
        te[k, 0:8, :] = jnp.zeros((8, NY), F32)

    def tile(t, carry):
        rows = pl.ds(pl.multiple_of(t * 8, 8), 8)
        wide = pl.ds(pl.multiple_of(t * 8 + 8, 8), 8)
        for c in copies(pl.multiple_of(t, 1)):
            c.wait()
        q = [grid3(lambda i, j: st[k27(v, i, j), rows, :]) for v in range(3)]
        b = grid3(lambda i, j: bt[i * 3 + j, rows, :])
        bx, by = bottom_slopes(b)
        lv = predict(q, bx, by)
        for m in range(3):
            for v in range(3):
                for i in range(3):
                    for j in range(3):
                        lv_o[m * 27 + k27(v, i, j), rows, :] = lv[m][v][i][j]
        up, lo = traces_x(lv)
        for m in range(3):
            for v in range(3):
                for j in range(3):
                    te[k27(m, v, j), wide, :] = up[m][v][j]
                    tw[k27(m, v, j), rows, :] = lo[m][v][j]
        up, lo = traces_y(lv)
        col = jnp.zeros((8, NY), F32)

        def put(col, k, x_lo, x_up):
            col = jnp.where(lan == k, lane(x_lo, 0), col)
            return jnp.where(lan == 64 + k, lane(x_up, NY - 1), col)

        for m in range(3):
            for c, v in enumerate((0, 2, 1)):
                for i in range(3):
                    k = k27(m, c, i)
                    col = put(col, k, lo[m][v][i], up[m][v][i])
                    tu[k, rows, :] = up[m][v][i]
                    tl[k, rows, :] = lo[m][v][i]
        for c, f in enumerate((q[0], q[2], q[1], b)):
            for i in range(3):
                e0, e6 = project_ends(f[i][0], f[i][1], f[i][2])
                col = put(col, NT + c * 3 + i, e0, e6)
        f = fg[rows, :].astype(F32)
        sq[rows, :] = put(col, NS - 1, f, f)
        return carry

    lax.fori_loop(0, TILES, tile, 0)

    for c in range(4):
        for j in range(3):
            if c < 3:
                lo_f = [st[k27(c, i, j), 0:8, :] for i in range(3)]
                up_f = [st[k27(c, i, j), NX - 8 : NX, :] for i in range(3)]
            else:
                lo_f = [bt[i * 3 + j, 0:8, :] for i in range(3)]
                up_f = [bt[i * 3 + j, NX - 8 : NX, :] for i in range(3)]
            ends[c * 3 + j, 0:8, :] = project_ends(*lo_f)[0]
            ends[c * 3 + j, 8:16, :] = project_ends(*up_f)[1]
    even_x = lax.axis_index("gx") % 2 == 0
    even_y = lax.axis_index("gy") % 2 == 0
    sets = (
        (0, NT, tw[:, 0, :], te[:, NX + 7, :]),
        (NT, NS - 1, ends[:, 0, :], ends[:, 15, :]),
        (NS - 1, NS, fg[0:1, :].astype(F32), fg[NX - 1 : NX, :].astype(F32)),
    )
    for a, b, lo_, up_ in sets:
        ax[a:b, :] = jnp.where(even_x, up_, lo_)
        bx_[a:b, :] = jnp.where(even_x, lo_, up_)
    turned = sq[...].T
    lo_, up_ = turned[0:NS], turned[64 : 64 + NS]
    ay[...] = jnp.where(even_y, up_, lo_)
    by_[...] = jnp.where(even_y, lo_, up_)


def subcell_tile(st, bt, c6, c0, mom):
    sub, lan = iotas()
    first_lane = lan == 0
    last_lane = lan == NY - 1

    def tile(t, carry):
        rows = pl.ds(pl.multiple_of(t * 8, 8), 8)
        wide = pl.ds(pl.multiple_of(t * 8 + 8, 8), 8)
        q = [grid3(lambda i, j: st[k27(v, i, j), rows, :]) for v in range(3)]
        q = q + [grid3(lambda i, j: bt[i * 3 + j, rows, :])]
        cols = [[project7(q[v][0][j], q[v][1][j], q[v][2][j]) for j in range(3)] for v in range(4)]
        rowm = []
        cell = []
        prev = None
        for a in range(7):
            cell.append([project7(cols[v][0][a], cols[v][1][a], cols[v][2][a]) for v in range(4)])
            hs, ps, rs, bs = cell[a]
            fl = []
            for c in range(7):
                h, p, r = hs[c], ps[c], rs[c]
                h2 = h * h
                y = lax.rsqrt(h2 + DRY2)
                k = h * (y * y)
                u = p * k
                w = r * k
                pr = 0.5 * h2
                ru = r * u
                cc = lax.rsqrt(y)
                fl.append((p * u + pr, ru, r * w + pr, jnp.abs(u) + cc, jnp.abs(w) + cc))
            if a == 0 or a == 6:
                dst, where_ = (c0, rows) if a == 0 else (c6, wide)
                for c in range(7):
                    for n, x in enumerate((hs[c], ps[c], rs[c], bs[c], fl[c][0], fl[c][1], fl[c][3])):
                        dst[n * 7 + c, where_, :] = x
            gy = []
            for c in range(7):
                f = fl[c]
                if c < 6:
                    g = fl[c + 1]
                    hn, pn, rn, f1, f2, sn = hs[c + 1], ps[c + 1], rs[c + 1], g[1], g[2], g[4]
                else:
                    g = fl[0]
                    hn, pn, rn, f1, f2, sn = [down(x) for x in (hs[0], ps[0], rs[0], g[1], g[2], g[4])]
                s = jnp.maximum(f[4], sn)
                gy.append(
                    (
                        (rs[c] + rn) - s * (hn - hs[c]),
                        (f[1] + f1) - s * (pn - ps[c]),
                        (f[2] + f2) - s * (rn - rs[c]),
                    )
                )
            gy[6] = tuple(jnp.where(last_lane, 0.0, x) for x in gy[6])
            gy = [tuple(up1(x) for x in gy[6])] + gy
            b_hi = jnp.where(last_lane, 0.0, down(bs[0]))
            b_lo = jnp.where(first_lane, 0.0, up1(bs[6]))
            bw = [b_lo] + bs + [b_hi]
            ch = [[gy[c][v] - gy[c + 1][v] for c in range(7)] for v in range(3)]
            ch[2] = [ch[2][c] - hs[c] * (bw[c + 2] - bw[c]) for c in range(7)]
            if prev is not None:
                ph, pp, prr, pb, pfl, pch = prev
                for c in range(7):
                    s = jnp.maximum(pfl[c][3], fl[c][3])
                    f = (
                        (pp[c] + ps[c]) - s * (hs[c] - ph[c]),
                        (pfl[c][0] + fl[c][0]) - s * (ps[c] - pp[c]),
                        (pfl[c][1] + fl[c][1]) - s * (rs[c] - prr[c]),
                    )
                    for v in range(3):
                        pch[v][c] = pch[v][c] - f[v]
                        ch[v][c] = ch[v][c] + f[v]
                for c in range(7):
                    bb = bs[c] - cell[a - 2][3][c] if a >= 2 else bs[c]
                    pch[1][c] = pch[1][c] - ph[c] * bb
                rowm.append([moments7(pch[v]) for v in range(3)])
            prev = (hs, ps, rs, bs, fl, ch)
        ch = prev[5]
        ch[1] = [ch[1][c] + cell[6][0][c] * cell[5][3][c] for c in range(7)]
        rowm.append([moments7(ch[v]) for v in range(3)])
        for v in range(3):
            for n in range(3):
                mm = moments7([rowm[a][v][n] for a in range(7)])
                for m in range(3):
                    mom[k27(v, m, n), rows, :] = mm[m]
        return carry

    return tile


def early_tiles():
    iy = lax.axis_index("gy")
    z = iy % CHIPS_Z
    n = jnp.where((z == 1) | (z == 3), EARLY_NEAR, 0)
    return jnp.where((z == 0) & (iy > 0), EARLY_LONG, n)


def limit_body(st, bt, c6, c0, mom):
    lax.fori_loop(0, early_tiles(), subcell_tile(st, bt, c6, c0, mom), 0)


def inner_body(st, bt, fg, lv_i, te, tw, tu, tl, e6, e0, em, out, c6, c0, mom, fx, dg, fd):
    sub, lan = iotas()
    last_lane = lan == NY - 1
    for n in range(9):
        fd[n, NX : NX + 8, :] = jnp.zeros((8, NY), F32)
        fx[n, NX : NX + 8, :] = jnp.zeros((8, NY), F32)
    for k in range(49):
        c6[k, 0:8, :] = jnp.zeros((8, NY), F32)
        c0[k, NX : NX + 8, :] = jnp.zeros((8, NY), F32)

    def keep(t, carry):
        rows = pl.ds(pl.multiple_of(t * 8, 8), 8)
        wide = pl.ds(pl.multiple_of(t * 8 + 8, 8), 8)
        for k in range(49):
            c6[k, wide, :] = e6[k, wide, :]
            c0[k, rows, :] = e0[k, rows, :]
        for k in range(27):
            mom[k, rows, :] = em[k, rows, :]
        return carry

    done = early_tiles()
    lax.fori_loop(0, done, keep, 0)
    lax.fori_loop(done, TILES, subcell_tile(st, bt, c6, c0, mom), 0)

    def dg_tile(t, carry):
        rows = pl.ds(pl.multiple_of(t * 8, 8), 8)
        b = grid3(lambda i, j: bt[i * 3 + j, rows, :])
        bx, by = bottom_slopes(b)
        lv = [[grid3(lambda i, j: lv_i[m * 27 + k27(v, i, j), rows, :]) for v in range(3)] for m in range(3)]
        acc = volume(lv, bx, by)
        flo = [[None] * 3 for _ in range(3)]
        fup = [[None] * 3 for _ in range(3)]
        for i in range(3):
            fu = []
            for m in range(3):
                qa = [tu[k27(m, c, i), rows, :] for c in range(3)]
                qb = [tl[k27(m, c, i), rows, :] for c in range(3)]
                fb = side_flux(*qb)
                qn = [down(x) for x in qb]
                fn = [qn[1]] + [down(x) for x in fb[1:]]
                fu.append(rusanov2(qa, side_flux(*qa), qn, fn))
            fum = face_mean(fu)
            for s, v in enumerate((0, 2, 1)):
                fup[v][i] = jnp.where(last_lane, 0.0, fum[s])
                flo[v][i] = up1(fup[v][i])
        acc = lift(acc, flo, fup, False, 0.5 / SLOPE)
        for v in range(3):
            for i in range(3):
                for j in range(3):
                    dg[k27(v, i, j), rows, :] = acc[v][i][j]
        back = pl.ds(t * 8 + 7, 8)
        wall = (sub == 0) & (t == 0)
        for j in range(3):
            f = []
            for m in range(3):
                qa = [te[k27(m, v, j), back, :] for v in range(3)]
                qb = [tw[k27(m, v, j), rows, :] for v in range(3)]
                f.append(rusanov2(qa, side_flux(*qa), qb, side_flux(*qb)))
            f = face_mean(f)
            for v in range(3):
                fd[v * 3 + j, rows, :] = jnp.where(wall, 0.0, f[v])
        return carry

    lax.fori_loop(0, TILES, dg_tile, 0)

    def faces(t, carry):
        rows = pl.ds(pl.multiple_of(t * 8, 8), 8)
        back = pl.ds(t * 8 + 7, 8)
        wall = (sub == 0) & (t == 0)
        cs = []
        for c in range(7):
            a = [c6[n * 7 + c, back, :] for n in (0, 1, 2, 4, 5, 6)]
            b = [c0[n * 7 + c, rows, :] for n in (0, 1, 2, 4, 5, 6)]
            cs.append(rusanov2(a[:3], (a[1], a[3], a[4], a[5]), b[:3], (b[1], b[3], b[4], b[5])))
        for v in range(3):
            mm = moments7([cs[c][v] for c in range(7)])
            for n in range(3):
                fx[v * 3 + n, rows, :] = jnp.where(wall, 0.0, mm[n])
        return carry

    lax.fori_loop(0, TILES, faces, 0)

    def finish(t, carry):
        rows = pl.ds(pl.multiple_of(t * 8, 8), 8)
        wide = pl.ds(pl.multiple_of(t * 8 + 8, 8), 8)
        back = pl.ds(t * 8 + 7, 8)
        nxt = pl.ds(t * 8 + 1, 8)
        flag = fg[rows, :] > 0
        acc = [grid3(lambda i, j: dg[k27(v, i, j), rows, :]) for v in range(3)]
        flo = [[fd[v * 3 + j, rows, :] for j in range(3)] for v in range(3)]
        fup = [[fd[v * 3 + j, nxt, :] for j in range(3)] for v in range(3)]
        acc = lift(acc, flo, fup, True, 0.5 / SLOPE)
        mm = [grid3(lambda m, n: mom[k27(v, m, n), rows, :]) for v in range(3)]
        slo = moments7([c0[c, rows, :] * c6[21 + c, back, :] for c in range(7)])
        shi = moments7([c6[c, wide, :] * c0[21 + c, nxt, :] for c in range(7)])
        for v in range(3):
            grid = [[None] * 3 for _ in range(3)]
            for n in range(3):
                lo_ = fx[v * 3 + n, rows, :]
                hi_ = fx[v * 3 + n, nxt, :]
                if v == 1:
                    lo_ = lo_ + slo[n]
                    hi_ = hi_ + shi[n]
                s = lo_ - hi_
                d = lo_ + hi_
                c = nodes_of_moments(mm[v][0][n] + s, mm[v][1][n] - 3.0 * d, mm[v][2][n] + 9.0 * s)
                for i in range(3):
                    grid[i][n] = c[i]
            for i in range(3):
                c = nodes_of_moments(grid[i][0], grid[i][1], grid[i][2])
                for j in range(3):
                    k = k27(v, i, j)
                    out[k, rows, :] = jnp.where(flag, 3.5 * c[j], (SLOPE * W[0]) * acc[v][i][j])
        return carry

    lax.fori_loop(0, TILES, finish, 0)


def edge_body(inc, ax, bx_, ay, by_, rax, rbx, ray, rby, out, own, rec, kq, kt, buf_o, sem):
    sub, lan = iotas()
    ix, iy = lax.axis_index("gx"), lax.axis_index("gy")
    nx, ny = lax.axis_size("gx"), lax.axis_size("gy")
    even_x = ix % 2 == 0
    even_y = iy % 2 == 0
    own[...] = jnp.zeros((NS, 8, NY), F32)
    rec[...] = jnp.zeros((NS, 8, NY), F32)
    for buf, a, b, c, d in ((own, ax, bx_, ay, by_), (rec, rax, rbx, ray, rby)):
        a, b, c, d = a[...], b[...], c[...], d[...]
        buf[:, 0, :] = jnp.where(even_x, b, a)
        buf[:, 7, :] = jnp.where(even_x, a, b)
        buf[:, 2, :] = jnp.where(even_y, d, c)
        buf[:, 3, :] = jnp.where(even_y, c, d)
    lower = (sub == 0) | (sub == 2)
    atwall = (
        ((sub == 0) & (ix == 0))
        | ((sub == 7) & (ix == nx - 1))
        | ((sub == 2) & (iy == 0))
        | ((sub == 3) & (iy == ny - 1))
    )
    sg = jnp.where(lower, -1.0, 1.0).astype(F32)
    sr = jnp.where(atwall, -sg, sg)
    flag = own[NS - 1] > 0.5

    def other(k):
        return jnp.where(atwall, own[k], rec[k])

    phd = []
    for n in range(3):
        f = []
        for m in range(3):
            qa = [own[k27(m, c, n)] for c in range(3)]
            qb = [other(k27(m, c, n)) for c in range(3)]
            qa[1] = qa[1] * sg
            qb[1] = qb[1] * sr
            f.append(rusanov2(qa, side_flux(*qa), qb, side_flux(*qb)))
        phd.append(face_mean(f))
    ua = [project7(*[own[NT + c * 3 + n] for n in range(3)]) for c in range(3)]
    ub = [project7(*[other(NT + c * 3 + n) for n in range(3)]) for c in range(4)]
    fl = []
    for c in range(7):
        qa = [ua[0][c], ua[1][c] * sg, ua[2][c]]
        qb = [ub[0][c], ub[1][c] * sr, ub[2][c]]
        f = rusanov2(qa, side_flux(*qa), qb, side_flux(*qb))
        f[1] = f[1] + qa[0] * ub[3][c]
        fl.append(f)
    phl = [nodes_of_moments(*moments7([fl[c][v] for c in range(7)])) for v in range(3)]
    rq = nodes_of_moments(1.0, 3.0, 9.0)
    for c in range(3):
        for n in range(3):
            vd = phd[n][c]
            vl = phl[c][n]
            if c == 1:
                vd = vd * sg
                vl = vl * sg
            for k in range(3):
                kq[k27(c, n, k)] = jnp.where(flag, (-3.5 * rq[k]) * vl, (-0.5 * W[0] * UPPER[k] / W[k]) * vd)
    low = kq[:, 2, :]
    high = kq[:, 3, :]
    both = jnp.concatenate([low, jnp.zeros((5, NY), F32), high, jnp.zeros((NY - 59, NY), F32)], 0)
    kt[...] = both.T
    first_lane = lan == 0
    last_lane = lan == NY - 1
    copies = []
    for t in range(TILES):
        rows = slice(t * 8, t * 8 + 8)
        z = kt[rows, :]
        for v in range(3):
            c = (0, 2, 1)[v]
            for i in range(3):
                for j in range(3):
                    k = k27(v, i, j)
                    lo_ = lane(z, k27(c, i, 2 - j))
                    up_ = lane(z, 32 + k27(c, i, j))
                    x = inc[k, rows, :]
                    x = x + jnp.where(first_lane, lo_, jnp.where(last_lane, up_, 0.0))
                    if t == 0:
                        x = x + jnp.where(sub == 0, kq[k27(v, j, 2 - i)], 0.0)
                    if t == TILES - 1:
                        x = x + jnp.where(sub == 7, kq[k27(v, j, i)], 0.0)
                    buf_o[k, rows, :] = x
        cp = pltpu.make_async_copy(buf_o.at[:, pl.ds(t * 8, 8), :], out.at[:, pl.ds(t * 8, 8), :], sem.at[t])
        cp.start()
        copies.append(cp)
    for cp in copies:
        cp.wait()


def swap_first(n):
    return [(i, i ^ 1) for i in range(n)]


def swap_second(nx, ny, axis):
    out = []
    for a in range(nx):
        for b in range(ny):
            i, n = (a, nx) if axis == 0 else (b, ny)
            j = i + 1 if i % 2 else i - 1
            if not 0 <= j < n:
                to = (a, b ^ CHIPS_Z) if axis == 0 else (a ^ 1, b)
            else:
                to = (j, b) if axis == 0 else (a, j)
            out.append((a * ny + b, to[0] * ny + to[1]))
    return out


VM = pl.BlockSpec(memory_space=pltpu.VMEM)
HB = pl.BlockSpec(memory_space=pltpu.HBM)
PARAMS = pltpu.CompilerParams(vmem_limit_bytes=16 * 1024 * 1024)


def planes(n, rows=NX):
    return pltpu.VMEM((n, rows, NY), F32)


def call(body, name, args, outs, scratch, cost, ins=VM, out_spec=VM):
    return pl.pallas_call(
        body,
        out_shape=outs,
        in_specs=[ins] * len(args),
        out_specs=jax.tree.map(lambda _: out_spec, outs),
        scratch_shapes=scratch,
        compiler_params=PARAMS,
        cost_estimate=pl.CostEstimate(flops=cost, transcendentals=0, bytes_accessed=min(cost, 2**20)),
        name=name,
    )(*args)


def shape(*dims, dtype=F32):
    return jax.ShapeDtypeStruct(dims, dtype)


def shards(state, bathymetry, flags):
    full = shape(27, NX, NY)
    edge = shape(NS, NY)
    nx, ny = lax.axis_size("gx"), lax.axis_size("gy")
    st, bt, fg, lv, te, tw, tu, tl, ax, bx, ay, by = call(
        load_body, "predict",
        tuple(pltpu.with_memory_space_constraint(x, pltpu.HBM)
              for x in (state.reshape(27, NX, NY), bathymetry.reshape(9, NX, NY), flags)),
        (full, shape(9, NX, NY), shape(NX, NY, dtype=jnp.int32), shape(81, NX, NY), shape(NT, NX + 8, NY),
         full, full, full, edge, edge, edge, edge),
        [planes(12, 16), pltpu.VMEM((NY, NY), F32), pltpu.SemaphoreType.DMA((3, TILES))],
        2**24, ins=HB,
    )
    ray = lax.ppermute(ay, "gy", swap_first(ny))
    rax = lax.ppermute(ax, "gx", swap_first(nx))
    rbx = lax.ppermute(bx, ("gx", "gy"), swap_second(nx, ny, 0))
    st_, rax = lax.optimization_barrier((st, rax))
    part = call(limit_body, "limit_early", (st_, bt), (shape(49, NX + 8, NY), shape(49, NX + 8, NY), full), [], 2**30)
    by_, part = lax.optimization_barrier((by, part))
    rby = lax.ppermute(by_, ("gx", "gy"), swap_second(nx, ny, 1))
    inc = call(
        inner_body, "inner", (st, bt, fg, lv, te, tw, tu, tl) + tuple(part), full,
        [planes(49, NX + 8), planes(49, NX + 8), planes(27), planes(9, NX + 8), planes(27), planes(9, NX + 8)], 2**10,
    )
    out = call(
        edge_body, "edge", (inc, ax, bx, ay, by, rax, rbx, ray, rby), full,
        [planes(NS, 8), planes(NS, 8), planes(27, 8), pltpu.VMEM((NY, NY), F32), planes(27),
         pltpu.SemaphoreType.DMA((TILES,))],
        2**20, out_spec=HB,
    )
    return out.reshape(3, 3, 3, NX, NY)


def solution(mesh):
    in_specs = (P(None, None, None, "gx", "gy"), P(None, None, "gx", "gy"), P("gx", "gy"))
    out_specs = P(None, None, None, "gx", "gy")
    return jax.shard_map(shards, mesh=mesh, in_specs=in_specs, out_specs=out_specs, check_vma=False)
```

```python
import math

import jax
import jax.numpy as jnp
from jax import lax
from jax.experimental import pallas as pl
from jax.experimental.pallas import tpu as pltpu
from jax.sharding import PartitionSpec as P

GRAV = 1.0
DRY2 = 0.05 * 0.05
COURANT = 0.05
SPREAD = math.sqrt(15.0) / 10.0
NODES = [0.5 - SPREAD, 0.5, 0.5 + SPREAD]
W = [5.0 / 18.0, 8.0 / 18.0, 5.0 / 18.0]


def _terms(k):
    o = [NODES[m] for m in range(3) if m != k]
    return o[0] + o[1], o[0] * o[1], (NODES[k] - o[0]) * (NODES[k] - o[1])


def _value(k, x):
    t = _terms(k)
    return (x * x - t[0] * x + t[1]) / t[2]


def _integral(k, x):
    t = _terms(k)
    return (x * x * x / 3.0 - t[0] * x * x / 2.0 + t[1] * x) / t[2]


UPPER = [_value(k, 1.0) for k in range(3)]
LOWER = [_value(k, 0.0) for k in range(3)]
AT = [[_integral(n, NODES[m]) for n in range(3)] for m in range(3)]
SLOPE = 0.5 / SPREAD
PA = 0.5 / SPREAD / 7.0
PE2 = 0.5 / (SPREAD * SPREAD) / 49.0
PE0 = PE2 / 12.0
_S2, _S4 = 28.0, 196.0
_DET = 7.0 * _S4 - _S2 * _S2


def _restorer():
    b0, b2 = -_S2 / _DET / PE2, 7.0 / _DET / PE2
    m0, m2 = _S4 / _DET - PE0 * b0, -_S2 / _DET - PE0 * b2
    return (m0, m2, m0 + b0 / 2.0, m2 + b2 / 2.0, 0.5 / _S2 / PA)


RM0, RM2, RE0, RE2, RA1 = _restorer()
NX, NY = 32, 128
F32 = jnp.float32


def deriv3(f0, f1, f2):
    a = f2 - f0
    e = f0 + f2
    c = (e + e) - 4.0 * f1
    return a - c, a, a + c


def stiff3(f0, f1, f2):
    a = f2 - f0
    g = f0 + f2 + 1.6 * f1
    a2 = a + a
    return a2 - g, -2.5 * a, a2 + g


def ends3(f0, f1, f2):
    m = (0.5 * (UPPER[0] + UPPER[2])) * (f0 + f2) + UPPER[1] * f1
    n = (0.5 * (UPPER[2] - UPPER[0])) * (f2 - f0)
    return m + n, m - n


def project7(f0, f1, f2):
    b = (f0 + f2) - (f1 + f1)
    x = PE2 * b
    y = PA * (f2 - f0)
    c = f1 + PE0 * b
    y2 = y + y
    y3 = y2 + y
    z1 = c + x
    z2 = c + 4.0 * x
    z3 = c + 9.0 * x
    return [z3 - y3, z2 - y2, z1 - y, c, z1 + y, z2 + y2, z3 + y3]


def project_ends(f0, f1, f2):
    b = (f0 + f2) - (f1 + f1)
    z = f1 + (PE0 + 9.0 * PE2) * b
    y = (3.0 * PA) * (f2 - f0)
    return z - y, z + y


def moments7(c):
    e1, a1 = c[4] + c[2], c[4] - c[2]
    e2, a2 = c[5] + c[1], c[5] - c[1]
    e3, a3 = c[6] + c[0], c[6] - c[0]
    return (
        (c[3] + e1) + (e2 + e3),
        a1 + (a2 + a2) + 3.0 * a3,
        e1 + 4.0 * e2 + 9.0 * e3,
    )


def nodes_of_moments(m0, m1, m2):
    e = RE0 * m0 + RE2 * m2
    a = RA1 * m1
    return e - a, RM0 * m0 + RM2 * m2, e + a


def node_fluxes(h, p, r):
    h2 = h * h
    y = lax.rsqrt(h2 + DRY2)
    k = h * (y * y)
    u = p * k
    pr = 0.5 * h2
    ru = r * u
    return p * u + pr, ru, r * (r * k) + pr


def side_flux(h, n, t):
    h2 = h * h
    y = lax.rsqrt(h2 + DRY2)
    u = n * (h * (y * y))
    return n, n * u + 0.5 * h2, t * u, jnp.abs(u) + lax.rsqrt(y)


def rusanov2(qa, fa, qb, fb):
    s = jnp.maximum(fa[3], fb[3])
    return [(fa[v] + fb[v]) - s * (qb[v] - qa[v]) for v in range(3)]


def grid3(f):
    return [[f(i, j) for j in range(3)] for i in range(3)]


def bottom_slopes(b):
    bx = [[None] * 3 for _ in range(3)]
    by = [[None] * 3 for _ in range(3)]
    for j in range(3):
        d = deriv3(b[0][j], b[1][j], b[2][j])
        for i in range(3):
            bx[i][j] = d[i]
    for i in range(3):
        by[i] = list(deriv3(b[i][0], b[i][1], b[i][2]))
    return bx, by


def rate(q, bx, by):
    fl = grid3(lambda i, j: node_fluxes(q[0][i][j], q[1][i][j], q[2][i][j]))
    pu = grid3(lambda i, j: fl[i][j][0])
    ru = grid3(lambda i, j: fl[i][j][1])
    rv = grid3(lambda i, j: fl[i][j][2])
    out = []
    for fx, gy in ((q[1], q[2]), (pu, ru), (ru, rv)):
        acc = [[None] * 3 for _ in range(3)]
        for j in range(3):
            d = deriv3(fx[0][j], fx[1][j], fx[2][j])
            for i in range(3):
                acc[i][j] = d[i]
        for i in range(3):
            d = deriv3(gy[i][0], gy[i][1], gy[i][2])
            for j in range(3):
                acc[i][j] = acc[i][j] + d[j]
        out.append(acc)
    for i in range(3):
        for j in range(3):
            out[1][i][j] = out[1][i][j] + q[0][i][j] * bx[i][j]
            out[2][i][j] = out[2][i][j] + q[0][i][j] * by[i][j]
    return out


def predict(q0, bx, by):
    f = -COURANT * SLOPE
    r = rate(q0, bx, by)
    lv = [[None] * 3 for _ in range(3)]
    for v in range(3):
        mid = grid3(lambda i, j: q0[v][i][j] + (f * 0.5) * r[v][i][j])
        dif = grid3(lambda i, j: (f * SPREAD) * r[v][i][j])
        lv[0][v] = grid3(lambda i, j: mid[i][j] - dif[i][j])
        lv[1][v] = mid
        lv[2][v] = grid3(lambda i, j: mid[i][j] + dif[i][j])
    ka = f * W[0] / 2.0
    kb = f * W[1] / 2.0
    k1 = f * (AT[1][0] - W[0] / 2.0)
    k2 = f * (AT[0][2] - W[2] / 2.0)
    for _ in range(2):
        rs = [rate(lv[m], bx, by) for m in range(3)]
        new = [[[[None] * 3 for _ in range(3)] for _ in range(3)] for _ in range(3)]
        for v in range(3):
            for i in range(3):
                for j in range(3):
                    r0, r1, r2 = rs[0][v][i][j], rs[1][v][i][j], rs[2][v][i][j]
                    base = q0[v][i][j] + ka * (r0 + r2) + kb * r1
                    c1 = (2.0 * k2) * r1
                    new[0][v][i][j] = base + (c1 + k2 * r2)
                    new[1][v][i][j] = base + k1 * (r0 - r2)
                    new[2][v][i][j] = base - (c1 + k2 * r0)
        lv = new
    return lv


def face_mean(f):
    return [(f[0][v] + f[2][v]) + 1.6 * f[1][v] for v in range(3)]


def volume(lv, bx, by):
    fl = [grid3(lambda i, j: node_fluxes(lv[m][0][i][j], lv[m][1][i][j], lv[m][2][i][j])) for m in range(3)]

    def mean(get):
        return grid3(lambda i, j: (get(0, i, j) + get(2, i, j)) + 1.6 * get(1, i, j))

    hm, pm, rm = [mean(lambda m, i, j: lv[m][v][i][j]) for v in range(3)]
    pu, ru, rv = [mean(lambda m, i, j: fl[m][i][j][c]) for c in range(3)]
    out = []
    for fx, gy in ((pm, rm), (pu, ru), (ru, rv)):
        acc = [[None] * 3 for _ in range(3)]
        for j in range(3):
            d = stiff3(fx[0][j], fx[1][j], fx[2][j])
            for i in range(3):
                acc[i][j] = d[i]
        for i in range(3):
            d = stiff3(gy[i][0], gy[i][1], gy[i][2])
            for j in range(3):
                acc[i][j] = acc[i][j] + d[j]
        out.append(acc)
    for i in range(3):
        for j in range(3):
            out[1][i][j] = out[1][i][j] - hm[i][j] * bx[i][j]
            out[2][i][j] = out[2][i][j] - hm[i][j] * by[i][j]
    return out


def traces_x(lv):
    up = [[[None] * 3 for _ in range(3)] for _ in range(3)]
    lo = [[[None] * 3 for _ in range(3)] for _ in range(3)]
    for m in range(3):
        for v in range(3):
            for j in range(3):
                up[m][v][j], lo[m][v][j] = ends3(lv[m][v][0][j], lv[m][v][1][j], lv[m][v][2][j])
    return up, lo


def traces_y(lv):
    up = [[[None] * 3 for _ in range(3)] for _ in range(3)]
    lo = [[[None] * 3 for _ in range(3)] for _ in range(3)]
    for m in range(3):
        for v in range(3):
            for i in range(3):
                up[m][v][i], lo[m][v][i] = ends3(lv[m][v][i][0], lv[m][v][i][1], lv[m][v][i][2])
    return up, lo


def lift(acc, lo, up, along_x, scale):
    ko = [scale * LOWER[i] / W[i] for i in range(3)]
    for v in range(3):
        for t in range(3):
            d = lo[v][t] - up[v][t]
            c = ko[1] * d
            x = ko[0] * lo[v][t] - ko[2] * up[v][t]
            z = ko[2] * lo[v][t] - ko[0] * up[v][t]
            for n, k in enumerate((x, c, z)):
                if along_x:
                    acc[v][n][t] = acc[v][n][t] + k
                else:
                    acc[v][t][n] = acc[v][t][n] + k
    return acc


NT = 27
NS = 40
TILES = NX // 8
CHIPS_Z = 8
EARLY_LONG, EARLY_NEAR = 0, 2


def k27(a, b, c):
    return a * 9 + b * 3 + c


def lane(x, k):
    return jnp.broadcast_to(x[:, k : k + 1], (8, NY))


def down(x):
    return pltpu.roll(x, NY - 1, 1)


def up1(x):
    return pltpu.roll(x, 1, 1)


def iotas():
    return (
        lax.broadcasted_iota(jnp.int32, (8, NY), 0),
        lax.broadcasted_iota(jnp.int32, (8, NY), 1),
    )


def send_body(st_h, bt_h, fg_h, st, bt, fg, ax, bx_, ay, by_, sq, kt, pk, sd, sem):
    sub, lan = iotas()

    def copies(t):
        rows = pl.ds(t * 8, 8)
        return [
            pltpu.make_async_copy(h.at[(slice(None),) * n + (rows,)], v.at[(slice(None),) * n + (rows,)], sem.at[k, t])
            for k, (h, v, n) in enumerate(((st_h, st, 1), (bt_h, bt, 1), (fg_h, fg, 0)))
        ]

    for t in range(TILES):
        for c in copies(t):
            c.start()
    sq[NX:, :] = jnp.zeros((NY - NX, NY), F32)
    half = ((lan + 1) & (NY - 1)) >> 1

    def columns(t, carry):
        rows = pl.ds(pl.multiple_of(t * 8, 8), 8)
        for c in copies(t):
            c.wait()
        col = jnp.zeros((8, NY), F32)
        for k in range(37):
            if k < 27:
                x = st[k, rows, :]
            elif k < 36:
                x = bt[k - 27, rows, :]
            else:
                x = fg[rows, :].astype(F32)
            col = jnp.where(half == k, pltpu.roll(x, 2 * k, 1) if k else x, col)
        sq[rows, :] = col
        return carry

    lax.fori_loop(0, TILES, columns, 0)
    for c in range(4):
        for n in range(3):
            to = slice(k27(c, n, 0), k27(c, n, 0) + 3)
            src, o = (st, c * 9) if c < 3 else (bt, 0)
            pk[to, 0, :] = src[o + (2 - n) * 3 : o + (2 - n) * 3 + 3, 0, :]
            pk[to, 7, :] = src[o + n * 3 : o + n * 3 + 3, NX - 1, :]
    pk[36:37, 0, :] = fg[0:1, :].astype(F32)
    pk[36:37, 7, :] = fg[NX - 1 : NX, :].astype(F32)
    kt[...] = sq[...].T
    for c, v in enumerate((0, 2, 1, 3)):
        for n in range(3):
            to = slice(k27(c, n, 0), k27(c, n, 0) + 3)
            pk[to, 2, :] = kt[pl.ds(2 * k27(v, 0, 2 - n), 3, stride=6), :]
            if v == 0 and n == 0:
                pk[0:1, 3, :] = kt[NY - 1 : NY, :]
                pk[1:3, 3, :] = kt[pl.ds(5, 2, stride=6), :]
            else:
                pk[to, 3, :] = kt[pl.ds(2 * k27(v, 0, n) - 1, 3, stride=6), :]
    pk[36:37, 2, :] = kt[72:73, :]
    pk[36:37, 3, :] = kt[71:72, :]
    sg = jnp.where((sub == 0) | (sub == 2), -1.0, 1.0).astype(F32)
    q = [grid3(lambda i, j: pk[k27(c, i, j)]) for c in range(4)]
    q[1] = grid3(lambda i, j: q[1][i][j] * sg)
    bx, by = bottom_slopes(q[3])
    lv = predict(q[:3], bx, by)
    for m in range(3):
        for c in range(3):
            for j in range(3):
                sd[k27(m, c, j)] = ends3(lv[m][c][0][j], lv[m][c][1][j], lv[m][c][2][j])[0]
    for c in range(4):
        for j in range(3):
            sd[NT + c * 3 + j] = project_ends(q[c][0][j], q[c][1][j], q[c][2][j])[1]
    sd[NS - 1] = pk[36]
    even_x = lax.axis_index("gx") % 2 == 0
    even_y = lax.axis_index("gy") % 2 == 0
    for a, b, lo_, up_, even in ((ax, bx_, 0, 7, even_x), (ay, by_, 2, 3, even_y)):
        lo_, up_ = sd[:, lo_, :], sd[:, up_, :]
        a[...] = jnp.where(even, up_, lo_)
        b[...] = jnp.where(even, lo_, up_)


def subcell_tile(st, bt, c6, c0, mom):
    sub, lan = iotas()
    first_lane = lan == 0
    last_lane = lan == NY - 1

    def tile(t, carry):
        rows = pl.ds(pl.multiple_of(t * 8, 8), 8)
        wide = pl.ds(pl.multiple_of(t * 8 + 8, 8), 8)
        q = [grid3(lambda i, j: st[k27(v, i, j), rows, :]) for v in range(3)]
        q = q + [grid3(lambda i, j: bt[i * 3 + j, rows, :])]
        cols = [[project7(q[v][0][j], q[v][1][j], q[v][2][j]) for j in range(3)] for v in range(4)]
        rowm = []
        cell = []
        prev = None
        for a in range(7):
            cell.append([project7(cols[v][0][a], cols[v][1][a], cols[v][2][a]) for v in range(4)])
            hs, ps, rs, bs = cell[a]
            fl = []
            for c in range(7):
                h, p, r = hs[c], ps[c], rs[c]
                h2 = h * h
                y = lax.rsqrt(h2 + DRY2)
                k = h * (y * y)
                u = p * k
                w = r * k
                pr = 0.5 * h2
                ru = r * u
                cc = lax.rsqrt(y)
                fl.append((p * u + pr, ru, r * w + pr, jnp.abs(u) + cc, jnp.abs(w) + cc))
            if a == 0 or a == 6:
                dst, where_ = (c0, rows) if a == 0 else (c6, wide)
                for c in range(7):
                    for n, x in enumerate((hs[c], ps[c], rs[c], bs[c], fl[c][0], fl[c][1], fl[c][3])):
                        dst[n * 7 + c, where_, :] = x
            gy = []
            for c in range(7):
                f = fl[c]
                if c < 6:
                    g = fl[c + 1]
                    hn, pn, rn, f1, f2, sn = hs[c + 1], ps[c + 1], rs[c + 1], g[1], g[2], g[4]
                else:
                    g = fl[0]
                    hn, pn, rn, f1, f2, sn = [down(x) for x in (hs[0], ps[0], rs[0], g[1], g[2], g[4])]
                s = jnp.maximum(f[4], sn)
                gy.append(
                    (
                        (rs[c] + rn) - s * (hn - hs[c]),
                        (f[1] + f1) - s * (pn - ps[c]),
                        (f[2] + f2) - s * (rn - rs[c]),
                    )
                )
            gy[6] = tuple(jnp.where(last_lane, 0.0, x) for x in gy[6])
            gy = [tuple(up1(x) for x in gy[6])] + gy
            b_hi = jnp.where(last_lane, 0.0, down(bs[0]))
            b_lo = jnp.where(first_lane, 0.0, up1(bs[6]))
            bw = [b_lo] + bs + [b_hi]
            ch = [[gy[c][v] - gy[c + 1][v] for c in range(7)] for v in range(3)]
            ch[2] = [ch[2][c] - hs[c] * (bw[c + 2] - bw[c]) for c in range(7)]
            if prev is not None:
                ph, pp, prr, pb, pfl, pch = prev
                for c in range(7):
                    s = jnp.maximum(pfl[c][3], fl[c][3])
                    f = (
                        (pp[c] + ps[c]) - s * (hs[c] - ph[c]),
                        (pfl[c][0] + fl[c][0]) - s * (ps[c] - pp[c]),
                        (pfl[c][1] + fl[c][1]) - s * (rs[c] - prr[c]),
                    )
                    for v in range(3):
                        pch[v][c] = pch[v][c] - f[v]
                        ch[v][c] = ch[v][c] + f[v]
                for c in range(7):
                    bb = bs[c] - cell[a - 2][3][c] if a >= 2 else bs[c]
                    pch[1][c] = pch[1][c] - ph[c] * bb
                rowm.append([moments7(pch[v]) for v in range(3)])
            prev = (hs, ps, rs, bs, fl, ch)
        ch = prev[5]
        ch[1] = [ch[1][c] + cell[6][0][c] * cell[5][3][c] for c in range(7)]
        rowm.append([moments7(ch[v]) for v in range(3)])
        for v in range(3):
            for n in range(3):
                mm = moments7([rowm[a][v][n] for a in range(7)])
                for m in range(3):
                    mom[k27(v, m, n), rows, :] = mm[m]
        return carry

    return tile


def dg_work(n, st, bt, te, tw, dg, fd):
    sub, lan = iotas()
    last_lane = lan == NY - 1
    for k in range(NT):
        te[k, 0:8, :] = jnp.zeros((8, NY), F32)
    for k in range(9):
        fd[k, NX : NX + 8, :] = jnp.zeros((8, NY), F32)

    def dg_tile(t, carry):
        rows = pl.ds(pl.multiple_of(t * 8, 8), 8)
        wide = pl.ds(pl.multiple_of(t * 8 + 8, 8), 8)
        b = grid3(lambda i, j: bt[i * 3 + j, rows, :])
        bx, by = bottom_slopes(b)
        q = [grid3(lambda i, j: st[k27(v, i, j), rows, :]) for v in range(3)]
        lv = predict(q, bx, by)
        acc = volume(lv, bx, by)
        up, lo = traces_x(lv)
        for m in range(3):
            for v in range(3):
                for j in range(3):
                    te[k27(m, v, j), wide, :] = up[m][v][j]
                    tw[k27(m, v, j), rows, :] = lo[m][v][j]
        up, lo = traces_y(lv)
        flo = [[None] * 3 for _ in range(3)]
        fup = [[None] * 3 for _ in range(3)]
        for i in range(3):
            fu = []
            for m in range(3):
                qa = [up[m][v][i] for v in (0, 2, 1)]
                qb = [lo[m][v][i] for v in (0, 2, 1)]
                fb = side_flux(*qb)
                qn = [down(x) for x in qb]
                fn = [qn[1]] + [down(x) for x in fb[1:]]
                fu.append(rusanov2(qa, side_flux(*qa), qn, fn))
            fum = face_mean(fu)
            for s, v in enumerate((0, 2, 1)):
                fup[v][i] = jnp.where(last_lane, 0.0, fum[s])
                flo[v][i] = up1(fup[v][i])
        acc = lift(acc, flo, fup, False, 0.5 / SLOPE)
        for v in range(3):
            for i in range(3):
                for j in range(3):
                    dg[k27(v, i, j), rows, :] = acc[v][i][j]
        return carry

    def x_faces(t, carry):
        rows = pl.ds(pl.multiple_of(t * 8, 8), 8)
        back = pl.ds(t * 8 + 7, 8)
        wall = (sub == 0) & (t == 0)
        for j in range(3):
            f = []
            for m in range(3):
                qa = [te[k27(m, v, j), back, :] for v in range(3)]
                qb = [tw[k27(m, v, j), rows, :] for v in range(3)]
                f.append(rusanov2(qa, side_flux(*qa), qb, side_flux(*qb)))
            f = face_mean(f)
            for v in range(3):
                fd[v * 3 + j, rows, :] = jnp.where(wall, 0.0, f[v])
        return carry

    lax.fori_loop(0, n, dg_tile, 0)
    lax.fori_loop(0, n, x_faces, 0)


def plan():
    z = lax.axis_index("gy") % CHIPS_Z
    dg_n = jnp.where(z == 0, TILES, 0)
    sub_n = jnp.where(z == 0, EARLY_LONG, jnp.where((z == 1) | (z == 3), EARLY_NEAR, 0))
    return dg_n, sub_n


def early_body(st, bt, dg, fd, c6, c0, mom, te, tw):
    dg_n, sub_n = plan()

    @pl.when(dg_n > 0)
    def _():
        dg_work(dg_n, st, bt, te, tw, dg, fd)

    lax.fori_loop(0, sub_n, subcell_tile(st, bt, c6, c0, mom), 0)


def inner_body(st, bt, fg, edg, efd, e6, e0, em, out, c6, c0, mom, fx, dg, fd, te, tw):
    sub, lan = iotas()
    dg_n, sub_n = plan()
    for n in range(9):
        fx[n, NX : NX + 8, :] = jnp.zeros((8, NY), F32)
    for k in range(49):
        c6[k, 0:8, :] = jnp.zeros((8, NY), F32)
        c0[k, NX : NX + 8, :] = jnp.zeros((8, NY), F32)

    @pl.when(dg_n > 0)
    def _():
        def keep_dg(t, carry):
            rows = pl.ds(pl.multiple_of(t * 8, 8), 8)
            for k in range(27):
                dg[k, rows, :] = edg[k, rows, :]
            return carry

        lax.fori_loop(0, TILES, keep_dg, 0)
        fd[...] = efd[...]

    @pl.when(dg_n == 0)
    def _():
        dg_work(TILES, st, bt, te, tw, dg, fd)

    def keep(t, carry):
        rows = pl.ds(pl.multiple_of(t * 8, 8), 8)
        wide = pl.ds(pl.multiple_of(t * 8 + 8, 8), 8)
        for k in range(49):
            c6[k, wide, :] = e6[k, wide, :]
            c0[k, rows, :] = e0[k, rows, :]
        for k in range(27):
            mom[k, rows, :] = em[k, rows, :]
        return carry

    lax.fori_loop(0, sub_n, keep, 0)
    lax.fori_loop(sub_n, TILES, subcell_tile(st, bt, c6, c0, mom), 0)

    def faces(t, carry):
        rows = pl.ds(pl.multiple_of(t * 8, 8), 8)
        back = pl.ds(t * 8 + 7, 8)
        wall = (sub == 0) & (t == 0)
        cs = []
        for c in range(7):
            a = [c6[n * 7 + c, back, :] for n in (0, 1, 2, 4, 5, 6)]
            b = [c0[n * 7 + c, rows, :] for n in (0, 1, 2, 4, 5, 6)]
            cs.append(rusanov2(a[:3], (a[1], a[3], a[4], a[5]), b[:3], (b[1], b[3], b[4], b[5])))
        for v in range(3):
            mm = moments7([cs[c][v] for c in range(7)])
            for n in range(3):
                fx[v * 3 + n, rows, :] = jnp.where(wall, 0.0, mm[n])
        return carry

    lax.fori_loop(0, TILES, faces, 0)

    def finish(t, carry):
        rows = pl.ds(pl.multiple_of(t * 8, 8), 8)
        wide = pl.ds(pl.multiple_of(t * 8 + 8, 8), 8)
        back = pl.ds(t * 8 + 7, 8)
        nxt = pl.ds(t * 8 + 1, 8)
        flag = fg[rows, :] > 0
        acc = [grid3(lambda i, j: dg[k27(v, i, j), rows, :]) for v in range(3)]
        flo = [[fd[v * 3 + j, rows, :] for j in range(3)] for v in range(3)]
        fup = [[fd[v * 3 + j, nxt, :] for j in range(3)] for v in range(3)]
        acc = lift(acc, flo, fup, True, 0.5 / SLOPE)
        mm = [grid3(lambda m, n: mom[k27(v, m, n), rows, :]) for v in range(3)]
        slo = moments7([c0[c, rows, :] * c6[21 + c, back, :] for c in range(7)])
        shi = moments7([c6[c, wide, :] * c0[21 + c, nxt, :] for c in range(7)])
        for v in range(3):
            grid = [[None] * 3 for _ in range(3)]
            for n in range(3):
                lo_ = fx[v * 3 + n, rows, :]
                hi_ = fx[v * 3 + n, nxt, :]
                if v == 1:
                    lo_ = lo_ + slo[n]
                    hi_ = hi_ + shi[n]
                s = lo_ - hi_
                d = lo_ + hi_
                c = nodes_of_moments(mm[v][0][n] + s, mm[v][1][n] - 3.0 * d, mm[v][2][n] + 9.0 * s)
                for i in range(3):
                    grid[i][n] = c[i]
            for i in range(3):
                c = nodes_of_moments(grid[i][0], grid[i][1], grid[i][2])
                for j in range(3):
                    k = k27(v, i, j)
                    out[k, rows, :] = jnp.where(flag, 3.5 * c[j], (SLOPE * W[0]) * acc[v][i][j])
        return carry

    lax.fori_loop(0, TILES, finish, 0)


def edge_body(inc, ax, bx_, ay, by_, rax, rbx, ray, rby, out, own, rec, kx, klo, khi, kz, kt, buf_o, sem):
    sub, lan = iotas()
    ix, iy = lax.axis_index("gx"), lax.axis_index("gy")
    nx, ny = lax.axis_size("gx"), lax.axis_size("gy")
    even_x = ix % 2 == 0
    even_y = iy % 2 == 0
    for buf, a, b, c, d in ((own, ax, bx_, ay, by_), (rec, rax, rbx, ray, rby)):
        a, b, c, d = a[...], b[...], c[...], d[...]
        buf[:, 0, :] = jnp.where(even_x, b, a)
        buf[:, 7, :] = jnp.where(even_x, a, b)
        buf[:, 2, :] = jnp.where(even_y, d, c)
        buf[:, 3, :] = jnp.where(even_y, c, d)
    lower = (sub == 0) | (sub == 2)
    atwall = (
        ((sub == 0) & (ix == 0))
        | ((sub == 7) & (ix == nx - 1))
        | ((sub == 2) & (iy == 0))
        | ((sub == 3) & (iy == ny - 1))
    )
    sg = jnp.where(lower, -1.0, 1.0).astype(F32)
    flag = own[NS - 1] > 0.5

    def other(k):
        return jnp.where(atwall, own[k], rec[k])

    phd = []
    for n in range(3):
        f = []
        for m in range(3):
            qa = [own[k27(m, c, n)] for c in range(3)]
            qb = [other(k27(m, c, n)) for c in range(3)]
            qb[1] = -qb[1]
            f.append(rusanov2(qa, side_flux(*qa), qb, side_flux(*qb)))
        phd.append(face_mean(f))
    ua = [project7(*[own[NT + c * 3 + n] for n in range(3)]) for c in range(3)]
    ub = [project7(*[other(NT + c * 3 + n) for n in range(3)]) for c in range(4)]
    fl = []
    for c in range(7):
        qa = [ua[0][c], ua[1][c], ua[2][c]]
        qb = [ub[0][c], -ub[1][c], ub[2][c]]
        f = rusanov2(qa, side_flux(*qa), qb, side_flux(*qb))
        f[1] = f[1] + qa[0] * ub[3][c]
        fl.append(f)
    phl = [nodes_of_moments(*moments7([fl[c][v] for c in range(7)])) for v in range(3)]
    rq = nodes_of_moments(1.0, 3.0, 9.0)
    for c in range(3):
        for n in range(3):
            vd = phd[n][c]
            vl = phl[c][n]
            if c == 1:
                vd = vd * sg
                vl = vl * sg
            v = (0, 2, 1)[c]
            for k in range(3):
                x = jnp.where(flag, (-3.5 * rq[k]) * vl, (-0.5 * W[0] * UPPER[k] / W[k]) * vd)
                klo[k27(v, n, 2 - k)] = x
                khi[k27(v, n, k)] = x
                kx[k27(c, n, k)] = x
    kz[...] = jnp.zeros((NY, NY), F32)
    kz[pl.ds(0, 27, stride=2), :] = klo[:, 2, :]
    kz[pl.ds(1, 26, stride=2), :] = khi[1:, 3, :]
    kz[NY - 1 : NY, :] = khi[0:1, 3, :]
    kt[...] = kz[...].T
    outer = (lan == 0) | (lan == NY - 1)
    copies = []
    for t in range(TILES):
        rows = slice(t * 8, t * 8 + 8)
        z = kt[rows, :]
        for v in range(3):
            for i in range(3):
                for j in range(3):
                    k = k27(v, i, j)
                    x = inc[k, rows, :] + jnp.where(outer, pltpu.roll(z, NY - 2 * k, 1) if k else z, 0.0)
                    if t == 0:
                        x = x + jnp.where(sub == 0, kx[k27(v, j, 2 - i)], 0.0)
                    if t == TILES - 1:
                        x = x + jnp.where(sub == 7, kx[k27(v, j, i)], 0.0)
                    buf_o[k, rows, :] = x
        cp = pltpu.make_async_copy(buf_o.at[:, pl.ds(t * 8, 8), :], out.at[:, pl.ds(t * 8, 8), :], sem.at[t])
        cp.start()
        copies.append(cp)
    for cp in copies:
        cp.wait()


def swap_first(n):
    return [(i, i ^ 1) for i in range(n)]


def swap_second(nx, ny, axis):
    out = []
    for a in range(nx):
        for b in range(ny):
            i, n = (a, nx) if axis == 0 else (b, ny)
            j = i + 1 if i % 2 else i - 1
            if not 0 <= j < n:
                to = (a, b ^ CHIPS_Z) if axis == 0 else (a ^ 1, b)
            else:
                to = (j, b) if axis == 0 else (a, j)
            out.append((a * ny + b, to[0] * ny + to[1]))
    return out


VM = pl.BlockSpec(memory_space=pltpu.VMEM)
HB = pl.BlockSpec(memory_space=pltpu.HBM)
PARAMS = pltpu.CompilerParams(vmem_limit_bytes=16 * 1024 * 1024)


def planes(n, rows=NX):
    return pltpu.VMEM((n, rows, NY), F32)


def call(body, name, args, outs, scratch, cost, ins=VM, out_spec=VM):
    return pl.pallas_call(
        body,
        out_shape=outs,
        in_specs=[ins] * len(args),
        out_specs=jax.tree.map(lambda _: out_spec, outs),
        scratch_shapes=scratch,
        compiler_params=PARAMS,
        cost_estimate=pl.CostEstimate(flops=cost, transcendentals=0, bytes_accessed=min(cost, 2**20)),
        name=name,
    )(*args)


def shape(*dims, dtype=F32):
    return jax.ShapeDtypeStruct(dims, dtype)


def shards(state, bathymetry, flags):
    full = shape(27, NX, NY)
    edge = shape(NS, NY)
    nx, ny = lax.axis_size("gx"), lax.axis_size("gy")
    st, bt, fg, ax, bx, ay, by = call(
        send_body, "sends",
        tuple(pltpu.with_memory_space_constraint(x, pltpu.HBM)
              for x in (state.reshape(27, NX, NY), bathymetry.reshape(9, NX, NY), flags)),
        (full, shape(9, NX, NY), shape(NX, NY, dtype=jnp.int32), edge, edge, edge, edge),
        [pltpu.VMEM((NY, NY), F32), pltpu.VMEM((NY, NY), F32), planes(37, 8), planes(NS, 8),
         pltpu.SemaphoreType.DMA((3, TILES))],
        2**24, ins=HB,
    )
    ray = lax.ppermute(ay, "gy", swap_first(ny))
    rax = lax.ppermute(ax, "gx", swap_first(nx))
    rbx = lax.ppermute(bx, ("gx", "gy"), swap_second(nx, ny, 0))
    st_, rax = lax.optimization_barrier((st, rax))
    nine = shape(9, NX + 8, NY)
    cells = shape(49, NX + 8, NY)
    part = call(
        early_body, "early", (st_, bt), (full, nine, cells, cells, full), [planes(NT, NX + 8), planes(NT)], 2**30,
    )
    by_, part = lax.optimization_barrier((by, part))
    rby = lax.ppermute(by_, ("gx", "gy"), swap_second(nx, ny, 1))
    inc = call(
        inner_body, "inner", (st, bt, fg) + tuple(part), full,
        [planes(49, NX + 8), planes(49, NX + 8), planes(27), planes(9, NX + 8), planes(27), planes(9, NX + 8),
         planes(NT, NX + 8), planes(NT)],
        2**10,
    )
    out = call(
        edge_body, "edge", (inc, ax, bx, ay, by, rax, rbx, ray, rby), full,
        [planes(NS, 8), planes(NS, 8), planes(27, 8), planes(27, 8), planes(27, 8), pltpu.VMEM((NY, NY), F32),
         pltpu.VMEM((NY, NY), F32), planes(27),
         pltpu.SemaphoreType.DMA((TILES,))],
        2**20, out_spec=HB,
    )
    return out.reshape(3, 3, 3, NX, NY)


def solution(mesh):
    in_specs = (P(None, None, None, "gx", "gy"), P(None, None, "gx", "gy"), P("gx", "gy"))
    out_specs = P(None, None, None, "gx", "gy")
    return jax.shard_map(shards, mesh=mesh, in_specs=in_specs, out_specs=out_specs, check_vma=False)
```

```python
import math

import jax
import jax.numpy as jnp
from jax import lax
from jax.experimental import pallas as pl
from jax.experimental.pallas import tpu as pltpu
from jax.sharding import PartitionSpec as P

GRAV = 1.0
DRY2 = 0.05 * 0.05
COURANT = 0.05
SPREAD = math.sqrt(15.0) / 10.0
NODES = [0.5 - SPREAD, 0.5, 0.5 + SPREAD]
W = [5.0 / 18.0, 8.0 / 18.0, 5.0 / 18.0]


def _terms(k):
    o = [NODES[m] for m in range(3) if m != k]
    return o[0] + o[1], o[0] * o[1], (NODES[k] - o[0]) * (NODES[k] - o[1])


def _value(k, x):
    t = _terms(k)
    return (x * x - t[0] * x + t[1]) / t[2]


def _integral(k, x):
    t = _terms(k)
    return (x * x * x / 3.0 - t[0] * x * x / 2.0 + t[1] * x) / t[2]


UPPER = [_value(k, 1.0) for k in range(3)]
LOWER = [_value(k, 0.0) for k in range(3)]
AT = [[_integral(n, NODES[m]) for n in range(3)] for m in range(3)]
SLOPE = 0.5 / SPREAD
PA = 0.5 / SPREAD / 7.0
PE2 = 0.5 / (SPREAD * SPREAD) / 49.0
PE0 = PE2 / 12.0
_S2, _S4 = 28.0, 196.0
_DET = 7.0 * _S4 - _S2 * _S2


def _restorer():
    b0, b2 = -_S2 / _DET / PE2, 7.0 / _DET / PE2
    m0, m2 = _S4 / _DET - PE0 * b0, -_S2 / _DET - PE0 * b2
    return (m0, m2, m0 + b0 / 2.0, m2 + b2 / 2.0, 0.5 / _S2 / PA)


RM0, RM2, RE0, RE2, RA1 = _restorer()
NX, NY = 32, 128
F32 = jnp.float32


def deriv3(f0, f1, f2):
    a = f2 - f0
    e = f0 + f2
    c = (e + e) - 4.0 * f1
    return a - c, a, a + c


def stiff3(f0, f1, f2):
    a = f2 - f0
    g = f0 + f2 + 1.6 * f1
    a2 = a + a
    return a2 - g, -2.5 * a, a2 + g


def ends3(f0, f1, f2):
    m = (0.5 * (UPPER[0] + UPPER[2])) * (f0 + f2) + UPPER[1] * f1
    n = (0.5 * (UPPER[2] - UPPER[0])) * (f2 - f0)
    return m + n, m - n


def project7(f0, f1, f2):
    b = (f0 + f2) - (f1 + f1)
    x = PE2 * b
    y = PA * (f2 - f0)
    c = f1 + PE0 * b
    y2 = y + y
    y3 = y2 + y
    z1 = c + x
    z2 = c + 4.0 * x
    z3 = c + 9.0 * x
    return [z3 - y3, z2 - y2, z1 - y, c, z1 + y, z2 + y2, z3 + y3]


def project_ends(f0, f1, f2):
    b = (f0 + f2) - (f1 + f1)
    z = f1 + (PE0 + 9.0 * PE2) * b
    y = (3.0 * PA) * (f2 - f0)
    return z - y, z + y


def moments7(c):
    e1, a1 = c[4] + c[2], c[4] - c[2]
    e2, a2 = c[5] + c[1], c[5] - c[1]
    e3, a3 = c[6] + c[0], c[6] - c[0]
    return (
        (c[3] + e1) + (e2 + e3),
        a1 + (a2 + a2) + 3.0 * a3,
        e1 + 4.0 * e2 + 9.0 * e3,
    )


def nodes_of_moments(m0, m1, m2):
    e = RE0 * m0 + RE2 * m2
    a = RA1 * m1
    return e - a, RM0 * m0 + RM2 * m2, e + a


def node_fluxes(h, p, r):
    h2 = h * h
    y = lax.rsqrt(h2 + DRY2)
    k = h * (y * y)
    u = p * k
    pr = 0.5 * h2
    ru = r * u
    return p * u + pr, ru, r * (r * k) + pr


def side_flux(h, n, t):
    h2 = h * h
    y = lax.rsqrt(h2 + DRY2)
    u = n * (h * (y * y))
    return n, n * u + 0.5 * h2, t * u, jnp.abs(u) + lax.rsqrt(y)


def rusanov2(qa, fa, qb, fb):
    s = jnp.maximum(fa[3], fb[3])
    return [(fa[v] + fb[v]) - s * (qb[v] - qa[v]) for v in range(3)]


def grid3(f):
    return [[f(i, j) for j in range(3)] for i in range(3)]


def bottom_slopes(b):
    bx = [[None] * 3 for _ in range(3)]
    by = [[None] * 3 for _ in range(3)]
    for j in range(3):
        d = deriv3(b[0][j], b[1][j], b[2][j])
        for i in range(3):
            bx[i][j] = d[i]
    for i in range(3):
        by[i] = list(deriv3(b[i][0], b[i][1], b[i][2]))
    return bx, by


def rate(q, bx, by):
    fl = grid3(lambda i, j: node_fluxes(q[0][i][j], q[1][i][j], q[2][i][j]))
    pu = grid3(lambda i, j: fl[i][j][0])
    ru = grid3(lambda i, j: fl[i][j][1])
    rv = grid3(lambda i, j: fl[i][j][2])
    out = []
    for fx, gy in ((q[1], q[2]), (pu, ru), (ru, rv)):
        acc = [[None] * 3 for _ in range(3)]
        for j in range(3):
            d = deriv3(fx[0][j], fx[1][j], fx[2][j])
            for i in range(3):
                acc[i][j] = d[i]
        for i in range(3):
            d = deriv3(gy[i][0], gy[i][1], gy[i][2])
            for j in range(3):
                acc[i][j] = acc[i][j] + d[j]
        out.append(acc)
    for i in range(3):
        for j in range(3):
            out[1][i][j] = out[1][i][j] + q[0][i][j] * bx[i][j]
            out[2][i][j] = out[2][i][j] + q[0][i][j] * by[i][j]
    return out


def predict(q0, bx, by):
    f = -COURANT * SLOPE
    r = rate(q0, bx, by)
    lv = [[None] * 3 for _ in range(3)]
    for v in range(3):
        mid = grid3(lambda i, j: q0[v][i][j] + (f * 0.5) * r[v][i][j])
        dif = grid3(lambda i, j: (f * SPREAD) * r[v][i][j])
        lv[0][v] = grid3(lambda i, j: mid[i][j] - dif[i][j])
        lv[1][v] = mid
        lv[2][v] = grid3(lambda i, j: mid[i][j] + dif[i][j])
    ka = f * W[0] / 2.0
    kb = f * W[1] / 2.0
    k1 = f * (AT[1][0] - W[0] / 2.0)
    k2 = f * (AT[0][2] - W[2] / 2.0)
    for _ in range(2):
        rs = [rate(lv[m], bx, by) for m in range(3)]
        new = [[[[None] * 3 for _ in range(3)] for _ in range(3)] for _ in range(3)]
        for v in range(3):
            for i in range(3):
                for j in range(3):
                    r0, r1, r2 = rs[0][v][i][j], rs[1][v][i][j], rs[2][v][i][j]
                    base = q0[v][i][j] + ka * (r0 + r2) + kb * r1
                    c1 = (2.0 * k2) * r1
                    new[0][v][i][j] = base + (c1 + k2 * r2)
                    new[1][v][i][j] = base + k1 * (r0 - r2)
                    new[2][v][i][j] = base - (c1 + k2 * r0)
        lv = new
    return lv


def face_mean(f):
    return [(f[0][v] + f[2][v]) + 1.6 * f[1][v] for v in range(3)]


def volume(lv, bx, by):
    fl = [grid3(lambda i, j: node_fluxes(lv[m][0][i][j], lv[m][1][i][j], lv[m][2][i][j])) for m in range(3)]

    def mean(get):
        return grid3(lambda i, j: (get(0, i, j) + get(2, i, j)) + 1.6 * get(1, i, j))

    hm, pm, rm = [mean(lambda m, i, j: lv[m][v][i][j]) for v in range(3)]
    pu, ru, rv = [mean(lambda m, i, j: fl[m][i][j][c]) for c in range(3)]
    out = []
    for fx, gy in ((pm, rm), (pu, ru), (ru, rv)):
        acc = [[None] * 3 for _ in range(3)]
        for j in range(3):
            d = stiff3(fx[0][j], fx[1][j], fx[2][j])
            for i in range(3):
                acc[i][j] = d[i]
        for i in range(3):
            d = stiff3(gy[i][0], gy[i][1], gy[i][2])
            for j in range(3):
                acc[i][j] = acc[i][j] + d[j]
        out.append(acc)
    for i in range(3):
        for j in range(3):
            out[1][i][j] = out[1][i][j] - hm[i][j] * bx[i][j]
            out[2][i][j] = out[2][i][j] - hm[i][j] * by[i][j]
    return out


def traces_x(lv):
    up = [[[None] * 3 for _ in range(3)] for _ in range(3)]
    lo = [[[None] * 3 for _ in range(3)] for _ in range(3)]
    for m in range(3):
        for v in range(3):
            for j in range(3):
                up[m][v][j], lo[m][v][j] = ends3(lv[m][v][0][j], lv[m][v][1][j], lv[m][v][2][j])
    return up, lo


def traces_y(lv):
    up = [[[None] * 3 for _ in range(3)] for _ in range(3)]
    lo = [[[None] * 3 for _ in range(3)] for _ in range(3)]
    for m in range(3):
        for v in range(3):
            for i in range(3):
                up[m][v][i], lo[m][v][i] = ends3(lv[m][v][i][0], lv[m][v][i][1], lv[m][v][i][2])
    return up, lo


def lift(acc, lo, up, along_x, scale):
    ko = [scale * LOWER[i] / W[i] for i in range(3)]
    for v in range(3):
        for t in range(3):
            d = lo[v][t] - up[v][t]
            c = ko[1] * d
            x = ko[0] * lo[v][t] - ko[2] * up[v][t]
            z = ko[2] * lo[v][t] - ko[0] * up[v][t]
            for n, k in enumerate((x, c, z)):
                if along_x:
                    acc[v][n][t] = acc[v][n][t] + k
                else:
                    acc[v][t][n] = acc[v][t][n] + k
    return acc


NT = 27
NS = 40
TILES = NX // 8
CHIPS_Z = 8
LONG, LONG_END, EARLY_NEAR = (4, 0), (3, 0), 2


def k27(a, b, c):
    return a * 9 + b * 3 + c


def lane(x, k):
    return jnp.broadcast_to(x[:, k : k + 1], (8, NY))


def down(x):
    return pltpu.roll(x, NY - 1, 1)


def up1(x):
    return pltpu.roll(x, 1, 1)


def iotas():
    return (
        lax.broadcasted_iota(jnp.int32, (8, NY), 0),
        lax.broadcasted_iota(jnp.int32, (8, NY), 1),
    )


def send_body(st_h, bt_h, fg_h, st, bt, fg, ax, bx_, ay, by_, sq, kt, pk, sd, sem):
    sub, lan = iotas()

    def copies(t):
        rows = pl.ds(t * 8, 8)
        return [
            pltpu.make_async_copy(h.at[(slice(None),) * n + (rows,)], v.at[(slice(None),) * n + (rows,)], sem.at[k, t])
            for k, (h, v, n) in enumerate(((st_h, st, 1), (bt_h, bt, 1), (fg_h, fg, 0)))
        ]

    for t in range(TILES):
        for c in copies(t):
            c.start()
    sq[NX:, :] = jnp.zeros((NY - NX, NY), F32)
    half = ((lan + 1) & (NY - 1)) >> 1

    def columns(t, carry):
        rows = pl.ds(pl.multiple_of(t * 8, 8), 8)
        for c in copies(t):
            c.wait()
        col = jnp.zeros((8, NY), F32)
        for k in range(37):
            if k < 27:
                x = st[k, rows, :]
            elif k < 36:
                x = bt[k - 27, rows, :]
            else:
                x = fg[rows, :].astype(F32)
            col = jnp.where(half == k, pltpu.roll(x, 2 * k, 1) if k else x, col)
        sq[rows, :] = col
        return carry

    lax.fori_loop(0, TILES, columns, 0)
    for c in range(4):
        for n in range(3):
            to = slice(k27(c, n, 0), k27(c, n, 0) + 3)
            src, o = (st, c * 9) if c < 3 else (bt, 0)
            pk[to, 0, :] = src[o + (2 - n) * 3 : o + (2 - n) * 3 + 3, 0, :]
            pk[to, 7, :] = src[o + n * 3 : o + n * 3 + 3, NX - 1, :]
    pk[36:37, 0, :] = fg[0:1, :].astype(F32)
    pk[36:37, 7, :] = fg[NX - 1 : NX, :].astype(F32)
    kt[...] = sq[...].T
    for c, v in enumerate((0, 2, 1, 3)):
        for n in range(3):
            to = slice(k27(c, n, 0), k27(c, n, 0) + 3)
            pk[to, 2, :] = kt[pl.ds(2 * k27(v, 0, 2 - n), 3, stride=6), :]
            if v == 0 and n == 0:
                pk[0:1, 3, :] = kt[NY - 1 : NY, :]
                pk[1:3, 3, :] = kt[pl.ds(5, 2, stride=6), :]
            else:
                pk[to, 3, :] = kt[pl.ds(2 * k27(v, 0, n) - 1, 3, stride=6), :]
    pk[36:37, 2, :] = kt[72:73, :]
    pk[36:37, 3, :] = kt[71:72, :]
    sg = jnp.where((sub == 0) | (sub == 2), -1.0, 1.0).astype(F32)
    q = [grid3(lambda i, j: pk[k27(c, i, j)]) for c in range(4)]
    q[1] = grid3(lambda i, j: q[1][i][j] * sg)
    bx, by = bottom_slopes(q[3])
    lv = predict(q[:3], bx, by)
    for m in range(3):
        for c in range(3):
            for j in range(3):
                sd[k27(m, c, j)] = ends3(lv[m][c][0][j], lv[m][c][1][j], lv[m][c][2][j])[0]
    for c in range(4):
        for j in range(3):
            sd[NT + c * 3 + j] = project_ends(q[c][0][j], q[c][1][j], q[c][2][j])[1]
    sd[NS - 1] = pk[36]
    even_x = lax.axis_index("gx") % 2 == 0
    even_y = lax.axis_index("gy") % 2 == 0
    for a, b, lo_, up_, even in ((ax, bx_, 0, 7, even_x), (ay, by_, 2, 3, even_y)):
        lo_, up_ = sd[:, lo_, :], sd[:, up_, :]
        a[...] = jnp.where(even, up_, lo_)
        b[...] = jnp.where(even, lo_, up_)


def subcell_tile(st, bt, c6, c0, mom):
    sub, lan = iotas()
    first_lane = lan == 0
    last_lane = lan == NY - 1

    def tile(t, carry):
        rows = pl.ds(pl.multiple_of(t * 8, 8), 8)
        wide = pl.ds(pl.multiple_of(t * 8 + 8, 8), 8)
        q = [grid3(lambda i, j: st[k27(v, i, j), rows, :]) for v in range(3)]
        q = q + [grid3(lambda i, j: bt[i * 3 + j, rows, :])]
        cols = [[project7(q[v][0][j], q[v][1][j], q[v][2][j]) for j in range(3)] for v in range(4)]
        rowm = []
        cell = []
        prev = None
        for a in range(7):
            cell.append([project7(cols[v][0][a], cols[v][1][a], cols[v][2][a]) for v in range(4)])
            hs, ps, rs, bs = cell[a]
            fl = []
            for c in range(7):
                h, p, r = hs[c], ps[c], rs[c]
                h2 = h * h
                y = lax.rsqrt(h2 + DRY2)
                k = h * (y * y)
                u = p * k
                w = r * k
                pr = 0.5 * h2
                ru = r * u
                cc = lax.rsqrt(y)
                fl.append((p * u + pr, ru, r * w + pr, jnp.abs(u) + cc, jnp.abs(w) + cc))
            if a == 0 or a == 6:
                dst, where_ = (c0, rows) if a == 0 else (c6, wide)
                for c in range(7):
                    for n, x in enumerate((hs[c], ps[c], rs[c], bs[c], fl[c][0], fl[c][1], fl[c][3])):
                        dst[n * 7 + c, where_, :] = x
            gy = []
            for c in range(7):
                f = fl[c]
                if c < 6:
                    g = fl[c + 1]
                    hn, pn, rn, f1, f2, sn = hs[c + 1], ps[c + 1], rs[c + 1], g[1], g[2], g[4]
                else:
                    g = fl[0]
                    hn, pn, rn, f1, f2, sn = [down(x) for x in (hs[0], ps[0], rs[0], g[1], g[2], g[4])]
                s = jnp.maximum(f[4], sn)
                gy.append(
                    (
                        (rs[c] + rn) - s * (hn - hs[c]),
                        (f[1] + f1) - s * (pn - ps[c]),
                        (f[2] + f2) - s * (rn - rs[c]),
                    )
                )
            gy[6] = tuple(jnp.where(last_lane, 0.0, x) for x in gy[6])
            gy = [tuple(up1(x) for x in gy[6])] + gy
            b_hi = jnp.where(last_lane, 0.0, down(bs[0]))
            b_lo = jnp.where(first_lane, 0.0, up1(bs[6]))
            bw = [b_lo] + bs + [b_hi]
            ch = [[gy[c][v] - gy[c + 1][v] for c in range(7)] for v in range(3)]
            ch[2] = [ch[2][c] - hs[c] * (bw[c + 2] - bw[c]) for c in range(7)]
            if prev is not None:
                ph, pp, prr, pb, pfl, pch = prev
                for c in range(7):
                    s = jnp.maximum(pfl[c][3], fl[c][3])
                    f = (
                        (pp[c] + ps[c]) - s * (hs[c] - ph[c]),
                        (pfl[c][0] + fl[c][0]) - s * (ps[c] - pp[c]),
                        (pfl[c][1] + fl[c][1]) - s * (rs[c] - prr[c]),
                    )
                    for v in range(3):
                        pch[v][c] = pch[v][c] - f[v]
                        ch[v][c] = ch[v][c] + f[v]
                for c in range(7):
                    bb = bs[c] - cell[a - 2][3][c] if a >= 2 else bs[c]
                    pch[1][c] = pch[1][c] - ph[c] * bb
                rowm.append([moments7(pch[v]) for v in range(3)])
            prev = (hs, ps, rs, bs, fl, ch)
        ch = prev[5]
        ch[1] = [ch[1][c] + cell[6][0][c] * cell[5][3][c] for c in range(7)]
        rowm.append([moments7(ch[v]) for v in range(3)])
        for v in range(3):
            for n in range(3):
                mm = moments7([rowm[a][v][n] for a in range(7)])
                for m in range(3):
                    mom[k27(v, m, n), rows, :] = mm[m]
        return carry

    return tile


def dg_tile_of(st, bt, te, tw, dg):
    sub, lan = iotas()
    last_lane = lan == NY - 1

    def dg_tile(t, carry):
        rows = pl.ds(pl.multiple_of(t * 8, 8), 8)
        wide = pl.ds(pl.multiple_of(t * 8 + 8, 8), 8)
        b = grid3(lambda i, j: bt[i * 3 + j, rows, :])
        bx, by = bottom_slopes(b)
        q = [grid3(lambda i, j: st[k27(v, i, j), rows, :]) for v in range(3)]
        lv = predict(q, bx, by)
        acc = volume(lv, bx, by)
        up, lo = traces_x(lv)
        for m in range(3):
            for v in range(3):
                for j in range(3):
                    te[k27(m, v, j), wide, :] = up[m][v][j]
                    tw[k27(m, v, j), rows, :] = lo[m][v][j]
        up, lo = traces_y(lv)
        flo = [[None] * 3 for _ in range(3)]
        fup = [[None] * 3 for _ in range(3)]
        for i in range(3):
            fu = []
            for m in range(3):
                qa = [up[m][v][i] for v in (0, 2, 1)]
                qb = [lo[m][v][i] for v in (0, 2, 1)]
                fb = side_flux(*qb)
                qn = [down(x) for x in qb]
                fn = [qn[1]] + [down(x) for x in fb[1:]]
                fu.append(rusanov2(qa, side_flux(*qa), qn, fn))
            fum = face_mean(fu)
            for s, v in enumerate((0, 2, 1)):
                fup[v][i] = jnp.where(last_lane, 0.0, fum[s])
                flo[v][i] = up1(fup[v][i])
        acc = lift(acc, flo, fup, False, 0.5 / SLOPE)
        for v in range(3):
            for i in range(3):
                for j in range(3):
                    dg[k27(v, i, j), rows, :] = acc[v][i][j]
        return carry

    return dg_tile


def x_faces_of(te, tw, fd):
    sub, lan = iotas()

    def x_faces(t, carry):
        rows = pl.ds(pl.multiple_of(t * 8, 8), 8)
        back = pl.ds(t * 8 + 7, 8)
        wall = (sub == 0) & (t == 0)
        for j in range(3):
            f = []
            for m in range(3):
                qa = [te[k27(m, v, j), back, :] for v in range(3)]
                qb = [tw[k27(m, v, j), rows, :] for v in range(3)]
                f.append(rusanov2(qa, side_flux(*qa), qb, side_flux(*qb)))
            f = face_mean(f)
            for v in range(3):
                fd[v * 3 + j, rows, :] = jnp.where(wall, 0.0, f[v])
        return carry

    return x_faces


def plan():
    z = lax.axis_index("gy") % CHIPS_Z
    end = (lax.axis_index("gx") == 0) & (lax.axis_index("gy") // CHIPS_Z == 2)
    dg_n = jnp.where(z == 0, jnp.where(end, LONG_END[0], LONG[0]), 0)
    sub_n = jnp.where(z == 0, jnp.where(end, LONG_END[1], LONG[1]), jnp.where((z == 1) | (z == 3), EARLY_NEAR, 0))
    return dg_n, sub_n


def early_body(st, bt, dg, te, tw, c6, c0, mom):
    dg_n, sub_n = plan()
    lax.fori_loop(0, dg_n, dg_tile_of(st, bt, te, tw, dg), 0)
    lax.fori_loop(0, sub_n, subcell_tile(st, bt, c6, c0, mom), 0)


def inner_body(st, bt, fg, edg, ete, etw, e6, e0, em, out, c6, c0, mom, fx, dg, fd, te, tw):
    sub, lan = iotas()
    dg_n, sub_n = plan()
    for n in range(9):
        fx[n, NX : NX + 8, :] = jnp.zeros((8, NY), F32)
    for k in range(49):
        c6[k, 0:8, :] = jnp.zeros((8, NY), F32)
        c0[k, NX : NX + 8, :] = jnp.zeros((8, NY), F32)

    for k in range(NT):
        te[k, 0:8, :] = jnp.zeros((8, NY), F32)
    for k in range(9):
        fd[k, NX : NX + 8, :] = jnp.zeros((8, NY), F32)

    def keep_dg(t, carry):
        rows = pl.ds(pl.multiple_of(t * 8, 8), 8)
        wide = pl.ds(pl.multiple_of(t * 8 + 8, 8), 8)
        for k in range(27):
            dg[k, rows, :] = edg[k, rows, :]
            te[k, wide, :] = ete[k, wide, :]
            tw[k, rows, :] = etw[k, rows, :]
        return carry

    lax.fori_loop(0, dg_n, keep_dg, 0)
    lax.fori_loop(dg_n, TILES, dg_tile_of(st, bt, te, tw, dg), 0)
    lax.fori_loop(0, TILES, x_faces_of(te, tw, fd), 0)

    def keep(t, carry):
        rows = pl.ds(pl.multiple_of(t * 8, 8), 8)
        wide = pl.ds(pl.multiple_of(t * 8 + 8, 8), 8)
        for k in range(49):
            c6[k, wide, :] = e6[k, wide, :]
            c0[k, rows, :] = e0[k, rows, :]
        for k in range(27):
            mom[k, rows, :] = em[k, rows, :]
        return carry

    lax.fori_loop(0, sub_n, keep, 0)
    lax.fori_loop(sub_n, TILES, subcell_tile(st, bt, c6, c0, mom), 0)

    def faces(t, carry):
        rows = pl.ds(pl.multiple_of(t * 8, 8), 8)
        back = pl.ds(t * 8 + 7, 8)
        wall = (sub == 0) & (t == 0)
        cs = []
        for c in range(7):
            a = [c6[n * 7 + c, back, :] for n in (0, 1, 2, 4, 5, 6)]
            b = [c0[n * 7 + c, rows, :] for n in (0, 1, 2, 4, 5, 6)]
            cs.append(rusanov2(a[:3], (a[1], a[3], a[4], a[5]), b[:3], (b[1], b[3], b[4], b[5])))
        for v in range(3):
            mm = moments7([cs[c][v] for c in range(7)])
            for n in range(3):
                fx[v * 3 + n, rows, :] = jnp.where(wall, 0.0, mm[n])
        return carry

    lax.fori_loop(0, TILES, faces, 0)

    def finish(t, carry):
        rows = pl.ds(pl.multiple_of(t * 8, 8), 8)
        wide = pl.ds(pl.multiple_of(t * 8 + 8, 8), 8)
        back = pl.ds(t * 8 + 7, 8)
        nxt = pl.ds(t * 8 + 1, 8)
        flag = fg[rows, :] > 0
        acc = [grid3(lambda i, j: dg[k27(v, i, j), rows, :]) for v in range(3)]
        flo = [[fd[v * 3 + j, rows, :] for j in range(3)] for v in range(3)]
        fup = [[fd[v * 3 + j, nxt, :] for j in range(3)] for v in range(3)]
        acc = lift(acc, flo, fup, True, 0.5 / SLOPE)
        mm = [grid3(lambda m, n: mom[k27(v, m, n), rows, :]) for v in range(3)]
        slo = moments7([c0[c, rows, :] * c6[21 + c, back, :] for c in range(7)])
        shi = moments7([c6[c, wide, :] * c0[21 + c, nxt, :] for c in range(7)])
        for v in range(3):
            grid = [[None] * 3 for _ in range(3)]
            for n in range(3):
                lo_ = fx[v * 3 + n, rows, :]
                hi_ = fx[v * 3 + n, nxt, :]
                if v == 1:
                    lo_ = lo_ + slo[n]
                    hi_ = hi_ + shi[n]
                s = lo_ - hi_
                d = lo_ + hi_
                c = nodes_of_moments(mm[v][0][n] + s, mm[v][1][n] - 3.0 * d, mm[v][2][n] + 9.0 * s)
                for i in range(3):
                    grid[i][n] = c[i]
            for i in range(3):
                c = nodes_of_moments(grid[i][0], grid[i][1], grid[i][2])
                for j in range(3):
                    k = k27(v, i, j)
                    out[k, rows, :] = jnp.where(flag, 3.5 * c[j], (SLOPE * W[0]) * acc[v][i][j])
        return carry

    lax.fori_loop(0, TILES, finish, 0)


def edge_body(inc, ax, bx_, ay, by_, rax, rbx, ray, rby, out, own, rec, kx, klo, khi, kz, kt, buf_o, sem):
    sub, lan = iotas()
    ix, iy = lax.axis_index("gx"), lax.axis_index("gy")
    nx, ny = lax.axis_size("gx"), lax.axis_size("gy")
    even_x = ix % 2 == 0
    even_y = iy % 2 == 0
    for buf, a, b, c, d in ((own, ax, bx_, ay, by_), (rec, rax, rbx, ray, rby)):
        a, b, c, d = a[...], b[...], c[...], d[...]
        buf[:, 0, :] = jnp.where(even_x, b, a)
        buf[:, 7, :] = jnp.where(even_x, a, b)
        buf[:, 2, :] = jnp.where(even_y, d, c)
        buf[:, 3, :] = jnp.where(even_y, c, d)
    lower = (sub == 0) | (sub == 2)
    atwall = (
        ((sub == 0) & (ix == 0))
        | ((sub == 7) & (ix == nx - 1))
        | ((sub == 2) & (iy == 0))
        | ((sub == 3) & (iy == ny - 1))
    )
    sg = jnp.where(lower, -1.0, 1.0).astype(F32)
    flag = own[NS - 1] > 0.5

    def other(k):
        return jnp.where(atwall, own[k], rec[k])

    phd = []
    for n in range(3):
        f = []
        for m in range(3):
            qa = [own[k27(m, c, n)] for c in range(3)]
            qb = [other(k27(m, c, n)) for c in range(3)]
            qb[1] = -qb[1]
            f.append(rusanov2(qa, side_flux(*qa), qb, side_flux(*qb)))
        phd.append(face_mean(f))
    ua = [project7(*[own[NT + c * 3 + n] for n in range(3)]) for c in range(3)]
    ub = [project7(*[other(NT + c * 3 + n) for n in range(3)]) for c in range(4)]
    fl = []
    for c in range(7):
        qa = [ua[0][c], ua[1][c], ua[2][c]]
        qb = [ub[0][c], -ub[1][c], ub[2][c]]
        f = rusanov2(qa, side_flux(*qa), qb, side_flux(*qb))
        f[1] = f[1] + qa[0] * ub[3][c]
        fl.append(f)
    phl = [nodes_of_moments(*moments7([fl[c][v] for c in range(7)])) for v in range(3)]
    rq = nodes_of_moments(1.0, 3.0, 9.0)
    for c in range(3):
        for n in range(3):
            vd = phd[n][c]
            vl = phl[c][n]
            if c == 1:
                vd = vd * sg
                vl = vl * sg
            v = (0, 2, 1)[c]
            for k in range(3):
                x = jnp.where(flag, (-3.5 * rq[k]) * vl, (-0.5 * W[0] * UPPER[k] / W[k]) * vd)
                klo[k27(v, n, 2 - k)] = x
                khi[k27(v, n, k)] = x
                kx[k27(c, n, k)] = x
    kz[...] = jnp.zeros((NY, NY), F32)
    kz[pl.ds(0, 27, stride=2), :] = klo[:, 2, :]
    kz[pl.ds(1, 26, stride=2), :] = khi[1:, 3, :]
    kz[NY - 1 : NY, :] = khi[0:1, 3, :]
    kt[...] = kz[...].T
    outer = (lan == 0) | (lan == NY - 1)
    copies = []
    for t in range(TILES):
        rows = slice(t * 8, t * 8 + 8)
        z = kt[rows, :]
        for v in range(3):
            for i in range(3):
                for j in range(3):
                    k = k27(v, i, j)
                    x = inc[k, rows, :] + jnp.where(outer, pltpu.roll(z, NY - 2 * k, 1) if k else z, 0.0)
                    if t == 0:
                        x = x + jnp.where(sub == 0, kx[k27(v, j, 2 - i)], 0.0)
                    if t == TILES - 1:
                        x = x + jnp.where(sub == 7, kx[k27(v, j, i)], 0.0)
                    buf_o[k, rows, :] = x
        cp = pltpu.make_async_copy(buf_o.at[:, pl.ds(t * 8, 8), :], out.at[:, pl.ds(t * 8, 8), :], sem.at[t])
        cp.start()
        copies.append(cp)
    for cp in copies:
        cp.wait()


def swap_first(n):
    return [(i, i ^ 1) for i in range(n)]


def swap_second(nx, ny, axis):
    out = []
    for a in range(nx):
        for b in range(ny):
            i, n = (a, nx) if axis == 0 else (b, ny)
            j = i + 1 if i % 2 else i - 1
            if not 0 <= j < n:
                to = (a, b ^ CHIPS_Z) if axis == 0 else (a ^ 1, b)
            else:
                to = (j, b) if axis == 0 else (a, j)
            out.append((a * ny + b, to[0] * ny + to[1]))
    return out


VM = pl.BlockSpec(memory_space=pltpu.VMEM)
HB = pl.BlockSpec(memory_space=pltpu.HBM)
PARAMS = pltpu.CompilerParams(vmem_limit_bytes=16 * 1024 * 1024)


def planes(n, rows=NX):
    return pltpu.VMEM((n, rows, NY), F32)


def call(body, name, args, outs, scratch, cost, ins=VM, out_spec=VM):
    return pl.pallas_call(
        body,
        out_shape=outs,
        in_specs=[ins] * len(args),
        out_specs=jax.tree.map(lambda _: out_spec, outs),
        scratch_shapes=scratch,
        compiler_params=PARAMS,
        cost_estimate=pl.CostEstimate(flops=cost, transcendentals=0, bytes_accessed=min(cost, 2**20)),
        name=name,
    )(*args)


def shape(*dims, dtype=F32):
    return jax.ShapeDtypeStruct(dims, dtype)


def shards(state, bathymetry, flags):
    full = shape(27, NX, NY)
    edge = shape(NS, NY)
    nx, ny = lax.axis_size("gx"), lax.axis_size("gy")
    st, bt, fg, ax, bx, ay, by = call(
        send_body, "sends",
        tuple(pltpu.with_memory_space_constraint(x, pltpu.HBM)
              for x in (state.reshape(27, NX, NY), bathymetry.reshape(9, NX, NY), flags)),
        (full, shape(9, NX, NY), shape(NX, NY, dtype=jnp.int32), edge, edge, edge, edge),
        [pltpu.VMEM((NY, NY), F32), pltpu.VMEM((NY, NY), F32), planes(37, 8), planes(NS, 8),
         pltpu.SemaphoreType.DMA((3, TILES))],
        2**24, ins=HB,
    )
    ray = lax.ppermute(ay, "gy", swap_first(ny))
    rax = lax.ppermute(ax, "gx", swap_first(nx))
    rbx = lax.ppermute(bx, ("gx", "gy"), swap_second(nx, ny, 0))
    st_, rax = lax.optimization_barrier((st, rax))
    cells = shape(49, NX + 8, NY)
    part = call(
        early_body, "early", (st_, bt), (full, shape(NT, NX + 8, NY), full, cells, cells, full), [], 2**30,
    )
    by_, part = lax.optimization_barrier((by, part))
    rby = lax.ppermute(by_, ("gx", "gy"), swap_second(nx, ny, 1))
    inc = call(
        inner_body, "inner", (st, bt, fg) + tuple(part), full,
        [planes(49, NX + 8), planes(49, NX + 8), planes(27), planes(9, NX + 8), planes(27), planes(9, NX + 8),
         planes(NT, NX + 8), planes(NT)],
        2**10,
    )
    out = call(
        edge_body, "edge", (inc, ax, bx, ay, by, rax, rbx, ray, rby), full,
        [planes(NS, 8), planes(NS, 8), planes(27, 8), planes(27, 8), planes(27, 8), pltpu.VMEM((NY, NY), F32),
         pltpu.VMEM((NY, NY), F32), planes(27),
         pltpu.SemaphoreType.DMA((TILES,))],
        2**20, out_spec=HB,
    )
    return out.reshape(3, 3, 3, NX, NY)


def solution(mesh):
    in_specs = (P(None, None, None, "gx", "gy"), P(None, None, "gx", "gy"), P("gx", "gy"))
    out_specs = P(None, None, None, "gx", "gy")
    return jax.shard_map(shards, mesh=mesh, in_specs=in_specs, out_specs=out_specs, check_vma=False)
```

```python
import math

import jax
import jax.numpy as jnp
from jax import lax
from jax.experimental import pallas as pl
from jax.experimental.pallas import tpu as pltpu
from jax.sharding import PartitionSpec as P

GRAV = 1.0
DRY2 = 0.05 * 0.05
COURANT = 0.05
SPREAD = math.sqrt(15.0) / 10.0
NODES = [0.5 - SPREAD, 0.5, 0.5 + SPREAD]
W = [5.0 / 18.0, 8.0 / 18.0, 5.0 / 18.0]


def _terms(k):
    o = [NODES[m] for m in range(3) if m != k]
    return o[0] + o[1], o[0] * o[1], (NODES[k] - o[0]) * (NODES[k] - o[1])


def _value(k, x):
    t = _terms(k)
    return (x * x - t[0] * x + t[1]) / t[2]


def _integral(k, x):
    t = _terms(k)
    return (x * x * x / 3.0 - t[0] * x * x / 2.0 + t[1] * x) / t[2]


UPPER = [_value(k, 1.0) for k in range(3)]
LOWER = [_value(k, 0.0) for k in range(3)]
AT = [[_integral(n, NODES[m]) for n in range(3)] for m in range(3)]
SLOPE = 0.5 / SPREAD
PA = 0.5 / SPREAD / 7.0
PE2 = 0.5 / (SPREAD * SPREAD) / 49.0
PE0 = PE2 / 12.0
_S2, _S4 = 28.0, 196.0
_DET = 7.0 * _S4 - _S2 * _S2


def _restorer():
    b0, b2 = -_S2 / _DET / PE2, 7.0 / _DET / PE2
    m0, m2 = _S4 / _DET - PE0 * b0, -_S2 / _DET - PE0 * b2
    return (m0, m2, m0 + b0 / 2.0, m2 + b2 / 2.0, 0.5 / _S2 / PA)


RM0, RM2, RE0, RE2, RA1 = _restorer()
NX, NY = 32, 128
F32 = jnp.float32


def deriv3(f0, f1, f2):
    a = f2 - f0
    e = f0 + f2
    c = (e + e) - 4.0 * f1
    return a - c, a, a + c


def stiff3(f0, f1, f2):
    a = f2 - f0
    g = f0 + f2 + 1.6 * f1
    a2 = a + a
    return a2 - g, -2.5 * a, a2 + g


def ends3(f0, f1, f2):
    m = (0.5 * (UPPER[0] + UPPER[2])) * (f0 + f2) + UPPER[1] * f1
    n = (0.5 * (UPPER[2] - UPPER[0])) * (f2 - f0)
    return m + n, m - n


def project7(f0, f1, f2):
    b = (f0 + f2) - (f1 + f1)
    x = PE2 * b
    y = PA * (f2 - f0)
    c = f1 + PE0 * b
    y2 = y + y
    y3 = y2 + y
    z1 = c + x
    z2 = c + 4.0 * x
    z3 = c + 9.0 * x
    return [z3 - y3, z2 - y2, z1 - y, c, z1 + y, z2 + y2, z3 + y3]


def project_ends(f0, f1, f2):
    b = (f0 + f2) - (f1 + f1)
    z = f1 + (PE0 + 9.0 * PE2) * b
    y = (3.0 * PA) * (f2 - f0)
    return z - y, z + y


def moments7(c):
    e1, a1 = c[4] + c[2], c[4] - c[2]
    e2, a2 = c[5] + c[1], c[5] - c[1]
    e3, a3 = c[6] + c[0], c[6] - c[0]
    return (
        (c[3] + e1) + (e2 + e3),
        a1 + (a2 + a2) + 3.0 * a3,
        e1 + 4.0 * e2 + 9.0 * e3,
    )


def nodes_of_moments(m0, m1, m2):
    e = RE0 * m0 + RE2 * m2
    a = RA1 * m1
    return e - a, RM0 * m0 + RM2 * m2, e + a


def node_fluxes(h, p, r):
    h2 = h * h
    y = lax.rsqrt(h2 + DRY2)
    k = h * (y * y)
    u = p * k
    pr = 0.5 * h2
    ru = r * u
    return p * u + pr, ru, r * (r * k) + pr


def side_flux(h, n, t):
    h2 = h * h
    y = lax.rsqrt(h2 + DRY2)
    u = n * (h * (y * y))
    return n, n * u + 0.5 * h2, t * u, jnp.abs(u) + lax.rsqrt(y)


def rusanov2(qa, fa, qb, fb):
    s = jnp.maximum(fa[3], fb[3])
    return [(fa[v] + fb[v]) - s * (qb[v] - qa[v]) for v in range(3)]


def grid3(f):
    return [[f(i, j) for j in range(3)] for i in range(3)]


def bottom_slopes(b):
    bx = [[None] * 3 for _ in range(3)]
    by = [[None] * 3 for _ in range(3)]
    for j in range(3):
        d = deriv3(b[0][j], b[1][j], b[2][j])
        for i in range(3):
            bx[i][j] = d[i]
    for i in range(3):
        by[i] = list(deriv3(b[i][0], b[i][1], b[i][2]))
    return bx, by


def rate(q, bx, by):
    fl = grid3(lambda i, j: node_fluxes(q[0][i][j], q[1][i][j], q[2][i][j]))
    pu = grid3(lambda i, j: fl[i][j][0])
    ru = grid3(lambda i, j: fl[i][j][1])
    rv = grid3(lambda i, j: fl[i][j][2])
    out = []
    for fx, gy in ((q[1], q[2]), (pu, ru), (ru, rv)):
        acc = [[None] * 3 for _ in range(3)]
        for j in range(3):
            d = deriv3(fx[0][j], fx[1][j], fx[2][j])
            for i in range(3):
                acc[i][j] = d[i]
        for i in range(3):
            d = deriv3(gy[i][0], gy[i][1], gy[i][2])
            for j in range(3):
                acc[i][j] = acc[i][j] + d[j]
        out.append(acc)
    for i in range(3):
        for j in range(3):
            out[1][i][j] = out[1][i][j] + q[0][i][j] * bx[i][j]
            out[2][i][j] = out[2][i][j] + q[0][i][j] * by[i][j]
    return out


def predict(q0, bx, by):
    f = -COURANT * SLOPE
    r = rate(q0, bx, by)
    lv = [[None] * 3 for _ in range(3)]
    for v in range(3):
        mid = grid3(lambda i, j: q0[v][i][j] + (f * 0.5) * r[v][i][j])
        dif = grid3(lambda i, j: (f * SPREAD) * r[v][i][j])
        lv[0][v] = grid3(lambda i, j: mid[i][j] - dif[i][j])
        lv[1][v] = mid
        lv[2][v] = grid3(lambda i, j: mid[i][j] + dif[i][j])
    ka = f * W[0] / 2.0
    kb = f * W[1] / 2.0
    k1 = f * (AT[1][0] - W[0] / 2.0)
    k2 = f * (AT[0][2] - W[2] / 2.0)
    for _ in range(2):
        rs = [rate(lv[m], bx, by) for m in range(3)]
        new = [[[[None] * 3 for _ in range(3)] for _ in range(3)] for _ in range(3)]
        for v in range(3):
            for i in range(3):
                for j in range(3):
                    r0, r1, r2 = rs[0][v][i][j], rs[1][v][i][j], rs[2][v][i][j]
                    base = q0[v][i][j] + ka * (r0 + r2) + kb * r1
                    c1 = (2.0 * k2) * r1
                    new[0][v][i][j] = base + (c1 + k2 * r2)
                    new[1][v][i][j] = base + k1 * (r0 - r2)
                    new[2][v][i][j] = base - (c1 + k2 * r0)
        lv = new
    return lv


def face_mean(f):
    return [(f[0][v] + f[2][v]) + 1.6 * f[1][v] for v in range(3)]


def volume(lv, bx, by):
    fl = [grid3(lambda i, j: node_fluxes(lv[m][0][i][j], lv[m][1][i][j], lv[m][2][i][j])) for m in range(3)]

    def mean(get):
        return grid3(lambda i, j: (get(0, i, j) + get(2, i, j)) + 1.6 * get(1, i, j))

    hm, pm, rm = [mean(lambda m, i, j: lv[m][v][i][j]) for v in range(3)]
    pu, ru, rv = [mean(lambda m, i, j: fl[m][i][j][c]) for c in range(3)]
    out = []
    for fx, gy in ((pm, rm), (pu, ru), (ru, rv)):
        acc = [[None] * 3 for _ in range(3)]
        for j in range(3):
            d = stiff3(fx[0][j], fx[1][j], fx[2][j])
            for i in range(3):
                acc[i][j] = d[i]
        for i in range(3):
            d = stiff3(gy[i][0], gy[i][1], gy[i][2])
            for j in range(3):
                acc[i][j] = acc[i][j] + d[j]
        out.append(acc)
    for i in range(3):
        for j in range(3):
            out[1][i][j] = out[1][i][j] - hm[i][j] * bx[i][j]
            out[2][i][j] = out[2][i][j] - hm[i][j] * by[i][j]
    return out


def traces_x(lv):
    up = [[[None] * 3 for _ in range(3)] for _ in range(3)]
    lo = [[[None] * 3 for _ in range(3)] for _ in range(3)]
    for m in range(3):
        for v in range(3):
            for j in range(3):
                up[m][v][j], lo[m][v][j] = ends3(lv[m][v][0][j], lv[m][v][1][j], lv[m][v][2][j])
    return up, lo


def traces_y(lv):
    up = [[[None] * 3 for _ in range(3)] for _ in range(3)]
    lo = [[[None] * 3 for _ in range(3)] for _ in range(3)]
    for m in range(3):
        for v in range(3):
            for i in range(3):
                up[m][v][i], lo[m][v][i] = ends3(lv[m][v][i][0], lv[m][v][i][1], lv[m][v][i][2])
    return up, lo


def lift(acc, lo, up, along_x, scale):
    ko = [scale * LOWER[i] / W[i] for i in range(3)]
    for v in range(3):
        for t in range(3):
            d = lo[v][t] - up[v][t]
            c = ko[1] * d
            x = ko[0] * lo[v][t] - ko[2] * up[v][t]
            z = ko[2] * lo[v][t] - ko[0] * up[v][t]
            for n, k in enumerate((x, c, z)):
                if along_x:
                    acc[v][n][t] = acc[v][n][t] + k
                else:
                    acc[v][t][n] = acc[v][t][n] + k
    return acc


NT = 27
NS = 40
TILES = NX // 8
CHIPS_Z = 8
LONG, LONG_END, EARLY_NEAR, FIRST = (4, 0), (3, 0), 2, 1


def k27(a, b, c):
    return a * 9 + b * 3 + c


def lane(x, k):
    return jnp.broadcast_to(x[:, k : k + 1], (8, NY))


def down(x):
    return pltpu.roll(x, NY - 1, 1)


def up1(x):
    return pltpu.roll(x, 1, 1)


def iotas():
    return (
        lax.broadcasted_iota(jnp.int32, (8, NY), 0),
        lax.broadcasted_iota(jnp.int32, (8, NY), 1),
    )


def send_body(st_h, bt_h, fg_h, st, bt, fg, ax, bx_, ay, by_, dg, te, tw, sq, kt, pk, sd, sem):
    sub, lan = iotas()

    def copies(t):
        rows = pl.ds(t * 8, 8)
        return [
            pltpu.make_async_copy(h.at[(slice(None),) * n + (rows,)], v.at[(slice(None),) * n + (rows,)], sem.at[k, t])
            for k, (h, v, n) in enumerate(((st_h, st, 1), (bt_h, bt, 1), (fg_h, fg, 0)))
        ]

    for t in range(TILES):
        for c in copies(t):
            c.start()
    sq[NX:, :] = jnp.zeros((NY - NX, NY), F32)
    half = ((lan + 1) & (NY - 1)) >> 1

    def columns(t, carry):
        rows = pl.ds(pl.multiple_of(t * 8, 8), 8)
        for c in copies(t):
            c.wait()
        col = jnp.zeros((8, NY), F32)
        for k in range(37):
            if k < 27:
                x = st[k, rows, :]
            elif k < 36:
                x = bt[k - 27, rows, :]
            else:
                x = fg[rows, :].astype(F32)
            col = jnp.where(half == k, pltpu.roll(x, 2 * k, 1) if k else x, col)
        sq[rows, :] = col
        return carry

    lax.fori_loop(0, TILES, columns, 0)
    for c in range(4):
        for n in range(3):
            to = slice(k27(c, n, 0), k27(c, n, 0) + 3)
            src, o = (st, c * 9) if c < 3 else (bt, 0)
            pk[to, 0, :] = src[o + (2 - n) * 3 : o + (2 - n) * 3 + 3, 0, :]
            pk[to, 7, :] = src[o + n * 3 : o + n * 3 + 3, NX - 1, :]
    pk[36:37, 0, :] = fg[0:1, :].astype(F32)
    pk[36:37, 7, :] = fg[NX - 1 : NX, :].astype(F32)
    kt[...] = sq[...].T
    for c, v in enumerate((0, 2, 1, 3)):
        for n in range(3):
            to = slice(k27(c, n, 0), k27(c, n, 0) + 3)
            pk[to, 2, :] = kt[pl.ds(2 * k27(v, 0, 2 - n), 3, stride=6), :]
            if v == 0 and n == 0:
                pk[0:1, 3, :] = kt[NY - 1 : NY, :]
                pk[1:3, 3, :] = kt[pl.ds(5, 2, stride=6), :]
            else:
                pk[to, 3, :] = kt[pl.ds(2 * k27(v, 0, n) - 1, 3, stride=6), :]
    pk[36:37, 2, :] = kt[72:73, :]
    pk[36:37, 3, :] = kt[71:72, :]
    sg = jnp.where((sub == 0) | (sub == 2), -1.0, 1.0).astype(F32)
    q = [grid3(lambda i, j: pk[k27(c, i, j)]) for c in range(4)]
    q[1] = grid3(lambda i, j: q[1][i][j] * sg)
    bx, by = bottom_slopes(q[3])
    lv = predict(q[:3], bx, by)
    for m in range(3):
        for c in range(3):
            for j in range(3):
                sd[k27(m, c, j)] = ends3(lv[m][c][0][j], lv[m][c][1][j], lv[m][c][2][j])[0]
    for c in range(4):
        for j in range(3):
            sd[NT + c * 3 + j] = project_ends(q[c][0][j], q[c][1][j], q[c][2][j])[1]
    sd[NS - 1] = pk[36]
    even_x = lax.axis_index("gx") % 2 == 0
    even_y = lax.axis_index("gy") % 2 == 0
    for a, b, lo_, up_, even in ((ax, bx_, 0, 7, even_x), (ay, by_, 2, 3, even_y)):
        lo_, up_ = sd[:, lo_, :], sd[:, up_, :]
        a[...] = jnp.where(even, up_, lo_)
        b[...] = jnp.where(even, lo_, up_)
    lax.fori_loop(0, first_n(), dg_tile_of(st, bt, te, tw, dg), 0)


def subcell_tile(st, bt, c6, c0, mom):
    sub, lan = iotas()
    first_lane = lan == 0
    last_lane = lan == NY - 1

    def tile(t, carry):
        rows = pl.ds(pl.multiple_of(t * 8, 8), 8)
        wide = pl.ds(pl.multiple_of(t * 8 + 8, 8), 8)
        q = [grid3(lambda i, j: st[k27(v, i, j), rows, :]) for v in range(3)]
        q = q + [grid3(lambda i, j: bt[i * 3 + j, rows, :])]
        cols = [[project7(q[v][0][j], q[v][1][j], q[v][2][j]) for j in range(3)] for v in range(4)]
        rowm = []
        cell = []
        prev = None
        for a in range(7):
            cell.append([project7(cols[v][0][a], cols[v][1][a], cols[v][2][a]) for v in range(4)])
            hs, ps, rs, bs = cell[a]
            fl = []
            for c in range(7):
                h, p, r = hs[c], ps[c], rs[c]
                h2 = h * h
                y = lax.rsqrt(h2 + DRY2)
                k = h * (y * y)
                u = p * k
                w = r * k
                pr = 0.5 * h2
                ru = r * u
                cc = lax.rsqrt(y)
                fl.append((p * u + pr, ru, r * w + pr, jnp.abs(u) + cc, jnp.abs(w) + cc))
            if a == 0 or a == 6:
                dst, where_ = (c0, rows) if a == 0 else (c6, wide)
                for c in range(7):
                    for n, x in enumerate((hs[c], ps[c], rs[c], bs[c], fl[c][0], fl[c][1], fl[c][3])):
                        dst[n * 7 + c, where_, :] = x
            gy = []
            for c in range(7):
                f = fl[c]
                if c < 6:
                    g = fl[c + 1]
                    hn, pn, rn, f1, f2, sn = hs[c + 1], ps[c + 1], rs[c + 1], g[1], g[2], g[4]
                else:
                    g = fl[0]
                    hn, pn, rn, f1, f2, sn = [down(x) for x in (hs[0], ps[0], rs[0], g[1], g[2], g[4])]
                s = jnp.maximum(f[4], sn)
                gy.append(
                    (
                        (rs[c] + rn) - s * (hn - hs[c]),
                        (f[1] + f1) - s * (pn - ps[c]),
                        (f[2] + f2) - s * (rn - rs[c]),
                    )
                )
            gy[6] = tuple(jnp.where(last_lane, 0.0, x) for x in gy[6])
            gy = [tuple(up1(x) for x in gy[6])] + gy
            b_hi = jnp.where(last_lane, 0.0, down(bs[0]))
            b_lo = jnp.where(first_lane, 0.0, up1(bs[6]))
            bw = [b_lo] + bs + [b_hi]
            ch = [[gy[c][v] - gy[c + 1][v] for c in range(7)] for v in range(3)]
            ch[2] = [ch[2][c] - hs[c] * (bw[c + 2] - bw[c]) for c in range(7)]
            if prev is not None:
                ph, pp, prr, pb, pfl, pch = prev
                for c in range(7):
                    s = jnp.maximum(pfl[c][3], fl[c][3])
                    f = (
                        (pp[c] + ps[c]) - s * (hs[c] - ph[c]),
                        (pfl[c][0] + fl[c][0]) - s * (ps[c] - pp[c]),
                        (pfl[c][1] + fl[c][1]) - s * (rs[c] - prr[c]),
                    )
                    for v in range(3):
                        pch[v][c] = pch[v][c] - f[v]
                        ch[v][c] = ch[v][c] + f[v]
                for c in range(7):
                    bb = bs[c] - cell[a - 2][3][c] if a >= 2 else bs[c]
                    pch[1][c] = pch[1][c] - ph[c] * bb
                rowm.append([moments7(pch[v]) for v in range(3)])
            prev = (hs, ps, rs, bs, fl, ch)
        ch = prev[5]
        ch[1] = [ch[1][c] + cell[6][0][c] * cell[5][3][c] for c in range(7)]
        rowm.append([moments7(ch[v]) for v in range(3)])
        for v in range(3):
            for n in range(3):
                mm = moments7([rowm[a][v][n] for a in range(7)])
                for m in range(3):
                    mom[k27(v, m, n), rows, :] = mm[m]
        return carry

    return tile


def dg_tile_of(st, bt, te, tw, dg):
    sub, lan = iotas()
    last_lane = lan == NY - 1

    def dg_tile(t, carry):
        rows = pl.ds(pl.multiple_of(t * 8, 8), 8)
        wide = pl.ds(pl.multiple_of(t * 8 + 8, 8), 8)
        b = grid3(lambda i, j: bt[i * 3 + j, rows, :])
        bx, by = bottom_slopes(b)
        q = [grid3(lambda i, j: st[k27(v, i, j), rows, :]) for v in range(3)]
        lv = predict(q, bx, by)
        acc = volume(lv, bx, by)
        up, lo = traces_x(lv)
        for m in range(3):
            for v in range(3):
                for j in range(3):
                    te[k27(m, v, j), wide, :] = up[m][v][j]
                    tw[k27(m, v, j), rows, :] = lo[m][v][j]
        up, lo = traces_y(lv)
        flo = [[None] * 3 for _ in range(3)]
        fup = [[None] * 3 for _ in range(3)]
        for i in range(3):
            fu = []
            for m in range(3):
                qa = [up[m][v][i] for v in (0, 2, 1)]
                qb = [lo[m][v][i] for v in (0, 2, 1)]
                fb = side_flux(*qb)
                qn = [down(x) for x in qb]
                fn = [qn[1]] + [down(x) for x in fb[1:]]
                fu.append(rusanov2(qa, side_flux(*qa), qn, fn))
            fum = face_mean(fu)
            for s, v in enumerate((0, 2, 1)):
                fup[v][i] = jnp.where(last_lane, 0.0, fum[s])
                flo[v][i] = up1(fup[v][i])
        acc = lift(acc, flo, fup, False, 0.5 / SLOPE)
        for v in range(3):
            for i in range(3):
                for j in range(3):
                    dg[k27(v, i, j), rows, :] = acc[v][i][j]
        return carry

    return dg_tile


def x_faces_of(te, tw, fd):
    sub, lan = iotas()

    def x_faces(t, carry):
        rows = pl.ds(pl.multiple_of(t * 8, 8), 8)
        back = pl.ds(t * 8 + 7, 8)
        wall = (sub == 0) & (t == 0)
        for j in range(3):
            f = []
            for m in range(3):
                qa = [te[k27(m, v, j), back, :] for v in range(3)]
                qb = [tw[k27(m, v, j), rows, :] for v in range(3)]
                f.append(rusanov2(qa, side_flux(*qa), qb, side_flux(*qb)))
            f = face_mean(f)
            for v in range(3):
                fd[v * 3 + j, rows, :] = jnp.where(wall, 0.0, f[v])
        return carry

    return x_faces


def plan():
    z = lax.axis_index("gy") % CHIPS_Z
    end = (lax.axis_index("gx") == 0) & (lax.axis_index("gy") // CHIPS_Z == 2)
    dg_n = jnp.where(z == 0, jnp.where(end, LONG_END[0], LONG[0]), 0)
    sub_n = jnp.where(z == 0, jnp.where(end, LONG_END[1], lax.axis_index("gx") % 2), jnp.where((z == 1) | (z == 3), EARLY_NEAR, 0))
    return dg_n, sub_n


def first_n():
    return jnp.where(lax.axis_index("gy") % CHIPS_Z == 0, FIRST, 0)


def early_body(st, bt, dg, te, tw, c6, c0, mom):
    dg_n, sub_n = plan()
    lax.fori_loop(first_n(), dg_n, dg_tile_of(st, bt, te, tw, dg), 0)
    lax.fori_loop(0, sub_n, subcell_tile(st, bt, c6, c0, mom), 0)


def inner_body(st, bt, fg, adg, ate, atw, edg, ete, etw, e6, e0, em, c6, c0, mom, fx, dg, fd, te, tw):
    sub, lan = iotas()
    dg_n, sub_n = plan()
    for n in range(9):
        fx[n, NX : NX + 8, :] = jnp.zeros((8, NY), F32)
    for k in range(21, 28):
        c6[k, 0:8, :] = jnp.zeros((8, NY), F32)
        c0[k, NX : NX + 8, :] = jnp.zeros((8, NY), F32)

    for k in range(9):
        fd[k, NX : NX + 8, :] = jnp.zeros((8, NY), F32)

    def keep_dg(fdg, fte, ftw):
        def copy(t, carry):
            rows = pl.ds(pl.multiple_of(t * 8, 8), 8)
            wide = pl.ds(pl.multiple_of(t * 8 + 8, 8), 8)
            for k in range(27):
                dg[k, rows, :] = fdg[k, rows, :]
                te[k, wide, :] = fte[k, wide, :]
                tw[k, rows, :] = ftw[k, rows, :]
            return carry

        return copy

    lax.fori_loop(0, first_n(), keep_dg(adg, ate, atw), 0)
    lax.fori_loop(first_n(), dg_n, keep_dg(edg, ete, etw), 0)
    lax.fori_loop(dg_n, TILES, dg_tile_of(st, bt, te, tw, dg), 0)
    lax.fori_loop(0, TILES, x_faces_of(te, tw, fd), 0)

    def keep(t, carry):
        rows = pl.ds(pl.multiple_of(t * 8, 8), 8)
        wide = pl.ds(pl.multiple_of(t * 8 + 8, 8), 8)
        for k in range(49):
            c6[k, wide, :] = e6[k, wide, :]
            c0[k, rows, :] = e0[k, rows, :]
        for k in range(27):
            mom[k, rows, :] = em[k, rows, :]
        return carry

    lax.fori_loop(0, sub_n, keep, 0)
    lax.fori_loop(sub_n, TILES, subcell_tile(st, bt, c6, c0, mom), 0)

    def faces(t, carry):
        rows = pl.ds(pl.multiple_of(t * 8, 8), 8)
        back = pl.ds(t * 8 + 7, 8)
        wall = (sub == 0) & (t == 0)
        cs = []
        for c in range(7):
            a = [c6[n * 7 + c, back, :] for n in (0, 1, 2, 4, 5, 6)]
            b = [c0[n * 7 + c, rows, :] for n in (0, 1, 2, 4, 5, 6)]
            cs.append(rusanov2(a[:3], (a[1], a[3], a[4], a[5]), b[:3], (b[1], b[3], b[4], b[5])))
        for v in range(3):
            mm = moments7([cs[c][v] for c in range(7)])
            for n in range(3):
                fx[v * 3 + n, rows, :] = jnp.where(wall, 0.0, mm[n])
        return carry

    lax.fori_loop(0, TILES, faces, 0)


def edge_body(fg, c6, c0, mom, fx, dg, fd, ax, bx_, ay, by_, rax, rbx, ray, rby, out, own, rec, kx, klo, khi, kz, kt, buf_o, sem):
    sub, lan = iotas()
    ix, iy = lax.axis_index("gx"), lax.axis_index("gy")
    nx, ny = lax.axis_size("gx"), lax.axis_size("gy")
    even_x = ix % 2 == 0
    even_y = iy % 2 == 0
    for buf, a, b, c, d in ((own, ax, bx_, ay, by_), (rec, rax, rbx, ray, rby)):
        a, b, c, d = a[...], b[...], c[...], d[...]
        buf[:, 0, :] = jnp.where(even_x, b, a)
        buf[:, 7, :] = jnp.where(even_x, a, b)
        buf[:, 2, :] = jnp.where(even_y, d, c)
        buf[:, 3, :] = jnp.where(even_y, c, d)
    lower = (sub == 0) | (sub == 2)
    atwall = (
        ((sub == 0) & (ix == 0))
        | ((sub == 7) & (ix == nx - 1))
        | ((sub == 2) & (iy == 0))
        | ((sub == 3) & (iy == ny - 1))
    )
    sg = jnp.where(lower, -1.0, 1.0).astype(F32)
    flag = own[NS - 1] > 0.5

    def other(k):
        return jnp.where(atwall, own[k], rec[k])

    phd = []
    for n in range(3):
        f = []
        for m in range(3):
            qa = [own[k27(m, c, n)] for c in range(3)]
            qb = [other(k27(m, c, n)) for c in range(3)]
            qb[1] = -qb[1]
            f.append(rusanov2(qa, side_flux(*qa), qb, side_flux(*qb)))
        phd.append(face_mean(f))
    ua = [project7(*[own[NT + c * 3 + n] for n in range(3)]) for c in range(3)]
    ub = [project7(*[other(NT + c * 3 + n) for n in range(3)]) for c in range(4)]
    fl = []
    for c in range(7):
        qa = [ua[0][c], ua[1][c], ua[2][c]]
        qb = [ub[0][c], -ub[1][c], ub[2][c]]
        f = rusanov2(qa, side_flux(*qa), qb, side_flux(*qb))
        f[1] = f[1] + qa[0] * ub[3][c]
        fl.append(f)
    phl = [nodes_of_moments(*moments7([fl[c][v] for c in range(7)])) for v in range(3)]
    rq = nodes_of_moments(1.0, 3.0, 9.0)
    for c in range(3):
        for n in range(3):
            vd = phd[n][c]
            vl = phl[c][n]
            if c == 1:
                vd = vd * sg
                vl = vl * sg
            v = (0, 2, 1)[c]
            for k in range(3):
                x = jnp.where(flag, (-3.5 * rq[k]) * vl, (-0.5 * W[0] * UPPER[k] / W[k]) * vd)
                klo[k27(v, n, 2 - k)] = x
                khi[k27(v, n, k)] = x
                kx[k27(c, n, k)] = x
    kz[...] = jnp.zeros((NY, NY), F32)
    kz[pl.ds(0, 27, stride=2), :] = klo[:, 2, :]
    kz[pl.ds(1, 26, stride=2), :] = khi[1:, 3, :]
    kz[NY - 1 : NY, :] = khi[0:1, 3, :]
    kt[...] = kz[...].T
    outer = (lan == 0) | (lan == NY - 1)
    copies = []
    for t in range(TILES):
        rows = slice(t * 8, t * 8 + 8)
        wide = slice(t * 8 + 8, t * 8 + 16)
        back = slice(t * 8 + 7, t * 8 + 15)
        nxt = slice(t * 8 + 1, t * 8 + 9)
        z = kt[rows, :]
        flag_t = fg[rows, :] > 0
        acc = [grid3(lambda i, j: dg[k27(v, i, j), rows, :]) for v in range(3)]
        flo = [[fd[v * 3 + j, rows, :] for j in range(3)] for v in range(3)]
        fup = [[fd[v * 3 + j, nxt, :] for j in range(3)] for v in range(3)]
        acc = lift(acc, flo, fup, True, 0.5 / SLOPE)
        mm = [grid3(lambda m, n: mom[k27(v, m, n), rows, :]) for v in range(3)]
        slo = moments7([c0[c, rows, :] * c6[21 + c, back, :] for c in range(7)])
        shi = moments7([c6[c, wide, :] * c0[21 + c, nxt, :] for c in range(7)])
        for v in range(3):
            grid = [[None] * 3 for _ in range(3)]
            for n in range(3):
                lo_ = fx[v * 3 + n, rows, :]
                hi_ = fx[v * 3 + n, nxt, :]
                if v == 1:
                    lo_ = lo_ + slo[n]
                    hi_ = hi_ + shi[n]
                s = lo_ - hi_
                d = lo_ + hi_
                c = nodes_of_moments(mm[v][0][n] + s, mm[v][1][n] - 3.0 * d, mm[v][2][n] + 9.0 * s)
                for i in range(3):
                    grid[i][n] = c[i]
            for i in range(3):
                c = nodes_of_moments(grid[i][0], grid[i][1], grid[i][2])
                for j in range(3):
                    k = k27(v, i, j)
                    x = jnp.where(flag_t, 3.5 * c[j], (SLOPE * W[0]) * acc[v][i][j])
                    x = x + jnp.where(outer, pltpu.roll(z, NY - 2 * k, 1) if k else z, 0.0)
                    if t == 0:
                        x = x + jnp.where(sub == 0, kx[k27(v, j, 2 - i)], 0.0)
                    if t == TILES - 1:
                        x = x + jnp.where(sub == 7, kx[k27(v, j, i)], 0.0)
                    buf_o[k, rows, :] = x
        cp = pltpu.make_async_copy(buf_o.at[:, pl.ds(t * 8, 8), :], out.at[:, pl.ds(t * 8, 8), :], sem.at[t])
        cp.start()
        copies.append(cp)
    for cp in copies:
        cp.wait()


def swap_first(n):
    return [(i, i ^ 1) for i in range(n)]


def swap_second(nx, ny, axis):
    out = []
    for a in range(nx):
        for b in range(ny):
            i, n = (a, nx) if axis == 0 else (b, ny)
            j = i + 1 if i % 2 else i - 1
            if not 0 <= j < n:
                to = (a, b ^ CHIPS_Z) if axis == 0 else (a ^ 1, b)
            else:
                to = (j, b) if axis == 0 else (a, j)
            out.append((a * ny + b, to[0] * ny + to[1]))
    return out


VM = pl.BlockSpec(memory_space=pltpu.VMEM)
HB = pl.BlockSpec(memory_space=pltpu.HBM)
PARAMS = pltpu.CompilerParams(vmem_limit_bytes=16 * 1024 * 1024)


def planes(n, rows=NX):
    return pltpu.VMEM((n, rows, NY), F32)


def call(body, name, args, outs, scratch, cost, ins=VM, out_spec=VM):
    return pl.pallas_call(
        body,
        out_shape=outs,
        in_specs=[ins] * len(args),
        out_specs=jax.tree.map(lambda _: out_spec, outs),
        scratch_shapes=scratch,
        compiler_params=PARAMS,
        cost_estimate=pl.CostEstimate(flops=cost, transcendentals=0, bytes_accessed=min(cost, 2**20)),
        name=name,
    )(*args)


def shape(*dims, dtype=F32):
    return jax.ShapeDtypeStruct(dims, dtype)


def shards(state, bathymetry, flags):
    full = shape(27, NX, NY)
    edge = shape(NS, NY)
    nx, ny = lax.axis_size("gx"), lax.axis_size("gy")
    sides = (full, shape(NT, NX + 8, NY), full)
    st, bt, fg, ax, bx, ay, by, *first = call(
        send_body, "sends",
        tuple(pltpu.with_memory_space_constraint(x, pltpu.HBM)
              for x in (state.reshape(27, NX, NY), bathymetry.reshape(9, NX, NY), flags)),
        (full, shape(9, NX, NY), shape(NX, NY, dtype=jnp.int32), edge, edge, edge, edge) + sides,
        [pltpu.VMEM((NY, NY), F32), pltpu.VMEM((NY, NY), F32), planes(37, 8), planes(NS, 8),
         pltpu.SemaphoreType.DMA((3, TILES))],
        2**24, ins=HB,
    )
    ray = lax.ppermute(ay, "gy", swap_first(ny))
    rax = lax.ppermute(ax, "gx", swap_first(nx))
    rbx = lax.ppermute(bx, ("gx", "gy"), swap_second(nx, ny, 0))
    st_, rax = lax.optimization_barrier((st, rax))
    cells = shape(49, NX + 8, NY)
    part = call(early_body, "early", (st_, bt), sides + (cells, cells, full), [], 2**30)
    by_, part = lax.optimization_barrier((by, part))
    rby = lax.ppermute(by_, ("gx", "gy"), swap_second(nx, ny, 1))
    nine = shape(9, NX + 8, NY)
    pieces = call(
        inner_body, "inner", (st, bt, fg) + tuple(first) + tuple(part),
        (cells, cells, full, nine, full, nine), [planes(NT, NX + 8), planes(NT)], 2**10,
    )
    out = call(
        edge_body, "edge", (fg, *pieces, ax, bx, ay, by, rax, rbx, ray, rby), full,
        [planes(NS, 8), planes(NS, 8), planes(27, 8), planes(27, 8), planes(27, 8), pltpu.VMEM((NY, NY), F32),
         pltpu.VMEM((NY, NY), F32), planes(27),
         pltpu.SemaphoreType.DMA((TILES,))],
        2**20, out_spec=HB,
    )
    return out.reshape(3, 3, 3, NX, NY)


def solution(mesh):
    in_specs = (P(None, None, None, "gx", "gy"), P(None, None, "gx", "gy"), P("gx", "gy"))
    out_specs = P(None, None, None, "gx", "gy")
    return jax.shard_map(shards, mesh=mesh, in_specs=in_specs, out_specs=out_specs, check_vma=False)
```

```python
import math

import jax
import jax.numpy as jnp
from jax import lax
from jax.experimental import pallas as pl
from jax.experimental.pallas import tpu as pltpu
from jax.sharding import PartitionSpec as P

GRAV = 1.0
DRY2 = 0.05 * 0.05
COURANT = 0.05
SPREAD = math.sqrt(15.0) / 10.0
NODES = [0.5 - SPREAD, 0.5, 0.5 + SPREAD]
W = [5.0 / 18.0, 8.0 / 18.0, 5.0 / 18.0]


def _terms(k):
    o = [NODES[m] for m in range(3) if m != k]
    return o[0] + o[1], o[0] * o[1], (NODES[k] - o[0]) * (NODES[k] - o[1])


def _value(k, x):
    t = _terms(k)
    return (x * x - t[0] * x + t[1]) / t[2]


def _integral(k, x):
    t = _terms(k)
    return (x * x * x / 3.0 - t[0] * x * x / 2.0 + t[1] * x) / t[2]


UPPER = [_value(k, 1.0) for k in range(3)]
LOWER = [_value(k, 0.0) for k in range(3)]
AT = [[_integral(n, NODES[m]) for n in range(3)] for m in range(3)]
SLOPE = 0.5 / SPREAD
PA = 0.5 / SPREAD / 7.0
PE2 = 0.5 / (SPREAD * SPREAD) / 49.0
PE0 = PE2 / 12.0
_S2, _S4 = 28.0, 196.0
_DET = 7.0 * _S4 - _S2 * _S2


def _restorer():
    b0, b2 = -_S2 / _DET / PE2, 7.0 / _DET / PE2
    m0, m2 = _S4 / _DET - PE0 * b0, -_S2 / _DET - PE0 * b2
    return (m0, m2, m0 + b0 / 2.0, m2 + b2 / 2.0, 0.5 / _S2 / PA)


RM0, RM2, RE0, RE2, RA1 = _restorer()
NX, NY = 32, 128
F32 = jnp.float32


def deriv3(f0, f1, f2):
    a = f2 - f0
    e = f0 + f2
    c = (e + e) - 4.0 * f1
    return a - c, a, a + c


def stiff3(f0, f1, f2):
    a = f2 - f0
    g = f0 + f2 + 1.6 * f1
    a2 = a + a
    return a2 - g, -2.5 * a, a2 + g


def ends3(f0, f1, f2):
    m = (0.5 * (UPPER[0] + UPPER[2])) * (f0 + f2) + UPPER[1] * f1
    n = (0.5 * (UPPER[2] - UPPER[0])) * (f2 - f0)
    return m + n, m - n


def project7(f0, f1, f2):
    b = (f0 + f2) - (f1 + f1)
    x = PE2 * b
    y = PA * (f2 - f0)
    c = f1 + PE0 * b
    y2 = y + y
    y3 = y2 + y
    z1 = c + x
    z2 = c + 4.0 * x
    z3 = c + 9.0 * x
    return [z3 - y3, z2 - y2, z1 - y, c, z1 + y, z2 + y2, z3 + y3]


def project_ends(f0, f1, f2):
    b = (f0 + f2) - (f1 + f1)
    z = f1 + (PE0 + 9.0 * PE2) * b
    y = (3.0 * PA) * (f2 - f0)
    return z - y, z + y


def moments7(c):
    e1, a1 = c[4] + c[2], c[4] - c[2]
    e2, a2 = c[5] + c[1], c[5] - c[1]
    e3, a3 = c[6] + c[0], c[6] - c[0]
    return (
        (c[3] + e1) + (e2 + e3),
        a1 + (a2 + a2) + 3.0 * a3,
        e1 + 4.0 * e2 + 9.0 * e3,
    )


def nodes_of_moments(m0, m1, m2):
    e = RE0 * m0 + RE2 * m2
    a = RA1 * m1
    return e - a, RM0 * m0 + RM2 * m2, e + a


def node_fluxes(h, p, r):
    h2 = h * h
    y = lax.rsqrt(h2 + DRY2)
    k = h * (y * y)
    u = p * k
    pr = 0.5 * h2
    ru = r * u
    return p * u + pr, ru, r * (r * k) + pr


def side_flux(h, n, t):
    h2 = h * h
    y = lax.rsqrt(h2 + DRY2)
    u = n * (h * (y * y))
    return n, n * u + 0.5 * h2, t * u, jnp.abs(u) + lax.rsqrt(y)


def rusanov2(qa, fa, qb, fb):
    s = jnp.maximum(fa[3], fb[3])
    return [(fa[v] + fb[v]) - s * (qb[v] - qa[v]) for v in range(3)]


def grid3(f):
    return [[f(i, j) for j in range(3)] for i in range(3)]


def bottom_slopes(b):
    bx = [[None] * 3 for _ in range(3)]
    by = [[None] * 3 for _ in range(3)]
    for j in range(3):
        d = deriv3(b[0][j], b[1][j], b[2][j])
        for i in range(3):
            bx[i][j] = d[i]
    for i in range(3):
        by[i] = list(deriv3(b[i][0], b[i][1], b[i][2]))
    return bx, by


def rate(q, bx, by):
    fl = grid3(lambda i, j: node_fluxes(q[0][i][j], q[1][i][j], q[2][i][j]))
    pu = grid3(lambda i, j: fl[i][j][0])
    ru = grid3(lambda i, j: fl[i][j][1])
    rv = grid3(lambda i, j: fl[i][j][2])
    out = []
    for fx, gy in ((q[1], q[2]), (pu, ru), (ru, rv)):
        acc = [[None] * 3 for _ in range(3)]
        for j in range(3):
            d = deriv3(fx[0][j], fx[1][j], fx[2][j])
            for i in range(3):
                acc[i][j] = d[i]
        for i in range(3):
            d = deriv3(gy[i][0], gy[i][1], gy[i][2])
            for j in range(3):
                acc[i][j] = acc[i][j] + d[j]
        out.append(acc)
    for i in range(3):
        for j in range(3):
            out[1][i][j] = out[1][i][j] + q[0][i][j] * bx[i][j]
            out[2][i][j] = out[2][i][j] + q[0][i][j] * by[i][j]
    return out


def upper3(f0, f1, f2):
    return (UPPER[0] * f0 + UPPER[2] * f2) + UPPER[1] * f1


def predict(q0, bx, by, end_only=False):
    f = -COURANT * SLOPE
    r = rate(q0, bx, by)
    lv = [[None] * 3 for _ in range(3)]
    for v in range(3):
        mid = grid3(lambda i, j: q0[v][i][j] + (f * 0.5) * r[v][i][j])
        dif = grid3(lambda i, j: (f * SPREAD) * r[v][i][j])
        lv[0][v] = grid3(lambda i, j: mid[i][j] - dif[i][j])
        lv[1][v] = mid
        lv[2][v] = grid3(lambda i, j: mid[i][j] + dif[i][j])
    ka = f * W[0] / 2.0
    kb = f * W[1] / 2.0
    k1 = f * (AT[1][0] - W[0] / 2.0)
    k2 = f * (AT[0][2] - W[2] / 2.0)
    for sweep in range(2):
        rs = [rate(lv[m], bx, by) for m in range(3)]
        nodes = 3
        if end_only and sweep == 1:
            nodes = 1
            q0 = [[[upper3(*[q[i][j] for i in range(3)]) for j in range(3)]] for q in q0]
            rs = [[[[upper3(*[r[i][j] for i in range(3)]) for j in range(3)]] for r in rr] for rr in rs]
        new = [[[[None] * 3 for _ in range(3)] for _ in range(3)] for _ in range(3)]
        for v in range(3):
            for i in range(nodes):
                for j in range(3):
                    r0, r1, r2 = rs[0][v][i][j], rs[1][v][i][j], rs[2][v][i][j]
                    base = q0[v][i][j] + ka * (r0 + r2) + kb * r1
                    c1 = (2.0 * k2) * r1
                    new[0][v][i][j] = base + (c1 + k2 * r2)
                    new[1][v][i][j] = base + k1 * (r0 - r2)
                    new[2][v][i][j] = base - (c1 + k2 * r0)
        lv = new
    return lv


def face_mean(f):
    return [(f[0][v] + f[2][v]) + 1.6 * f[1][v] for v in range(3)]


def volume(lv, bx, by):
    fl = [grid3(lambda i, j: node_fluxes(lv[m][0][i][j], lv[m][1][i][j], lv[m][2][i][j])) for m in range(3)]

    def mean(get):
        return grid3(lambda i, j: (get(0, i, j) + get(2, i, j)) + 1.6 * get(1, i, j))

    hm, pm, rm = [mean(lambda m, i, j: lv[m][v][i][j]) for v in range(3)]
    pu, ru, rv = [mean(lambda m, i, j: fl[m][i][j][c]) for c in range(3)]
    out = []
    for fx, gy in ((pm, rm), (pu, ru), (ru, rv)):
        acc = [[None] * 3 for _ in range(3)]
        for j in range(3):
            d = stiff3(fx[0][j], fx[1][j], fx[2][j])
            for i in range(3):
                acc[i][j] = d[i]
        for i in range(3):
            d = stiff3(gy[i][0], gy[i][1], gy[i][2])
            for j in range(3):
                acc[i][j] = acc[i][j] + d[j]
        out.append(acc)
    for i in range(3):
        for j in range(3):
            out[1][i][j] = out[1][i][j] - hm[i][j] * bx[i][j]
            out[2][i][j] = out[2][i][j] - hm[i][j] * by[i][j]
    return out


def traces_x(lv):
    up = [[[None] * 3 for _ in range(3)] for _ in range(3)]
    lo = [[[None] * 3 for _ in range(3)] for _ in range(3)]
    for m in range(3):
        for v in range(3):
            for j in range(3):
                up[m][v][j], lo[m][v][j] = ends3(lv[m][v][0][j], lv[m][v][1][j], lv[m][v][2][j])
    return up, lo


def traces_y(lv):
    up = [[[None] * 3 for _ in range(3)] for _ in range(3)]
    lo = [[[None] * 3 for _ in range(3)] for _ in range(3)]
    for m in range(3):
        for v in range(3):
            for i in range(3):
                up[m][v][i], lo[m][v][i] = ends3(lv[m][v][i][0], lv[m][v][i][1], lv[m][v][i][2])
    return up, lo


def lift(acc, lo, up, along_x, scale):
    ko = [scale * LOWER[i] / W[i] for i in range(3)]
    for v in range(3):
        for t in range(3):
            d = lo[v][t] - up[v][t]
            c = ko[1] * d
            x = ko[0] * lo[v][t] - ko[2] * up[v][t]
            z = ko[2] * lo[v][t] - ko[0] * up[v][t]
            for n, k in enumerate((x, c, z)):
                if along_x:
                    acc[v][n][t] = acc[v][n][t] + k
                else:
                    acc[v][t][n] = acc[v][t][n] + k
    return acc


NT = 27
NS = 40
TILES = NX // 8
CHIPS_Z = 8
LONG, LONG_END, EARLY_NEAR, FIRST = (4, 0), (3, 0), 2, 1


def k27(a, b, c):
    return a * 9 + b * 3 + c


def lane(x, k):
    return jnp.broadcast_to(x[:, k : k + 1], (8, NY))


def down(x):
    return pltpu.roll(x, NY - 1, 1)


def up1(x):
    return pltpu.roll(x, 1, 1)


def iotas():
    return (
        lax.broadcasted_iota(jnp.int32, (8, NY), 0),
        lax.broadcasted_iota(jnp.int32, (8, NY), 1),
    )


def send_body(st_h, bt_h, fg_h, st, bt, fg, ax, bx_, ay, by_, dg, te, tw, sq, kt, pk, sd, sem):
    sub, lan = iotas()

    def copies(t):
        rows = pl.ds(t * 8, 8)
        return [
            pltpu.make_async_copy(h.at[(slice(None),) * n + (rows,)], v.at[(slice(None),) * n + (rows,)], sem.at[k, t])
            for k, (h, v, n) in enumerate(((st_h, st, 1), (bt_h, bt, 1), (fg_h, fg, 0)))
        ]

    for t in range(TILES):
        for c in copies(t):
            c.start()
    sq[NX:, :] = jnp.zeros((NY - NX, NY), F32)
    half = ((lan + 1) & (NY - 1)) >> 1

    def columns(t, carry):
        rows = pl.ds(pl.multiple_of(t * 8, 8), 8)
        for c in copies(t):
            c.wait()
        col = jnp.zeros((8, NY), F32)
        for k in range(37):
            if k < 27:
                x = st[k, rows, :]
            elif k < 36:
                x = bt[k - 27, rows, :]
            else:
                x = fg[rows, :].astype(F32)
            col = jnp.where(half == k, pltpu.roll(x, 2 * k, 1) if k else x, col)
        sq[rows, :] = col
        return carry

    lax.fori_loop(0, TILES, columns, 0)
    for c in range(4):
        for n in range(3):
            to = slice(k27(c, n, 0), k27(c, n, 0) + 3)
            src, o = (st, c * 9) if c < 3 else (bt, 0)
            pk[to, 0, :] = src[o + (2 - n) * 3 : o + (2 - n) * 3 + 3, 0, :]
            pk[to, 7, :] = src[o + n * 3 : o + n * 3 + 3, NX - 1, :]
    pk[36:37, 0, :] = fg[0:1, :].astype(F32)
    pk[36:37, 7, :] = fg[NX - 1 : NX, :].astype(F32)
    kt[...] = sq[...].T
    for c, v in enumerate((0, 2, 1, 3)):
        for n in range(3):
            to = slice(k27(c, n, 0), k27(c, n, 0) + 3)
            pk[to, 2, :] = kt[pl.ds(2 * k27(v, 0, 2 - n), 3, stride=6), :]
            if v == 0 and n == 0:
                pk[0:1, 3, :] = kt[NY - 1 : NY, :]
                pk[1:3, 3, :] = kt[pl.ds(5, 2, stride=6), :]
            else:
                pk[to, 3, :] = kt[pl.ds(2 * k27(v, 0, n) - 1, 3, stride=6), :]
    pk[36:37, 2, :] = kt[72:73, :]
    pk[36:37, 3, :] = kt[71:72, :]
    sg = jnp.where((sub == 0) | (sub == 2), -1.0, 1.0).astype(F32)
    q = [grid3(lambda i, j: pk[k27(c, i, j)]) for c in range(4)]
    q[1] = grid3(lambda i, j: q[1][i][j] * sg)
    bx, by = bottom_slopes(q[3])
    lv = predict(q[:3], bx, by, True)
    for m in range(3):
        for c in range(3):
            for j in range(3):
                sd[k27(m, c, j)] = lv[m][c][0][j]
    for c in range(4):
        for j in range(3):
            sd[NT + c * 3 + j] = project_ends(q[c][0][j], q[c][1][j], q[c][2][j])[1]
    sd[NS - 1] = pk[36]
    even_x = lax.axis_index("gx") % 2 == 0
    even_y = lax.axis_index("gy") % 2 == 0
    for a, b, lo_, up_, even in ((ax, bx_, 0, 7, even_x), (ay, by_, 2, 3, even_y)):
        lo_, up_ = sd[:, lo_, :], sd[:, up_, :]
        a[...] = jnp.where(even, up_, lo_)
        b[...] = jnp.where(even, lo_, up_)
    lax.fori_loop(0, first_n(), dg_tile_of(st, bt, te, tw, dg), 0)


def subcell_tile(st, bt, c6, c0, mom):
    sub, lan = iotas()
    first_lane = lan == 0
    last_lane = lan == NY - 1

    def tile(t, carry):
        rows = pl.ds(pl.multiple_of(t * 8, 8), 8)
        wide = pl.ds(pl.multiple_of(t * 8 + 8, 8), 8)
        q = [grid3(lambda i, j: st[k27(v, i, j), rows, :]) for v in range(3)]
        q = q + [grid3(lambda i, j: bt[i * 3 + j, rows, :])]
        cols = [[project7(q[v][0][j], q[v][1][j], q[v][2][j]) for j in range(3)] for v in range(4)]
        rowm = []
        cell = []
        prev = None
        for a in range(7):
            cell.append([project7(cols[v][0][a], cols[v][1][a], cols[v][2][a]) for v in range(4)])
            hs, ps, rs, bs = cell[a]
            fl = []
            for c in range(7):
                h, p, r = hs[c], ps[c], rs[c]
                h2 = h * h
                y = lax.rsqrt(h2 + DRY2)
                k = h * (y * y)
                u = p * k
                w = r * k
                pr = 0.5 * h2
                ru = r * u
                cc = lax.rsqrt(y)
                fl.append((p * u + pr, ru, r * w + pr, jnp.abs(u) + cc, jnp.abs(w) + cc))
            if a == 0 or a == 6:
                dst, where_ = (c0, rows) if a == 0 else (c6, wide)
                for c in range(7):
                    for n, x in enumerate((hs[c], ps[c], rs[c], bs[c], fl[c][0], fl[c][1], fl[c][3])):
                        dst[n * 7 + c, where_, :] = x
            gy = []
            for c in range(7):
                f = fl[c]
                if c < 6:
                    g = fl[c + 1]
                    hn, pn, rn, f1, f2, sn = hs[c + 1], ps[c + 1], rs[c + 1], g[1], g[2], g[4]
                else:
                    g = fl[0]
                    hn, pn, rn, f1, f2, sn = [down(x) for x in (hs[0], ps[0], rs[0], g[1], g[2], g[4])]
                s = jnp.maximum(f[4], sn)
                gy.append(
                    (
                        (rs[c] + rn) - s * (hn - hs[c]),
                        (f[1] + f1) - s * (pn - ps[c]),
                        (f[2] + f2) - s * (rn - rs[c]),
                    )
                )
            gy[6] = tuple(jnp.where(last_lane, 0.0, x) for x in gy[6])
            gy = [tuple(up1(x) for x in gy[6])] + gy
            b_hi = jnp.where(last_lane, 0.0, down(bs[0]))
            b_lo = jnp.where(first_lane, 0.0, up1(bs[6]))
            bw = [b_lo] + bs + [b_hi]
            ch = [[gy[c][v] - gy[c + 1][v] for c in range(7)] for v in range(3)]
            ch[2] = [ch[2][c] - hs[c] * (bw[c + 2] - bw[c]) for c in range(7)]
            if prev is not None:
                ph, pp, prr, pb, pfl, pch = prev
                for c in range(7):
                    s = jnp.maximum(pfl[c][3], fl[c][3])
                    f = (
                        (pp[c] + ps[c]) - s * (hs[c] - ph[c]),
                        (pfl[c][0] + fl[c][0]) - s * (ps[c] - pp[c]),
                        (pfl[c][1] + fl[c][1]) - s * (rs[c] - prr[c]),
                    )
                    for v in range(3):
                        pch[v][c] = pch[v][c] - f[v]
                        ch[v][c] = ch[v][c] + f[v]
                for c in range(7):
                    bb = bs[c] - cell[a - 2][3][c] if a >= 2 else bs[c]
                    pch[1][c] = pch[1][c] - ph[c] * bb
                rowm.append([moments7(pch[v]) for v in range(3)])
            prev = (hs, ps, rs, bs, fl, ch)
        ch = prev[5]
        ch[1] = [ch[1][c] + cell[6][0][c] * cell[5][3][c] for c in range(7)]
        rowm.append([moments7(ch[v]) for v in range(3)])
        for v in range(3):
            for n in range(3):
                mm = moments7([rowm[a][v][n] for a in range(7)])
                for m in range(3):
                    mom[k27(v, m, n), rows, :] = mm[m]
        return carry

    return tile


def dg_tile_of(st, bt, te, tw, dg):
    sub, lan = iotas()
    last_lane = lan == NY - 1

    def dg_tile(t, carry):
        rows = pl.ds(pl.multiple_of(t * 8, 8), 8)
        wide = pl.ds(pl.multiple_of(t * 8 + 8, 8), 8)
        b = grid3(lambda i, j: bt[i * 3 + j, rows, :])
        bx, by = bottom_slopes(b)
        q = [grid3(lambda i, j: st[k27(v, i, j), rows, :]) for v in range(3)]
        lv = predict(q, bx, by)
        acc = volume(lv, bx, by)
        up, lo = traces_x(lv)
        for m in range(3):
            for v in range(3):
                for j in range(3):
                    te[k27(m, v, j), wide, :] = up[m][v][j]
                    tw[k27(m, v, j), rows, :] = lo[m][v][j]
        up, lo = traces_y(lv)
        flo = [[None] * 3 for _ in range(3)]
        fup = [[None] * 3 for _ in range(3)]
        for i in range(3):
            fu = []
            for m in range(3):
                qa = [up[m][v][i] for v in (0, 2, 1)]
                qb = [lo[m][v][i] for v in (0, 2, 1)]
                fb = side_flux(*qb)
                qn = [down(x) for x in qb]
                fn = [qn[1]] + [down(x) for x in fb[1:]]
                fu.append(rusanov2(qa, side_flux(*qa), qn, fn))
            fum = face_mean(fu)
            for s, v in enumerate((0, 2, 1)):
                fup[v][i] = jnp.where(last_lane, 0.0, fum[s])
                flo[v][i] = up1(fup[v][i])
        acc = lift(acc, flo, fup, False, 0.5 / SLOPE)
        for v in range(3):
            for i in range(3):
                for j in range(3):
                    dg[k27(v, i, j), rows, :] = acc[v][i][j]
        return carry

    return dg_tile


def x_faces_of(te, tw, fd):
    sub, lan = iotas()

    def x_faces(t, carry):
        rows = pl.ds(pl.multiple_of(t * 8, 8), 8)
        back = pl.ds(t * 8 + 7, 8)
        wall = (sub == 0) & (t == 0)
        for j in range(3):
            f = []
            for m in range(3):
                qa = [te[k27(m, v, j), back, :] for v in range(3)]
                qb = [tw[k27(m, v, j), rows, :] for v in range(3)]
                f.append(rusanov2(qa, side_flux(*qa), qb, side_flux(*qb)))
            f = face_mean(f)
            for v in range(3):
                fd[v * 3 + j, rows, :] = jnp.where(wall, 0.0, f[v])
        return carry

    return x_faces


def plan():
    z = lax.axis_index("gy") % CHIPS_Z
    end = (lax.axis_index("gx") == 0) & (lax.axis_index("gy") // CHIPS_Z == 2)
    dg_n = jnp.where(z == 0, jnp.where(end, LONG_END[0], LONG[0]), 0)
    sub_n = jnp.where(z == 0, jnp.where(end, LONG_END[1], lax.axis_index("gx") % 2), jnp.where((z == 1) | (z == 3), EARLY_NEAR, 0))
    return dg_n, sub_n


def first_n():
    return jnp.where(lax.axis_index("gy") % CHIPS_Z == 0, FIRST, 0)


def early_body(st, bt, dg, te, tw, c6, c0, mom):
    dg_n, sub_n = plan()
    lax.fori_loop(first_n(), dg_n, dg_tile_of(st, bt, te, tw, dg), 0)
    lax.fori_loop(0, sub_n, subcell_tile(st, bt, c6, c0, mom), 0)


def inner_body(st, bt, fg, adg, ate, atw, edg, ete, etw, e6, e0, em, c6, c0, mom, fx, dg, fd, te, tw):
    sub, lan = iotas()
    dg_n, sub_n = plan()
    for n in range(9):
        fx[n, NX : NX + 8, :] = jnp.zeros((8, NY), F32)
    for k in range(21, 28):
        c6[k, 0:8, :] = jnp.zeros((8, NY), F32)
        c0[k, NX : NX + 8, :] = jnp.zeros((8, NY), F32)

    for k in range(9):
        fd[k, NX : NX + 8, :] = jnp.zeros((8, NY), F32)

    def keep_dg(fdg, fte, ftw):
        def copy(t, carry):
            rows = pl.ds(pl.multiple_of(t * 8, 8), 8)
            wide = pl.ds(pl.multiple_of(t * 8 + 8, 8), 8)
            for k in range(27):
                dg[k, rows, :] = fdg[k, rows, :]
                te[k, wide, :] = fte[k, wide, :]
                tw[k, rows, :] = ftw[k, rows, :]
            return carry

        return copy

    lax.fori_loop(0, first_n(), keep_dg(adg, ate, atw), 0)
    lax.fori_loop(first_n(), dg_n, keep_dg(edg, ete, etw), 0)
    lax.fori_loop(dg_n, TILES, dg_tile_of(st, bt, te, tw, dg), 0)
    lax.fori_loop(0, TILES, x_faces_of(te, tw, fd), 0)

    def keep(t, carry):
        rows = pl.ds(pl.multiple_of(t * 8, 8), 8)
        wide = pl.ds(pl.multiple_of(t * 8 + 8, 8), 8)
        for k in range(49):
            c6[k, wide, :] = e6[k, wide, :]
            c0[k, rows, :] = e0[k, rows, :]
        for k in range(27):
            mom[k, rows, :] = em[k, rows, :]
        return carry

    lax.fori_loop(0, sub_n, keep, 0)
    lax.fori_loop(sub_n, TILES, subcell_tile(st, bt, c6, c0, mom), 0)

    def faces(t, carry):
        rows = pl.ds(pl.multiple_of(t * 8, 8), 8)
        back = pl.ds(t * 8 + 7, 8)
        wall = (sub == 0) & (t == 0)
        cs = []
        for c in range(7):
            a = [c6[n * 7 + c, back, :] for n in (0, 1, 2, 4, 5, 6)]
            b = [c0[n * 7 + c, rows, :] for n in (0, 1, 2, 4, 5, 6)]
            cs.append(rusanov2(a[:3], (a[1], a[3], a[4], a[5]), b[:3], (b[1], b[3], b[4], b[5])))
        for v in range(3):
            mm = moments7([cs[c][v] for c in range(7)])
            for n in range(3):
                fx[v * 3 + n, rows, :] = jnp.where(wall, 0.0, mm[n])
        return carry

    lax.fori_loop(0, TILES, faces, 0)


def edge_body(fg, c6, c0, mom, fx, dg, fd, ax, bx_, ay, by_, rax, rbx, ray, rby, out, own, rec, kx, klo, khi, kz, kt, buf_o, sem):
    sub, lan = iotas()
    ix, iy = lax.axis_index("gx"), lax.axis_index("gy")
    nx, ny = lax.axis_size("gx"), lax.axis_size("gy")
    even_x = ix % 2 == 0
    even_y = iy % 2 == 0
    for buf, a, b, c, d in ((own, ax, bx_, ay, by_), (rec, rax, rbx, ray, rby)):
        a, b, c, d = a[...], b[...], c[...], d[...]
        buf[:, 0, :] = jnp.where(even_x, b, a)
        buf[:, 7, :] = jnp.where(even_x, a, b)
        buf[:, 2, :] = jnp.where(even_y, d, c)
        buf[:, 3, :] = jnp.where(even_y, c, d)
    lower = (sub == 0) | (sub == 2)
    atwall = (
        ((sub == 0) & (ix == 0))
        | ((sub == 7) & (ix == nx - 1))
        | ((sub == 2) & (iy == 0))
        | ((sub == 3) & (iy == ny - 1))
    )
    sg = jnp.where(lower, -1.0, 1.0).astype(F32)
    flag = own[NS - 1] > 0.5

    def other(k):
        return jnp.where(atwall, own[k], rec[k])

    phd = []
    for n in range(3):
        f = []
        for m in range(3):
            qa = [own[k27(m, c, n)] for c in range(3)]
            qb = [other(k27(m, c, n)) for c in range(3)]
            qb[1] = -qb[1]
            f.append(rusanov2(qa, side_flux(*qa), qb, side_flux(*qb)))
        phd.append(face_mean(f))
    ua = [project7(*[own[NT + c * 3 + n] for n in range(3)]) for c in range(3)]
    ub = [project7(*[other(NT + c * 3 + n) for n in range(3)]) for c in range(4)]
    fl = []
    for c in range(7):
        qa = [ua[0][c], ua[1][c], ua[2][c]]
        qb = [ub[0][c], -ub[1][c], ub[2][c]]
        f = rusanov2(qa, side_flux(*qa), qb, side_flux(*qb))
        f[1] = f[1] + qa[0] * ub[3][c]
        fl.append(f)
    phl = [nodes_of_moments(*moments7([fl[c][v] for c in range(7)])) for v in range(3)]
    rq = nodes_of_moments(1.0, 3.0, 9.0)
    for c in range(3):
        for n in range(3):
            vd = phd[n][c]
            vl = phl[c][n]
            if c == 1:
                vd = vd * sg
                vl = vl * sg
            v = (0, 2, 1)[c]
            for k in range(3):
                x = jnp.where(flag, (-3.5 * rq[k]) * vl, (-0.5 * W[0] * UPPER[k] / W[k]) * vd)
                klo[k27(v, n, 2 - k)] = x
                khi[k27(v, n, k)] = x
                kx[k27(c, n, k)] = x
    kz[...] = jnp.zeros((NY, NY), F32)
    kz[pl.ds(0, 27, stride=2), :] = klo[:, 2, :]
    kz[pl.ds(1, 26, stride=2), :] = khi[1:, 3, :]
    kz[NY - 1 : NY, :] = khi[0:1, 3, :]
    kt[...] = kz[...].T
    outer = (lan == 0) | (lan == NY - 1)
    copies = []
    for t in range(TILES):
        rows = slice(t * 8, t * 8 + 8)
        wide = slice(t * 8 + 8, t * 8 + 16)
        back = slice(t * 8 + 7, t * 8 + 15)
        nxt = slice(t * 8 + 1, t * 8 + 9)
        z = kt[rows, :]
        flag_t = fg[rows, :] > 0
        acc = [grid3(lambda i, j: dg[k27(v, i, j), rows, :]) for v in range(3)]
        flo = [[fd[v * 3 + j, rows, :] for j in range(3)] for v in range(3)]
        fup = [[fd[v * 3 + j, nxt, :] for j in range(3)] for v in range(3)]
        acc = lift(acc, flo, fup, True, 0.5 / SLOPE)
        mm = [grid3(lambda m, n: mom[k27(v, m, n), rows, :]) for v in range(3)]
        slo = moments7([c0[c, rows, :] * c6[21 + c, back, :] for c in range(7)])
        shi = moments7([c6[c, wide, :] * c0[21 + c, nxt, :] for c in range(7)])
        for v in range(3):
            grid = [[None] * 3 for _ in range(3)]
            for n in range(3):
                lo_ = fx[v * 3 + n, rows, :]
                hi_ = fx[v * 3 + n, nxt, :]
                if v == 1:
                    lo_ = lo_ + slo[n]
                    hi_ = hi_ + shi[n]
                s = lo_ - hi_
                d = lo_ + hi_
                c = nodes_of_moments(mm[v][0][n] + s, mm[v][1][n] - 3.0 * d, mm[v][2][n] + 9.0 * s)
                for i in range(3):
                    grid[i][n] = c[i]
            for i in range(3):
                c = nodes_of_moments(grid[i][0], grid[i][1], grid[i][2])
                for j in range(3):
                    k = k27(v, i, j)
                    x = jnp.where(flag_t, 3.5 * c[j], (SLOPE * W[0]) * acc[v][i][j])
                    x = x + jnp.where(outer, pltpu.roll(z, NY - 2 * k, 1) if k else z, 0.0)
                    if t == 0:
                        x = x + jnp.where(sub == 0, kx[k27(v, j, 2 - i)], 0.0)
                    if t == TILES - 1:
                        x = x + jnp.where(sub == 7, kx[k27(v, j, i)], 0.0)
                    buf_o[k, rows, :] = x
        cp = pltpu.make_async_copy(buf_o.at[:, pl.ds(t * 8, 8), :], out.at[:, pl.ds(t * 8, 8), :], sem.at[t])
        cp.start()
        copies.append(cp)
    for cp in copies:
        cp.wait()


def swap_first(n):
    return [(i, i ^ 1) for i in range(n)]


def swap_second(nx, ny, axis):
    out = []
    for a in range(nx):
        for b in range(ny):
            i, n = (a, nx) if axis == 0 else (b, ny)
            j = i + 1 if i % 2 else i - 1
            if not 0 <= j < n:
                to = (a, b ^ CHIPS_Z) if axis == 0 else (a ^ 1, b)
            else:
                to = (j, b) if axis == 0 else (a, j)
            out.append((a * ny + b, to[0] * ny + to[1]))
    return out


VM = pl.BlockSpec(memory_space=pltpu.VMEM)
HB = pl.BlockSpec(memory_space=pltpu.HBM)
PARAMS = pltpu.CompilerParams(vmem_limit_bytes=16 * 1024 * 1024)


def planes(n, rows=NX):
    return pltpu.VMEM((n, rows, NY), F32)


def call(body, name, args, outs, scratch, cost, ins=VM, out_spec=VM):
    return pl.pallas_call(
        body,
        out_shape=outs,
        in_specs=[ins] * len(args),
        out_specs=jax.tree.map(lambda _: out_spec, outs),
        scratch_shapes=scratch,
        compiler_params=PARAMS,
        cost_estimate=pl.CostEstimate(flops=cost, transcendentals=0, bytes_accessed=min(cost, 2**20)),
        name=name,
    )(*args)


def shape(*dims, dtype=F32):
    return jax.ShapeDtypeStruct(dims, dtype)


def shards(state, bathymetry, flags):
    full = shape(27, NX, NY)
    edge = shape(NS, NY)
    nx, ny = lax.axis_size("gx"), lax.axis_size("gy")
    sides = (full, shape(NT, NX + 8, NY), full)
    st, bt, fg, ax, bx, ay, by, *first = call(
        send_body, "sends",
        tuple(pltpu.with_memory_space_constraint(x, pltpu.HBM)
              for x in (state.reshape(27, NX, NY), bathymetry.reshape(9, NX, NY), flags)),
        (full, shape(9, NX, NY), shape(NX, NY, dtype=jnp.int32), edge, edge, edge, edge) + sides,
        [pltpu.VMEM((NY, NY), F32), pltpu.VMEM((NY, NY), F32), planes(37, 8), planes(NS, 8),
         pltpu.SemaphoreType.DMA((3, TILES))],
        2**24, ins=HB,
    )
    ray = lax.ppermute(ay, "gy", swap_first(ny))
    rax = lax.ppermute(ax, "gx", swap_first(nx))
    rbx = lax.ppermute(bx, ("gx", "gy"), swap_second(nx, ny, 0))
    st_, rax = lax.optimization_barrier((st, rax))
    cells = shape(49, NX + 8, NY)
    part = call(early_body, "early", (st_, bt), sides + (cells, cells, full), [], 2**30)
    by_, part = lax.optimization_barrier((by, part))
    rby = lax.ppermute(by_, ("gx", "gy"), swap_second(nx, ny, 1))
    nine = shape(9, NX + 8, NY)
    pieces = call(
        inner_body, "inner", (st, bt, fg) + tuple(first) + tuple(part),
        (cells, cells, full, nine, full, nine), [planes(NT, NX + 8), planes(NT)], 2**10,
    )
    out = call(
        edge_body, "edge", (fg, *pieces, ax, bx, ay, by, rax, rbx, ray, rby), full,
        [planes(NS, 8), planes(NS, 8), planes(27, 8), planes(27, 8), planes(27, 8), pltpu.VMEM((NY, NY), F32),
         pltpu.VMEM((NY, NY), F32), planes(27),
         pltpu.SemaphoreType.DMA((TILES,))],
        2**20, out_spec=HB,
    )
    return out.reshape(3, 3, 3, NX, NY)


def solution(mesh):
    in_specs = (P(None, None, None, "gx", "gy"), P(None, None, "gx", "gy"), P("gx", "gy"))
    out_specs = P(None, None, None, "gx", "gy")
    return jax.shard_map(shards, mesh=mesh, in_specs=in_specs, out_specs=out_specs, check_vma=False)
```
